32 devices in a mesh: row: 8 (over z, y), col: 4 (over x, core).
Axes of the slice: x: 2, y: 2, z: 4, core: 2. Of those that a mesh axis runs over, the one named last changes fastest.
Arguments:
- hidden_in: bfloat16 [1024, 32768], P('col', 'row'), may hold values from -6 to 6
- query_key_value_weight: bfloat16 [3, 1024, 1024], P(None, 'row', 'col'), may hold values from -0.1875 to 0.1875
- output_weight: bfloat16 [1024, 1024], P('col', 'row'), may hold values from -0.75 to 0.75
- up_weight: bfloat16 [1024, 4096], P('row', 'col'), may hold values from -0.1875 to 0.1875
- down_weight: bfloat16 [4096, 1024], P('col', 'row'), may hold values from -0.09375 to 0.09375
- w_time: bfloat16 [256, 4, 1024], P('row', None, 'col'), may hold values from -0.375 to 0.375
- segment_ids: int32 [8, 4096], P('row'), may hold values from 0 to 11, as said below
- positions: int32 [8, 4096], P('row'), may hold values from 0 to 1999, as said below
- time_step: int32 [8], P('row'), may hold values from 0 to 999
- cotangent: bfloat16 [1024, 32768], P('col', 'row'), may hold values from -6 to 6
Outputs:
- output: bfloat16 [1024, 32768], P('col', 'row')
- grad_hidden: bfloat16 [1024, 32768], P('col', 'row')
- grad_qkv: float32 [3, 1024, 1024], P(None, 'row', 'col')
- grad_out: float32 [1024, 1024], P('col', 'row')
- grad_up: float32 [1024, 4096], P('row', 'col')
- grad_down: float32 [4096, 1024], P('col', 'row')
- grad_time: float32 [256, 4, 1024], P('row', None, 'col')
The draws below stay inside these ranges and needn't reach their ends.
Inputs may be any that keep to these rules, and one draw needn't show every extreme that they name: segment_ids number the documents of each sequence from 0 upward and never fall; each document has at most 2000 tokens, every one but the last of its sequence 200 or more, and each sequence has one of exactly 2000. positions count a token's place in its document from 0.
All inputs are finite; a program needn't handle non-finite values.
Results may differ from the reference program's by a relative error of at most 0.02.
Values may be sent and summed in bfloat16 or wider, within the bound.
No kernel may reach another device: no remote copies, remote signals or barrier semaphores. Data moves between devices by JAX's collectives and lax.ppermute only.
A program may use at most 384 MiB of HBM per device.

```python
import math
import jax
import jax.numpy as jnp
from jax import lax

D = 1024
HEADS = 16
HEAD_DIM = 64
FF = 4096
TEMB = 256
SEQ_LEN = 4096
QBLOCK = 512
DOC_MOST = 2000
DOC_LEAST = 200
SEQS = 8
TOKENS = 32768


def doc_layout(key):
    base = jax.random.fold_in(key, 11)
    length_key, place_key = jax.random.split(base)
    doc_slots = SEQ_LEN // DOC_LEAST + 1
    lengths = jax.random.randint(length_key, (SEQS, doc_slots), DOC_LEAST, DOC_MOST + 1)
    seq_index = jnp.arange(SEQS, dtype=jnp.int32)
    lengths = jnp.where(seq_index[:, None] == 0, DOC_LEAST, lengths)
    longest = jax.random.randint(place_key, (SEQS,), 0, 2)
    slot_index = jnp.arange(doc_slots, dtype=jnp.int32)
    lengths = jnp.where(slot_index[None, :] == longest[:, None], DOC_MOST, lengths).astype(jnp.int32)
    doc_ends = jnp.cumsum(lengths, axis=1).astype(jnp.int32)
    places = jnp.arange(SEQ_LEN, dtype=jnp.int32)
    passed = doc_ends[:, None, :] <= places[None, :, None]
    segment_ids = jnp.sum(passed.astype(jnp.int32), axis=2).astype(jnp.int32)
    doc_start = jnp.max(jnp.where(passed, doc_ends[:, None, :], 0), axis=2).astype(jnp.int32)
    positions = (places[None, :] - doc_start).astype(jnp.int32)
    return (segment_ids, positions)


def draw_segment_ids(key, part):
    return doc_layout(key)[0]


def draw_positions(key, part):
    return doc_layout(key)[1]


def set_ends(values, rng, smallest, high):
    spot = [jax.random.randint(jax.random.fold_in(rng, axis), (), 0, length) for axis, length in enumerate(values.shape)]
    widest = values.shape.index(max(values.shape))
    neighbour = spot[:widest] + [(spot[widest] + 1) % values.shape[widest]] + spot[widest + 1:]
    return values.at[tuple(spot)].set(smallest).at[tuple(neighbour)].set(high)


def levels(stream_key, extent, cuts, low, largest):
    level = 1.0
    for dim, shards_of in cuts:
        heights = jax.random.uniform(jax.random.fold_in(jax.random.fold_in(stream_key, 6), dim), (shards_of,), jnp.float32, low / len(cuts), largest / len(cuts))
        level = level * jnp.repeat(jnp.exp(heights), extent[dim] // shards_of).reshape((-1,) + (1,) * (len(extent) - 1 - dim))
    return level


def bell_draw(own_key, dims, deviation, most, cuts=(), kind=jnp.bfloat16):
    gain = levels(own_key, dims, cuts, -0.22, 0.18) if cuts else 1.0
    entries = jax.random.normal(own_key, dims, jnp.float32) * deviation * gain
    return jnp.minimum(jnp.maximum(entries, -most), most).astype(kind)


def setup_inputs(seed: int = 0) -> dict:
    streams_of = jax.random.split(jax.random.key(seed), 11)
    return {
        "hidden_in": bell_draw(streams_of[0], (D, TOKENS), 1.0, 6.0, ((0, 4), (1, 8))),
        "query_key_value_weight": bell_draw(streams_of[1], (3, D, D), D ** -0.5, 0.1875, ((1, 8), (2, 4))),
        "output_weight": bell_draw(streams_of[2], (D, D), (D // 16) ** -0.5, 0.75, ((0, 4), (1, 8))),
        "up_weight": bell_draw(streams_of[3], (D, FF), D ** -0.5, 0.1875, ((0, 8), (1, 4))),
        "down_weight": bell_draw(streams_of[4], (FF, D), FF ** -0.5, 0.09375, ((0, 4), (1, 8))),
        "w_time": bell_draw(streams_of[5], (TEMB, 4, D), TEMB ** -0.5, 0.375, ((0, 8), (2, 4))),
        "segment_ids": draw_segment_ids(jax.random.fold_in(streams_of[10], 71), 0),
        "positions": draw_positions(jax.random.fold_in(streams_of[10], 71), 0),
        "time_step": set_ends(jax.random.randint(streams_of[8], (SEQS,), 0, 1000), jax.random.fold_in(streams_of[8], 1), 0, 999).astype(jnp.int32),
        "cotangent": bell_draw(streams_of[9], (D, TOKENS), 1.0, 6.0, ((0, 4), (1, 8))),
    }


norm_eps = 1e-05
masked_score = -1e+30
highest_precision = lax.Precision.HIGHEST

@jax.custom_vjp
def low(v):
    return lax.optimization_barrier(v.astype(jnp.bfloat16)).astype(jnp.float32)

@jax.custom_vjp
def lower_backward(v):
    return v

def low_keep(v):
    return (low(v), None)

def low_pass(kept, grad):
    return (grad,)

def back_keep(v):
    return (v, None)

def back_low(kept, grad):
    return (low(grad),)
low.defvjp(low_keep, low_pass)
lower_backward.defvjp(back_keep, back_low)

def time_features(time_steps, feature_count):
    half_dim = feature_count // 2
    frequency = jnp.exp(-math.log(10000.0) * jnp.arange(half_dim, dtype=jnp.float32) / half_dim)
    angles = time_steps.astype(jnp.float32)[:, None] * frequency[None, :]
    return jnp.concatenate([jnp.sin(angles), jnp.cos(angles)], axis=1)

def rotary_tables(places, head_width):
    half_dim = head_width // 2
    inverse = jnp.exp(-math.log(10000.0) * jnp.arange(half_dim, dtype=jnp.float32) * 2.0 / head_width)
    angles = places.astype(jnp.float32)[..., None] * inverse
    return (jnp.cos(angles), jnp.sin(angles))

def rotate(values, cosine_table, sine_table):
    half_dim = values.shape[-1] // 2
    lead_part = values[..., :half_dim]
    tail_part = values[..., half_dim:]
    cosine_table = cosine_table[..., None, :]
    sine_table = sine_table[..., None, :]
    return jnp.concatenate([lead_part * cosine_table - tail_part * sine_table, lead_part * sine_table + tail_part * cosine_table], axis=-1)

def modulated_norm(values, scales, shifts):
    row_mean = lax.optimization_barrier(jnp.mean(values, axis=-1, keepdims=True))
    spread = lax.optimization_barrier(jnp.mean(values * values, axis=-1, keepdims=True)) - row_mean * row_mean
    normed_input = (values - row_mean) * lax.rsqrt(spread + norm_eps)
    return normed_input * (1.0 + scales[:, None, :]) + shifts[:, None, :]

def block_attention(query_block, query_segs, seq_keys, seq_values, key_segs):
    scores = lower_backward(jnp.einsum('qhd,khd->hqk', query_block, seq_keys, precision=highest_precision) * HEAD_DIM ** (-0.5))
    same_doc = query_segs[:, None] == key_segs[None, :]
    scores = jnp.where(same_doc[None], scores, masked_score)
    softmax_out = low(jax.nn.softmax(scores, axis=-1))
    return jnp.einsum('hqk,khd->qhd', softmax_out, seq_values, precision=highest_precision)
checked_attention = jax.checkpoint(block_attention)

def sequence_attention(packed):
    seq_queries, seq_keys, seq_values, seq_segs = packed
    blocks = SEQ_LEN // QBLOCK
    query_blocks = seq_queries.reshape(blocks, QBLOCK, HEADS, HEAD_DIM)
    seg_blocks = seq_segs.reshape(blocks, QBLOCK)
    attended_values = lax.map(lambda block_in: checked_attention(block_in[0], block_in[1], seq_keys, seq_values, seq_segs), (query_blocks, seg_blocks))
    return attended_values.reshape(SEQ_LEN, HEADS, HEAD_DIM)

def layer_forward(hidden, query_key_value_weight, output_weight, up_weight, down_weight, w_time, segment_ids, positions, time_step):
    embedded = time_features(time_step, TEMB)
    modulation = jnp.einsum('st,tkd->skd', embedded, w_time, precision=highest_precision)
    residual_state = hidden.reshape(SEQS, SEQ_LEN, D)
    normed_input = low(modulated_norm(residual_state, modulation[:, 0], modulation[:, 1]))
    cosine_table, sine_table = rotary_tables(positions, HEAD_DIM)

    def project(layer_index):
        layer_result = lower_backward(jnp.einsum('iux,xt->iut', normed_input, query_key_value_weight[layer_index], precision=highest_precision))
        return layer_result.reshape(SEQS, SEQ_LEN, HEADS, HEAD_DIM)
    queries = low(rotate(project(0), cosine_table, sine_table))
    keys_all = low(rotate(project(1), cosine_table, sine_table))
    values_all = low(project(2))
    attended_values = lax.map(sequence_attention, (queries, keys_all, values_all, segment_ids))
    attended_values = low(lower_backward(attended_values)).reshape(SEQS, SEQ_LEN, D)
    residual_state = residual_state + lower_backward(jnp.einsum('hvf,fa->hva', attended_values, output_weight, precision=highest_precision))
    second_normed = low(modulated_norm(residual_state, modulation[:, 2], modulation[:, 3]))
    up_projected = lower_backward(jnp.einsum('jbt,tm->jbm', second_normed, up_weight, precision=highest_precision))
    active_hidden = low(jax.nn.gelu(up_projected, approximate=False))
    residual_state = residual_state + jnp.einsum('ocp,pq->ocq', active_hidden, down_weight, precision=highest_precision)
    return residual_state.reshape(SEQS * SEQ_LEN, D)

def reference(hidden_in, query_key_value_weight, output_weight, up_weight, down_weight, w_time, segment_ids, positions, time_step, cotangent):
    floats = [hidden_in.T, query_key_value_weight, output_weight, up_weight, down_weight, w_time]
    floats = [item.astype(jnp.float32) for item in floats]

    def closed(hidden, wq, wo, wu, wd, wt):
        return layer_forward(hidden, wq, wo, wu, wd, wt, segment_ids, positions, time_step)
    layer_result, pullback = jax.vjp(closed, *floats)
    grads = pullback(cotangent.T.astype(jnp.float32))
    return (layer_result.T.astype(jnp.bfloat16), grads[0].T.astype(jnp.bfloat16), grads[1], grads[2], grads[3], grads[4], grads[5])
```

```python
from functools import partial
import math

import jax
import jax.numpy as jnp
from jax import lax
from jax.experimental import pallas as pl
from jax.experimental.pallas import tpu as pltpu
from jax.sharding import PartitionSpec as P

D = 1024
HEAD_DIM = 64
TEMB = 256
HALF = HEAD_DIM // 2
SCORE_SCALE = HEAD_DIM**-0.5
SCORE_LOG2 = SCORE_SCALE * math.log2(math.e)
SAFE_LOG2 = 60.0
STRIP = 512

norm_eps = 1e-05
masked_score = -1e30
highest_precision = lax.Precision.HIGHEST
f32 = jnp.float32
bf16 = jnp.bfloat16


def matmul(a, b, ca=1, cb=0):
    return lax.dot_general(a, b, (((ca,), (cb,)), ((), ())), preferred_element_type=f32)


def head_rows(h):
    return slice(h * HEAD_DIM, (h + 1) * HEAD_DIM)


def attend_kernel(
    lo_ref, n_ref, q_ref, k_ref, v_ref, segq_ref, segs_ref, o_ref, lse_ref,
    k_sc, v_sc, segk_ref, acc_sc, kmax_sc, *, heads, tq, tk,
):
    i = pl.program_id(0)
    tokens = k_ref.shape[1]

    @pl.when(i == 0)
    def _():
        def strip(b, most):
            cols = pl.ds(pl.multiple_of(b * STRIP, STRIP), STRIP)
            segk_ref[cols, :] = jnp.broadcast_to(segs_ref[:, cols], (128, STRIP)).T
            for h in range(heads):
                kk = k_ref[head_rows(h), cols]
                k_sc[h, cols, :] = kk.T
                kf = kk.astype(f32)
                most = jnp.maximum(most, jnp.sum(kf * kf, axis=0, keepdims=True))
                v_sc[h, :HEAD_DIM, cols] = v_ref[head_rows(h), cols]
                v_sc[h, HEAD_DIM:, cols] = jnp.ones((8, STRIP), bf16)
            return most

        most = lax.fori_loop(0, tokens // STRIP, strip, jnp.zeros((1, STRIP), f32))
        kmax_sc[0] = jnp.max(most)

    segq = segq_ref[...]
    queries = [q_ref[head_rows(h), :] for h in range(heads)]
    qmost = jnp.zeros((1, tq), f32)
    for h in range(heads):
        qf = queries[h].astype(f32)
        qmost = jnp.maximum(qmost, jnp.sum(qf * qf, axis=0, keepdims=True))
    small = jnp.max(qmost) * kmax_sc[0] * (SCORE_LOG2 * SCORE_LOG2) <= SAFE_LOG2 * SAFE_LOG2
    lo = lo_ref[i]
    n = n_ref[i]
    acc_sc[...] = jnp.zeros_like(acc_sc)

    def finish(tops):
        for h in range(heads):
            total = acc_sc[h, HEAD_DIM : HEAD_DIM + 1, :]
            o_ref[head_rows(h), :] = (acc_sc[h, :HEAD_DIM, :] / total).astype(bf16)
            lse_ref[h : h + 1, :] = tops[h] + jnp.log2(total)

    @pl.when(small)
    def _():
        def step(j, _):
            off = pl.multiple_of(lo + j * tk, 128)
            same = segk_ref[pl.ds(off, tk), :][:, :1] == segq
            scores = lambda h: matmul(k_sc[h, pl.ds(off, tk), :], queries[h])
            ahead = scores(0)
            for h in range(heads):
                s = ahead
                if h + 1 < heads:
                    ahead = scores(h + 1)
                p = jnp.exp2(jnp.where(same, s * SCORE_LOG2, masked_score)).astype(bf16)
                acc_sc[h] += matmul(v_sc[h, :, pl.ds(off, tk)], p)
            return 0

        lax.fori_loop(0, n, step, 0)
        finish([jnp.zeros((1, tq), f32)] * heads)

    @pl.when(jnp.logical_not(small))
    def _():
        def step(j, tops):
            off = pl.multiple_of(lo + j * tk, 128)
            same = segk_ref[pl.ds(off, tk), :][:, :1] == segq
            grown = []
            for h in range(heads):
                s = matmul(k_sc[h, pl.ds(off, tk), :], queries[h]) * SCORE_LOG2
                s = jnp.where(same, s, masked_score)
                top = jnp.maximum(tops[h], jnp.max(s, axis=0, keepdims=True))
                p = jnp.exp2(s - top).astype(bf16)
                acc_sc[h] = acc_sc[h] * jnp.exp2(tops[h] - top) + matmul(
                    v_sc[h, :, pl.ds(off, tk)], p
                )
                grown.append(top)
            return tuple(grown)

        start = tuple(jnp.full((1, tq), masked_score, f32) for _ in range(heads))
        finish(lax.fori_loop(0, n, step, start))


def block_ranges(segments, positions, tq, tk):
    tokens = segments.shape[0]
    blocks = tokens // tq
    firsts = jnp.arange(blocks, dtype=jnp.int32) * tq
    lo = ((firsts - positions[::tq]) // 128) * 128
    last = segments.reshape(blocks, tq)[:, -1]
    end = jnp.sum((segments[None, :] <= last[:, None]).astype(jnp.int32), axis=1)
    n = (end - lo + tk - 1) // tk
    lo = jnp.maximum(jnp.minimum(lo, tokens - n * tk), 0)
    return lo.astype(jnp.int32), n.astype(jnp.int32)


def resident(shape):
    return pl.BlockSpec(shape, lambda i, lo, n: (0, 0), pipeline_mode=pl.Buffered(1))


def attend(q, k, v, segments, positions, seg_rows, tq=512, tk=512):
    rows, tokens = q.shape
    heads = rows // HEAD_DIM
    lo, n = block_ranges(segments, positions, tq, tk)
    block = lambda r: pl.BlockSpec((r, tq), lambda i, lo, n: (0, i))
    pairs = tokens * tokens * heads // 2
    return pl.pallas_call(
        partial(attend_kernel, heads=heads, tq=tq, tk=tk),
        out_shape=(
            jax.ShapeDtypeStruct((rows, tokens), bf16),
            jax.ShapeDtypeStruct((heads, tokens), f32),
        ),
        grid_spec=pltpu.PrefetchScalarGridSpec(
            num_scalar_prefetch=2,
            grid=(tokens // tq,),
            in_specs=[
                block(rows), resident((rows, tokens)), resident((rows, tokens)),
                block(1), resident((1, tokens)),
            ],
            out_specs=(block(rows), block(heads)),
            scratch_shapes=[
                pltpu.VMEM((heads, tokens, HEAD_DIM), bf16),
                pltpu.VMEM((heads, HEAD_DIM + 8, tokens), bf16),
                pltpu.VMEM((tokens, 128), jnp.int32),
                pltpu.VMEM((heads, HEAD_DIM + 8, tq), f32),
                pltpu.SMEM((1,), f32),
            ],
        ),
        compiler_params=pltpu.CompilerParams(vmem_limit_bytes=48 << 20),
        cost_estimate=pl.CostEstimate(
            flops=16 * HEAD_DIM * pairs, bytes_accessed=8 * rows * tokens, transcendentals=pairs
        ),
        name="attend",
    )(lo, n, q, k, v, seg_rows, seg_rows)


def unrotate(g, cosine, sine):
    a = g[:HALF]
    b = g[HALF:]
    return jnp.concatenate([a * cosine + b * sine, b * cosine - a * sine], axis=0).astype(bf16)


def attend_back_kernel(
    lo_ref, n_ref, q_ref, k_ref, v_ref, o_ref, do_ref, lse_ref, segq_ref, segs_ref,
    cosq_ref, sinq_ref, cos_ref, sin_ref, dq_ref, dk_ref, dv_ref,
    k_sc, v_sc, segk_ref, dk_sc, dv_sc, dq_sc, *, heads, tq, tk,
):
    i = pl.program_id(0)
    tokens = k_ref.shape[1]

    @pl.when(i == 0)
    def _():
        def strip(b, _):
            cols = pl.ds(pl.multiple_of(b * STRIP, STRIP), STRIP)
            segk_ref[cols, :] = jnp.broadcast_to(segs_ref[:, cols], (128, STRIP)).T
            for h in range(heads):
                k_sc[h, cols, :] = k_ref[head_rows(h), cols].T
                v_sc[h, cols, :] = v_ref[head_rows(h), cols].T
            return 0

        lax.fori_loop(0, tokens // STRIP, strip, 0)
        dk_sc[...] = jnp.zeros_like(dk_sc)
        dv_sc[...] = jnp.zeros_like(dv_sc)

    segq = segq_ref[...]
    deltas = [
        jnp.sum(
            do_ref[head_rows(h), :].astype(f32) * o_ref[head_rows(h), :].astype(f32),
            axis=0,
            keepdims=True,
        )
        for h in range(heads)
    ]
    lo = lo_ref[i]
    dq_sc[...] = jnp.zeros_like(dq_sc)

    def step(j, _):
        off = pl.multiple_of(lo + j * tk, 128)
        cols = pl.ds(off, tk)
        same = segk_ref[cols, :][:, :1] == segq

        def products(h):
            rows = head_rows(h)
            return matmul(k_sc[h, cols, :], q_ref[rows, :]), matmul(v_sc[h, cols, :], do_ref[rows, :])

        ahead = products(0)
        for h in range(heads):
            rows = head_rows(h)
            s, dp = ahead
            if h + 1 < heads:
                ahead = products(h + 1)
            p = jnp.exp2(jnp.where(same, s * SCORE_LOG2 - lse_ref[h : h + 1, :], masked_score))
            ds = (p * (dp - deltas[h])).astype(bf16)
            dv_sc[rows, cols] += matmul(do_ref[rows, :], p.astype(bf16), 1, 1)
            dk_sc[rows, cols] += matmul(q_ref[rows, :], ds, 1, 1)
            dq_sc[rows, :] += matmul(k_ref[rows, cols], ds)
        return 0

    lax.fori_loop(0, n_ref[i], step, 0)
    cosine = cosq_ref[...] * SCORE_SCALE
    sine = sinq_ref[...] * SCORE_SCALE
    for h in range(heads):
        dq_ref[head_rows(h), :] = unrotate(dq_sc[head_rows(h), :], cosine, sine)

    @pl.when(i == pl.num_programs(0) - 1)
    def _():
        def strip(b, _):
            cols = pl.ds(pl.multiple_of(b * STRIP, STRIP), STRIP)
            c = cos_ref[:, cols] * SCORE_SCALE
            s = sin_ref[:, cols] * SCORE_SCALE
            for h in range(heads):
                dk_ref[head_rows(h), cols] = unrotate(dk_sc[head_rows(h), cols], c, s)
            dv_ref[:, cols] = dv_sc[:, cols].astype(bf16)
            return 0

        lax.fori_loop(0, tokens // STRIP, strip, 0)


def attend_back(
    q, k, v, o, do, lse, segments, positions, seg_rows, cosine, sine, tq=256, tk=512
):
    rows, tokens = q.shape
    heads = rows // HEAD_DIM
    lo, n = block_ranges(segments, positions, tq, tk)
    block = lambda r: pl.BlockSpec((r, tq), lambda i, lo, n: (0, i))
    whole = resident((rows, tokens))
    pairs = tokens * tokens * heads // 2
    return pl.pallas_call(
        partial(attend_back_kernel, heads=heads, tq=tq, tk=tk),
        out_shape=[jax.ShapeDtypeStruct((rows, tokens), bf16)] * 3,
        grid_spec=pltpu.PrefetchScalarGridSpec(
            num_scalar_prefetch=2,
            grid=(tokens // tq,),
            in_specs=[
                block(rows), whole, whole, block(rows), block(rows), block(heads),
                block(1), resident((1, tokens)), block(HALF), block(HALF),
                resident((HALF, tokens)), resident((HALF, tokens)),
            ],
            out_specs=[block(rows), whole, whole],
            scratch_shapes=[
                pltpu.VMEM((heads, tokens, HEAD_DIM), bf16),
                pltpu.VMEM((heads, tokens, HEAD_DIM), bf16),
                pltpu.VMEM((tokens, 128), jnp.int32),
                pltpu.VMEM((rows, tokens), f32),
                pltpu.VMEM((rows, tokens), f32),
                pltpu.VMEM((rows, tq), f32),
            ],
        ),
        compiler_params=pltpu.CompilerParams(vmem_limit_bytes=56 << 20),
        cost_estimate=pl.CostEstimate(
            flops=40 * HEAD_DIM * pairs, bytes_accessed=16 * rows * tokens, transcendentals=pairs
        ),
        name="attend_back",
    )(lo, n, q, k, v, o, do, lse, seg_rows, seg_rows, cosine, sine, cosine, sine)


def project_kernel(order_ref, *refs, cols, tt):
    x_refs = refs[:cols]
    w_ref, mod_ref, cos_ref, sin_ref, q_ref, k_ref, v_ref, mean_ref, inv_ref = refs[cols : cols + 9]
    w_sc, n_sc = refs[cols + 9 :]
    block = x_refs[0].shape[0]

    @pl.when(pl.program_id(0) == 0)
    def _():
        for b in range(cols):
            start = pl.multiple_of(order_ref[b] * block, block)
            w_sc[:, b * block : (b + 1) * block] = w_ref[pl.ds(start, block), :].T

    total = jnp.zeros((1, tt), f32)
    squares = jnp.zeros((1, tt), f32)
    for b in range(cols):
        x = x_refs[b][...].astype(f32)
        total = total + jnp.sum(x, axis=0, keepdims=True)
        squares = squares + jnp.sum(x * x, axis=0, keepdims=True)
    mean = total * (1.0 / D)
    inv = lax.rsqrt(squares * (1.0 / D) - mean * mean + norm_eps)
    mean_ref[...] = mean
    inv_ref[...] = inv
    for b in range(cols):
        rows = slice(b * block, (b + 1) * block)
        n = (x_refs[b][...].astype(f32) - mean) * inv
        n_sc[rows, :] = (n * (1.0 + mod_ref[rows, 0:1]) + mod_ref[rows, 1:2]).astype(bf16)
    out = matmul(w_sc[...], n_sc[...])
    cosine = cos_ref[...]
    sine = sin_ref[...]
    for j, ref in ((0, q_ref), (1, k_ref)):
        for h in range(block // HEAD_DIM):
            first = j * block + h * HEAD_DIM
            a = out[first : first + HALF]
            b = out[first + HALF : first + HEAD_DIM]
            ref[h * HEAD_DIM : h * HEAD_DIM + HALF, :] = (a * cosine - b * sine).astype(bf16)
            ref[h * HEAD_DIM + HALF : (h + 1) * HEAD_DIM, :] = (a * sine + b * cosine).astype(bf16)
    v_ref[...] = out[2 * block :].astype(bf16)


def project(meta, pieces, w_qkv, mod, cosine, sine, tt=512):
    cols = len(pieces)
    block, tokens = pieces[0].shape
    strip = lambda r: pl.BlockSpec((r, tt), lambda t, order: (0, t))
    whole = lambda s: pl.BlockSpec(s, lambda t, order: (0, 0), pipeline_mode=pl.Buffered(1))
    return pl.pallas_call(
        partial(project_kernel, cols=cols, tt=tt),
        out_shape=[jax.ShapeDtypeStruct((block, tokens), bf16)] * 3
        + [jax.ShapeDtypeStruct((1, tokens), f32)] * 2,
        grid_spec=pltpu.PrefetchScalarGridSpec(
            num_scalar_prefetch=1,
            grid=(tokens // tt,),
            in_specs=[strip(block)] * cols
            + [whole(w_qkv.shape), whole(mod.shape), strip(HALF), strip(HALF)],
            out_specs=[strip(block)] * 3 + [strip(1)] * 2,
            scratch_shapes=[pltpu.VMEM((3 * block, D), bf16), pltpu.VMEM((D, tt), bf16)],
        ),
        compiler_params=pltpu.CompilerParams(vmem_limit_bytes=40 << 20),
        cost_estimate=pl.CostEstimate(
            flops=6 * D * block * tokens,
            bytes_accessed=2 * (D + 3 * block) * tokens,
            transcendentals=tokens,
        ),
        name="project",
    )(meta, *pieces, w_qkv, mod, cosine, sine)


def relative_rows(b, block):
    return slice(b * block, (b + 1) * block)


def feed_forward_kernel(meta_ref, *refs, cols, hidden, tb, hb, sub):
    x_refs = refs[:cols]
    own_ref, recv_ref = refs[cols : cols + 2]
    cot_refs = refs[cols + 2 : 2 * cols + 2]
    w_refs = refs[2 * cols + 2 : 3 * cols + 2]
    (
        mod_ref, act_ref, du_ref, n_ref, cot_ref, mid_ref, mean_ref, inv_ref,
        keep_ref, send_ref, dn_ref, up_sc, down_sc, y_sc, dn_sc,
    ) = refs[3 * cols + 2 :]
    block = x_refs[0].shape[0]
    h = pl.program_id(1)
    hs = pl.ds(pl.multiple_of(h * hb, hb), hb)

    @pl.when(pl.program_id(0) == 0)
    def _():
        down_cols = pl.ds(pl.multiple_of(hidden + h * hb, hb), hb)
        for b in range(cols):
            up_sc[hs, relative_rows(b, block)] = w_refs[b][:, hs].T
            down_sc[hs, relative_rows(b, block)] = w_refs[b][:, down_cols].T

    @pl.when(h == 0)
    def _():
        total = jnp.zeros((1, tb), f32)
        squares = jnp.zeros((1, tb), f32)
        for b in range(cols):
            rows = relative_rows(b, block)
            mid = (
                x_refs[b][...].astype(f32)
                + own_ref[rows, :].astype(f32)
                + recv_ref[relative_rows(b ^ 1, block), :].astype(f32)
            )
            mid_ref[rows, :] = mid
            total = total + jnp.sum(mid, axis=0, keepdims=True)
            squares = squares + jnp.sum(mid * mid, axis=0, keepdims=True)
            cot_ref[rows, :] = cot_refs[b][...]
        mean = total * (1.0 / D)
        inv = lax.rsqrt(squares * (1.0 / D) - mean * mean + norm_eps)
        mean_ref[...] = mean
        inv_ref[...] = inv
        for b in range(cols):
            rows = relative_rows(b, block)
            n = (mid_ref[rows, :] - mean) * inv
            n_ref[rows, :] = (n * (1.0 + mod_ref[rows, 2:3]) + mod_ref[rows, 3:4]).astype(bf16)
        y_sc[...] = jnp.zeros_like(y_sc)
        dn_sc[...] = jnp.zeros_like(dn_sc)

    def products(s):
        rows = pl.ds(pl.multiple_of(h * hb + s * sub, sub), sub)
        return matmul(up_sc[rows, :], n_ref[...]), matmul(down_sc[rows, :], cot_ref[...])

    ahead = products(0)
    for s in range(hb // sub):
        up, grad_active = ahead
        if s + 1 < hb // sub:
            ahead = products(s + 1)
        cdf = 0.5 * (1.0 + lax.erf(up * math.sqrt(0.5)))
        density = jnp.exp(-0.5 * up * up) * (1.0 / math.sqrt(2.0 * math.pi))
        act_ref[s * sub : (s + 1) * sub, :] = (up * cdf).astype(bf16)
        du_ref[s * sub : (s + 1) * sub, :] = (grad_active * (cdf + up * density)).astype(bf16)
    down_cols = pl.ds(pl.multiple_of(hidden + h * hb, hb), hb)
    for b in range(cols):
        rows = relative_rows(b, block)
        dn_sc[rows, :] += matmul(w_refs[b][:, hs], du_ref[...])
        y_sc[rows, :] += matmul(w_refs[b][:, down_cols], act_ref[...])

    @pl.when(h == pl.num_programs(1) - 1)
    def _():
        dn_ref[...] = dn_sc[...].astype(bf16)
        for i in range(cols // 2):
            rows = relative_rows(2 * i, block)
            keep_ref[relative_rows(i, block), :] = mid_ref[rows, :] + y_sc[rows, :]
            send_ref[relative_rows(i, block), :] = y_sc[relative_rows(2 * i + 1, block), :].astype(
                bf16
            )


def feed_forward(meta, pieces, own, recv, cot_pieces, ff_all, hidden, mod, tb=512, hb=512):
    cols = len(pieces)
    block = pieces[0].shape[0]
    part = own.shape[1]
    tb = min(tb, part)
    strip = lambda r: pl.BlockSpec((r, tb), lambda t, h, meta: (0, t))
    tile = pl.BlockSpec((hb, tb), lambda t, h, meta: (h, t))

    def weight_rows(b):
        return pl.BlockSpec(
            (block, ff_all.shape[1]), lambda t, h, meta: (meta[b], 0), pipeline_mode=pl.Buffered(1)
        )

    shape = lambda r, kind: jax.ShapeDtypeStruct((r, part), kind)
    return pl.pallas_call(
        partial(feed_forward_kernel, cols=cols, hidden=hidden, tb=tb, hb=hb, sub=256),
        out_shape=[
            shape(hidden, bf16), shape(hidden, bf16), shape(D, bf16), shape(D, bf16),
            shape(D, f32), shape(1, f32), shape(1, f32), shape(D // 2, f32),
            shape(D // 2, bf16), shape(D, bf16),
        ],
        grid_spec=pltpu.PrefetchScalarGridSpec(
            num_scalar_prefetch=1,
            grid=(part // tb, hidden // hb),
            in_specs=[pl.BlockSpec((block, tb), lambda t, h, meta: (0, meta[cols] // tb + t))] * cols
            + [strip(D), strip(D)]
            + [strip(block)] * cols
            + [weight_rows(b) for b in range(cols)]
            + [
                pl.BlockSpec(
                    mod.shape, lambda t, h, meta: (0, 0), pipeline_mode=pl.Buffered(1)
                )
            ],
            out_specs=[
                tile, tile, strip(D), strip(D), strip(D), strip(1), strip(1),
                strip(D // 2), strip(D // 2), strip(D),
            ],
            scratch_shapes=[
                pltpu.VMEM((hidden, D), bf16),
                pltpu.VMEM((hidden, D), bf16),
                pltpu.VMEM((D, tb), f32),
                pltpu.VMEM((D, tb), f32),
            ],
        ),
        compiler_params=pltpu.CompilerParams(vmem_limit_bytes=58 << 20),
        cost_estimate=pl.CostEstimate(
            flops=8 * D * hidden * part,
            bytes_accessed=4 * D * hidden + 24 * D * part,
            transcendentals=2 * hidden * part,
        ),
        name="feed_forward",
    )(meta, *pieces, own, recv, *cot_pieces, *([ff_all] * cols), mod)


def mid_back_kernel(meta_ref, *refs, cols):
    dn_ref, recv_ref, mid_ref, mean_ref, inv_ref, cot_ref, mod_ref = refs[:7]
    w_refs = refs[7 : 7 + cols]
    kept_ref, branch_ref, att_ref, sums_ref, r_sc, w_sc, sum_sc = refs[7 + cols :]
    block = w_refs[0].shape[0]
    tb = dn_ref.shape[1]
    t = pl.program_id(0)

    @pl.when(t == 0)
    def _():
        sum_sc[...] = jnp.zeros_like(sum_sc)
        for b in range(cols):
            w_sc[:, relative_rows(b, block)] = w_refs[b][...].T

    mean = mean_ref[...]
    inv = inv_ref[...]
    total = jnp.zeros((1, tb), f32)
    cross = jnp.zeros((1, tb), f32)
    for b in range(cols):
        rows = relative_rows(b, block)
        r = dn_ref[rows, :].astype(f32) + recv_ref[relative_rows(b ^ 1, block), :].astype(f32)
        n = (mid_ref[rows, :] - mean) * inv
        sum_sc[rows, 0:1] += jnp.sum(r * n, axis=1, keepdims=True)
        sum_sc[rows, 1:2] += jnp.sum(r, axis=1, keepdims=True)
        m = r * (1.0 + mod_ref[rows, 2:3])
        total = total + jnp.sum(m, axis=0, keepdims=True)
        cross = cross + jnp.sum(m * n, axis=0, keepdims=True)
        r_sc[rows, :] = m
    total = total * (1.0 / D)
    cross = cross * (1.0 / D)
    for b in range(cols):
        rows = relative_rows(b, block)
        n = (mid_ref[rows, :] - mean) * inv
        grad = cot_ref[rows, :].astype(f32) + inv * (r_sc[rows, :] - total - n * cross)
        if b % 2 == 0:
            kept_ref[relative_rows(b // 2, block), :] = grad
        branch_ref[rows, :] = grad.astype(bf16)
    att_ref[...] = matmul(w_sc[...], branch_ref[...]).astype(bf16)

    @pl.when(t == pl.num_programs(0) - 1)
    def _():
        sums_ref[...] = sum_sc[...]


def mid_back(cols, meta, own, recv, mid, mean, inv, cot, mod, ff_all, hidden, tb=256):
    block = D // cols
    part = own.shape[1]
    tb = min(tb, part)
    width = ff_all.shape[1] - 2 * hidden
    strip = lambda r: pl.BlockSpec((r, tb), lambda t, meta: (0, t))
    whole = lambda s: pl.BlockSpec(s, lambda t, meta: (0, 0), pipeline_mode=pl.Buffered(1))

    def weight_rows(b):
        return pl.BlockSpec(
            (block, width),
            lambda t, meta: (meta[b], 2 * hidden // width),
            pipeline_mode=pl.Buffered(1),
        )

    shape = lambda r, kind: jax.ShapeDtypeStruct((r, part), kind)
    return pl.pallas_call(
        partial(mid_back_kernel, cols=cols),
        out_shape=[
            shape(D // 2, f32), shape(D, bf16), shape(width, bf16),
            jax.ShapeDtypeStruct((D, 2), f32),
        ],
        grid_spec=pltpu.PrefetchScalarGridSpec(
            num_scalar_prefetch=1,
            grid=(part // tb,),
            in_specs=[strip(D), strip(D), strip(D), strip(1), strip(1), strip(D), whole(mod.shape)]
            + [weight_rows(b) for b in range(cols)],
            out_specs=[strip(D // 2), strip(D), strip(width), whole((D, 2))],
            scratch_shapes=[
                pltpu.VMEM((D, tb), f32),
                pltpu.VMEM((width, D), bf16),
                pltpu.VMEM((D, 2), f32),
            ],
        ),
        compiler_params=pltpu.CompilerParams(vmem_limit_bytes=40 << 20),
        cost_estimate=pl.CostEstimate(
            flops=2 * D * width * part, bytes_accessed=18 * D * part, transcendentals=0
        ),
        name="mid_back",
    )(meta, own, recv, mid, mean, inv, cot, mod, *([ff_all] * cols))


def project_back_kernel(meta_ref, *refs, cols, tt):
    x_refs = refs[:cols]
    (
        mean_ref, inv_ref, dq_ref, dk_ref, dv_ref, w_ref, mod_ref, kept_ref,
        keep_ref, send_ref, g_ref, sums_ref, w_sc, d_sc, n_sc, r_sc, g_sc, sum_sc,
    ) = refs[cols:]
    block = x_refs[0].shape[0]
    t = pl.program_id(0)

    @pl.when(t == 0)
    def _():
        sum_sc[...] = jnp.zeros_like(sum_sc)
        g_sc[...] = jnp.zeros_like(g_sc)
        for b in range(cols):
            start = pl.multiple_of(meta_ref[b] * block, block)
            w_sc[relative_rows(b, block), :] = w_ref[pl.ds(start, block), :]

    for j, ref in enumerate((dq_ref, dk_ref, dv_ref)):
        d_sc[j * block : (j + 1) * block, :] = ref[...]
    mean = mean_ref[...]
    inv = inv_ref[...]
    r_sc[...] = matmul(w_sc[...], d_sc[...])
    total = jnp.zeros((1, tt), f32)
    cross = jnp.zeros((1, tt), f32)
    for b in range(cols):
        rows = relative_rows(b, block)
        n = (x_refs[b][...].astype(f32) - mean) * inv
        gain = 1.0 + mod_ref[rows, 0:1]
        n_sc[rows, :] = (n * gain + mod_ref[rows, 1:2]).astype(bf16)
        r = r_sc[rows, :]
        sum_sc[rows, 0:1] += jnp.sum(r * n, axis=1, keepdims=True)
        sum_sc[rows, 1:2] += jnp.sum(r, axis=1, keepdims=True)
        m = r * gain
        total = total + jnp.sum(m, axis=0, keepdims=True)
        cross = cross + jnp.sum(m * n, axis=0, keepdims=True)
    g_sc[...] += matmul(n_sc[...], d_sc[...], 1, 1)
    total = total * (1.0 / D)
    cross = cross * (1.0 / D)
    mine = jnp.where(
        jnp.logical_and(t * tt >= meta_ref[cols], t * tt < meta_ref[cols] + meta_ref[cols + 1]),
        1.0,
        0.0,
    )
    for b in range(cols):
        rows = relative_rows(b, block)
        n = (x_refs[b][...].astype(f32) - mean) * inv
        grad = inv * (r_sc[rows, :] * (1.0 + mod_ref[rows, 0:1]) - total - n * cross)
        half = relative_rows(b // 2, block)
        if b % 2 == 0:
            keep_ref[half, :] = grad + mine * kept_ref[half, :]
        else:
            send_ref[half, :] = grad.astype(bf16)

    @pl.when(t == pl.num_programs(0) - 1)
    def _():
        sums_ref[...] = sum_sc[...]
        for b in range(cols):
            start = pl.multiple_of(meta_ref[b] * block, block)
            g_ref[pl.ds(start, block), :] = g_sc[relative_rows(b, block), :].astype(bf16)


def project_back(meta, pieces, mean, inv, grads, w_qkv, mod, kept, tt=256):
    cols = len(pieces)
    block, tokens = pieces[0].shape
    part = kept.shape[1]
    tt = min(tt, part)
    width = w_qkv.shape[1]
    strip = lambda r: pl.BlockSpec((r, tt), lambda t, meta: (0, t))
    whole = lambda s: pl.BlockSpec(s, lambda t, meta: (0, 0), pipeline_mode=pl.Buffered(1))

    def kept_strip(t, meta):
        last = part // tt - 1
        return (0, jnp.clip(t - meta[cols] // tt, 0, last))

    return pl.pallas_call(
        partial(project_back_kernel, cols=cols, tt=tt),
        out_shape=[
            jax.ShapeDtypeStruct((D // 2, tokens), f32),
            jax.ShapeDtypeStruct((D // 2, tokens), bf16),
            jax.ShapeDtypeStruct((D, width), bf16),
            jax.ShapeDtypeStruct((D, 2), f32),
        ],
        grid_spec=pltpu.PrefetchScalarGridSpec(
            num_scalar_prefetch=1,
            grid=(tokens // tt,),
            in_specs=[strip(block)] * cols
            + [strip(1), strip(1)]
            + [strip(block)] * 3
            + [whole(w_qkv.shape), whole(mod.shape), pl.BlockSpec((D // 2, tt), kept_strip)],
            out_specs=[strip(D // 2), strip(D // 2), whole((D, width)), whole((D, 2))],
            scratch_shapes=[
                pltpu.VMEM((D, width), bf16),
                pltpu.VMEM((width, tt), bf16),
                pltpu.VMEM((D, tt), bf16),
                pltpu.VMEM((D, tt), f32),
                pltpu.VMEM((D, width), f32),
                pltpu.VMEM((D, 2), f32),
            ],
        ),
        compiler_params=pltpu.CompilerParams(vmem_limit_bytes=48 << 20),
        cost_estimate=pl.CostEstimate(
            flops=4 * D * width * tokens, bytes_accessed=8 * D * tokens, transcendentals=0
        ),
        name="project_back",
    )(meta, *pieces, mean, inv, *grads, w_qkv, mod, kept)


def time_features(time_steps, feature_count):
    half_dim = feature_count // 2
    frequency = jnp.exp(-math.log(10000.0) * jnp.arange(half_dim, dtype=f32) / half_dim)
    angles = time_steps.astype(f32)[:, None] * frequency[None, :]
    return jnp.concatenate([jnp.sin(angles), jnp.cos(angles)], axis=1)


def rotary_tables(places):
    inverse = jnp.exp(-math.log(10000.0) * jnp.arange(HALF, dtype=f32) * 2.0 / HEAD_DIM)
    angles = inverse[:, None] * places.astype(f32)[None, :]
    return jnp.cos(angles), jnp.sin(angles)


def local(
    chips,
    rows,
    hidden_in,
    query_key_value_weight,
    output_weight,
    up_weight,
    down_weight,
    w_time,
    segment_ids,
    positions,
    time_step,
    cotangent,
):
    cols = 2 * chips
    me = lax.axis_index("col")
    chip = me // 2
    core = me % 2
    row = lax.axis_index("row")
    block, tokens = hidden_in.shape
    part = tokens // chips

    def from_core(v):
        return lax.ppermute(v, "col", [(c, c ^ 1) for c in range(cols)])

    def from_chip(v, i):
        return lax.ppermute(v, "col", [(c, c ^ (2 * i)) for c in range(cols)])

    def from_col(v, b):
        return lax.ppermute(v, "col", [(c, c ^ b) for c in range(cols)])

    def from_row(v, a):
        return lax.ppermute(v, "row", [(r, r ^ a) for r in range(rows)])

    def gather_rows(v):
        return [v] + [from_row(v, a) for a in range(1, rows)]

    def gather_chips(v):
        return [v] + [from_chip(v, i) for i in range(1, chips)]

    def exchange_chips(pieces):
        return [pieces[0]] + [from_chip(pieces[i], i) for i in range(1, chips)]

    def token_part(v, i):
        return lax.dynamic_slice_in_dim(v, (chip ^ i) * part, part, axis=1)

    def place_parts(pieces):
        whole = jnp.zeros((pieces[0].shape[0], tokens), pieces[0].dtype)
        for i, piece in enumerate(pieces):
            whole = lax.dynamic_update_slice_in_dim(whole, piece, (chip ^ i) * part, axis=1)
        return whole

    def reorder(v):
        size = v.shape[0] // cols
        return jnp.concatenate(
            [lax.dynamic_slice_in_dim(v, (me ^ b) * size, size, axis=0) for b in range(cols)]
        )

    qkv_shard = jnp.transpose(query_key_value_weight, (1, 0, 2)).reshape(
        query_key_value_weight.shape[1], -1
    )
    qkv_width = qkv_shard.shape[1]
    qkv_shard = jnp.concatenate([qkv_shard, w_time.reshape(-1, block)], axis=1)
    qkv_all = lax.all_gather(qkv_shard, "row", axis=0, tiled=True)
    w_qkv = qkv_all[:, :qkv_width]
    w_time_all = qkv_all[:, qkv_width:].reshape(TEMB, 4, block)
    order = me ^ jnp.arange(cols, dtype=jnp.int32)
    meta = jnp.concatenate([order, jnp.stack([chip * part, jnp.int32(part)])])
    ff_shard = jnp.concatenate([up_weight, down_weight.T, output_weight.T], axis=1)
    ff_shards = gather_chips(ff_shard)
    ff_local = up_weight.shape[1]
    up_down = 2 * ff_local
    ff_packed = jnp.concatenate(
        [s[:, :ff_local] for s in ff_shards]
        + [s[:, ff_local:up_down] for s in ff_shards]
        + [s[:, up_down:] for s in ff_shards],
        axis=1,
    )
    ff_all = lax.all_gather(ff_packed, "row", axis=0, tiled=True)
    hidden = ff_local * chips
    w_out = reorder(ff_all[:, 2 * hidden :])

    pieces = []
    for piece in gather_chips(hidden_in):
        pieces += [piece, from_core(piece)]

    embedded = time_features(time_step, TEMB)[0]
    mod_own = jnp.sum(embedded[:, None, None] * w_time_all.astype(f32), axis=0)
    mod_all = jnp.stack([mod_own] + [from_col(mod_own, b) for b in range(1, cols)], axis=1)
    mod_columns = mod_all.reshape(4, D).T

    seg = segment_ids[0]
    pos = positions[0]
    cosine, sine = rotary_tables(pos)

    after, _ = lax.optimization_barrier((cotangent, pieces[-2]))
    cot_pieces = []
    for piece in exchange_chips([token_part(after, i) for i in range(chips)]):
        cot_pieces += [piece, from_core(piece)]

    q, k, v, mean_one, inv_one = project(meta, pieces, w_qkv, mod_columns, cosine, sine)
    q, k, v, *cot_pieces = lax.optimization_barrier((q, k, v, *cot_pieces))
    attended, lse = attend(q, k, v, seg, pos, segment_ids)
    att_part = jnp.concatenate(exchange_chips([token_part(attended, i) for i in range(chips)]))
    mid_share = matmul(w_out, att_part).astype(bf16)

    active, grad_up_b, normed_two, cot, middle, mean_two, inv_two, done_keep, done_send, dn_two = (
        feed_forward(
            meta, pieces, mid_share, from_core(mid_share), cot_pieces, ff_all, hidden, mod_columns
        )
    )
    dn_recv = from_core(dn_two)

    def rows_total(shares):
        return lax.psum_scatter(shares, "row", scatter_dimension=0, tiled=True)

    shares_ff = jnp.concatenate(
        [matmul(normed_two, grad_up_b, 1, 1).astype(bf16), matmul(cot, active, 1, 1).astype(bf16)],
        axis=1,
    )
    grads_ff = rows_total(reorder(shares_ff))
    done = (done_keep + from_core(done_send).astype(f32)).astype(bf16)
    done = done.reshape(chips, block, part)
    layer_result = place_parts(exchange_chips([done[i] for i in range(chips)]))

    grad_mid_kept, grad_branch, grad_att_part, sums_two = mid_back(
        cols, meta, dn_two, dn_recv, middle, mean_two, inv_two, cot, mod_columns, ff_all, hidden
    )
    grad_att_part = grad_att_part.reshape(chips, block, part)
    grad_attended = place_parts(exchange_chips([grad_att_part[i] for i in range(chips)]))
    shares_out = reorder(matmul(grad_branch, att_part, 1, 1).astype(bf16))
    grad_attended, shares_ff = lax.optimization_barrier((grad_attended, shares_ff))

    dq, dk, dv = attend_back(
        q, k, v, attended, grad_attended, lse, seg, pos, segment_ids, cosine, sine
    )
    keep, send, shares_qkv, sums_one = project_back(
        meta, pieces, mean_one, inv_one, (dq, dk, dv), w_qkv, mod_columns, grad_mid_kept
    )
    shares_qkv = jnp.concatenate([shares_qkv, shares_out], axis=1)
    shares_qkv, grads_ff = lax.optimization_barrier((shares_qkv, grads_ff))
    grads_qkv = rows_total(shares_qkv)
    total = (keep + from_core(send).astype(f32)).reshape(chips, block, tokens)
    grad_hidden = total[0]
    for i in range(1, chips):
        grad_hidden = grad_hidden + from_chip(total[i].astype(bf16), i).astype(f32)
    grad_hidden = grad_hidden.astype(bf16)

    pieces_ff = [
        jnp.concatenate(
            [
                grads_ff[:, i * ff_local : (i + 1) * ff_local],
                grads_ff[:, hidden + i * ff_local : hidden + (i + 1) * ff_local],
            ],
            axis=1,
        )
        for i in range(chips)
    ]
    summed = pieces_ff[0].astype(f32)
    for piece in exchange_chips(pieces_ff)[1:]:
        summed = summed + piece.astype(f32)
    summed_up = summed[:, :ff_local]
    summed_down = summed[:, ff_local:].T
    summed_qkv = jnp.transpose(
        grads_qkv[:, :qkv_width].astype(f32).reshape(-1, 3, block), (1, 0, 2)
    )
    pieces_out = [
        grads_qkv[:, qkv_width + i * block : qkv_width + (i + 1) * block] for i in range(chips)
    ]
    summed_out = pieces_out[0].astype(f32)
    for piece in exchange_chips(pieces_out)[1:]:
        summed_out = summed_out + piece.astype(f32)
    summed_out = summed_out.T

    once = (core == 0).astype(f32)
    grad_mod = jnp.concatenate([sums_one, sums_two * once], axis=1).T.reshape(4, cols, block)
    mod_total = grad_mod[:, 0]
    for b in range(1, cols):
        mod_total = mod_total + from_col(grad_mod[:, b], b)
    mod_total = jnp.concatenate([mod_total, jnp.broadcast_to(time_step.astype(f32), (1, block))])
    mod_rows = jnp.stack(gather_rows(mod_total))
    temb_share = w_time.shape[0]
    embed_rows = time_features(mod_rows[:, 4, 0], TEMB)
    embed_share = lax.dynamic_slice_in_dim(embed_rows, row * temb_share, temb_share, axis=1)
    grad_time = jnp.einsum(
        "st,skc->tkc", embed_share, mod_rows[:, :4], precision=highest_precision
    )
    return (layer_result, grad_hidden, summed_qkv, summed_out, summed_up, summed_down, grad_time)


def solution(mesh):
    in_specs = (
        P("col", "row"),
        P(None, "row", "col"),
        P("col", "row"),
        P("row", "col"),
        P("col", "row"),
        P("row", None, "col"),
        P("row", None),
        P("row", None),
        P("row"),
        P("col", "row"),
    )
    out_specs = (
        P("col", "row"),
        P("col", "row"),
        P(None, "row", "col"),
        P("col", "row"),
        P("row", "col"),
        P("col", "row"),
        P("row", None, "col"),
    )
    return jax.shard_map(
        partial(local, mesh.shape["col"] // 2, mesh.shape["row"]),
        mesh=mesh,
        in_specs=in_specs,
        out_specs=out_specs,
        check_vma=False,
    )
```

```python
from functools import partial
import math

import jax
import jax.numpy as jnp
from jax import lax
from jax.experimental import pallas as pl
from jax.experimental.pallas import tpu as pltpu
from jax.sharding import PartitionSpec as P

D = 1024
HEAD_DIM = 64
TEMB = 256
HALF = HEAD_DIM // 2
SCORE_SCALE = HEAD_DIM**-0.5
SCORE_LOG2 = SCORE_SCALE * math.log2(math.e)
SAFE_LOG2 = 60.0
STRIP = 512
SEGMENTS = 16
DEPTH = 128
AWAY = 2.0**100

norm_eps = 1e-05
masked_score = -1e30
highest_precision = lax.Precision.HIGHEST
f32 = jnp.float32
bf16 = jnp.bfloat16


def matmul(a, b, ca=1, cb=0):
    return lax.dot_general(a, b, (((ca,), (cb,)), ((), ())), preferred_element_type=f32)


def head_rows(h):
    return slice(h * HEAD_DIM, (h + 1) * HEAD_DIM)


def attend_kernel(
    lo_ref, n_ref, base_ref, q_ref, k_ref, v_ref, segq_ref, segs_ref, o_ref, lse_ref,
    k_sc, v_sc, q_sc, acc_sc, kmax_sc, *, heads, tq, tk,
):
    i = pl.program_id(0)
    tokens = k_ref.shape[1]
    rest = DEPTH - HEAD_DIM - SEGMENTS

    @pl.when(i == 0)
    def _():
        number = lax.broadcasted_iota(jnp.int32, (SEGMENTS, STRIP), 0)

        def strip(b, most):
            cols = pl.ds(pl.multiple_of(b * STRIP, STRIP), STRIP)
            member = jnp.where(number == segs_ref[:, cols], 1.0, 0.0).astype(bf16)
            for h in range(heads):
                kk = k_ref[head_rows(h), cols]
                k_sc[h, cols, :] = jnp.concatenate(
                    [kk, member, jnp.zeros((rest, STRIP), bf16)], axis=0
                ).T
                kf = kk.astype(f32)
                most = jnp.maximum(most, jnp.sum(kf * kf, axis=0, keepdims=True))
                v_sc[h, :HEAD_DIM, cols] = v_ref[head_rows(h), cols]
                v_sc[h, HEAD_DIM:, cols] = jnp.ones((8, STRIP), bf16)
            return most

        most = lax.fori_loop(0, tokens // STRIP, strip, jnp.zeros((1, STRIP), f32))
        kmax_sc[0] = jnp.max(most)

    number = lax.broadcasted_iota(jnp.int32, (SEGMENTS, tq), 0)
    away = jnp.where(number == segq_ref[...], 0.0, -AWAY).astype(bf16)
    qmost = jnp.zeros((1, tq), f32)
    for h in range(heads):
        qq = q_ref[head_rows(h), :]
        qf = qq.astype(f32)
        qmost = jnp.maximum(qmost, jnp.sum(qf * qf, axis=0, keepdims=True))
        q_sc[h, :HEAD_DIM, :] = qq
        q_sc[h, HEAD_DIM : HEAD_DIM + SEGMENTS, :] = away
        q_sc[h, HEAD_DIM + SEGMENTS :, :] = jnp.zeros((rest, tq), bf16)
    small = jnp.max(qmost) * kmax_sc[0] * (SCORE_LOG2 * SCORE_LOG2) <= SAFE_LOG2 * SAFE_LOG2
    lo = lo_ref[base_ref[0] + i]
    n = n_ref[base_ref[0] + i]
    acc_sc[...] = jnp.zeros_like(acc_sc)

    def finish(tops):
        for h in range(heads):
            total = acc_sc[h, HEAD_DIM : HEAD_DIM + 1, :]
            o_ref[head_rows(h), :] = (acc_sc[h, :HEAD_DIM, :] / total).astype(bf16)
            lse_ref[h : h + 1, :] = tops[h] + jnp.log2(total)

    @pl.when(small)
    def _():
        def step(j, _):
            off = pl.multiple_of(lo + j * tk, 128)
            scores = lambda h: matmul(k_sc[h, pl.ds(off, tk), :], q_sc[h])
            ahead = scores(0)
            for h in range(heads):
                s = ahead
                if h + 1 < heads:
                    ahead = scores(h + 1)
                p = jnp.exp2(s * SCORE_LOG2).astype(bf16)
                acc_sc[h] += matmul(v_sc[h, :, pl.ds(off, tk)], p)
            return 0

        lax.fori_loop(0, n, step, 0)
        finish([jnp.zeros((1, tq), f32)] * heads)

    @pl.when(jnp.logical_not(small))
    def _():
        def step(j, tops):
            off = pl.multiple_of(lo + j * tk, 128)
            grown = []
            for h in range(heads):
                s = matmul(k_sc[h, pl.ds(off, tk), :], q_sc[h]) * SCORE_LOG2
                top = jnp.maximum(tops[h], jnp.max(s, axis=0, keepdims=True))
                p = jnp.exp2(s - top).astype(bf16)
                acc_sc[h] = acc_sc[h] * jnp.exp2(tops[h] - top) + matmul(
                    v_sc[h, :, pl.ds(off, tk)], p
                )
                grown.append(top)
            return tuple(grown)

        start = tuple(jnp.full((1, tq), masked_score, f32) for _ in range(heads))
        finish(lax.fori_loop(0, n, step, start))


def block_ranges(segments, positions, tq, tk):
    tokens = segments.shape[0]
    blocks = tokens // tq
    firsts = jnp.arange(blocks, dtype=jnp.int32) * tq
    lo = ((firsts - positions[::tq]) // 128) * 128
    last = segments.reshape(blocks, tq)[:, -1]
    end = jnp.sum((segments[None, :] <= last[:, None]).astype(jnp.int32), axis=1)
    n = (end - lo + tk - 1) // tk
    lo = jnp.maximum(jnp.minimum(lo, tokens - n * tk), 0)
    return lo.astype(jnp.int32), n.astype(jnp.int32)


def resident(shape):
    return pl.BlockSpec(shape, lambda i, lo, n: (0, 0), pipeline_mode=pl.Buffered(1))


def attend(first, part, q, k, v, segments, positions, seg_rows, tq=512, tk=512):
    rows, tokens = q.shape
    heads = rows // HEAD_DIM
    lo, n = block_ranges(segments, positions, tq, tk)
    block = lambda r: pl.BlockSpec((r, tq), lambda i, lo, n, base: (0, base[0] + i))
    out = lambda r: pl.BlockSpec((r, tq), lambda i, lo, n, base: (0, i))
    whole = lambda s: pl.BlockSpec(
        s, lambda i, lo, n, base: (0, 0), pipeline_mode=pl.Buffered(1)
    )
    pairs = tokens * part * heads // 2
    return pl.pallas_call(
        partial(attend_kernel, heads=heads, tq=tq, tk=tk),
        out_shape=(
            jax.ShapeDtypeStruct((rows, part), bf16),
            jax.ShapeDtypeStruct((heads, part), f32),
        ),
        grid_spec=pltpu.PrefetchScalarGridSpec(
            num_scalar_prefetch=3,
            grid=(part // tq,),
            in_specs=[
                block(rows), whole((rows, tokens)), whole((rows, tokens)),
                block(1), whole((1, tokens)),
            ],
            out_specs=(out(rows), out(heads)),
            scratch_shapes=[
                pltpu.VMEM((heads, tokens, DEPTH), bf16),
                pltpu.VMEM((heads, HEAD_DIM + 8, tokens), bf16),
                pltpu.VMEM((heads, DEPTH, tq), bf16),
                pltpu.VMEM((heads, HEAD_DIM + 8, tq), f32),
                pltpu.SMEM((1,), f32),
            ],
        ),
        compiler_params=pltpu.CompilerParams(vmem_limit_bytes=48 << 20),
        cost_estimate=pl.CostEstimate(
            flops=16 * HEAD_DIM * pairs, bytes_accessed=8 * rows * tokens, transcendentals=pairs
        ),
        name="attend",
    )(lo, n, jnp.reshape(first // tq, (1,)).astype(jnp.int32), q, k, v, seg_rows, seg_rows)


def unrotate(g, cosine, sine):
    a = g[:HALF]
    b = g[HALF:]
    return jnp.concatenate([a * cosine + b * sine, b * cosine - a * sine], axis=0).astype(bf16)


def attend_back_kernel(
    lo_ref, n_ref, q_ref, k_ref, v_ref, o_ref, do_ref, lse_ref, segq_ref, segs_ref,
    cosq_ref, sinq_ref, cos_ref, sin_ref, dq_ref, dk_ref, dv_ref,
    k_sc, v_sc, segk_ref, dk_sc, dv_sc, dq_sc, *, heads, tq, tk,
):
    i = pl.program_id(0)
    tokens = k_ref.shape[1]

    @pl.when(i == 0)
    def _():
        def strip(b, _):
            cols = pl.ds(pl.multiple_of(b * STRIP, STRIP), STRIP)
            segk_ref[cols, :] = jnp.broadcast_to(segs_ref[:, cols], (128, STRIP)).T
            for h in range(heads):
                k_sc[h, cols, :] = k_ref[head_rows(h), cols].T
                v_sc[h, cols, :] = v_ref[head_rows(h), cols].T
            return 0

        lax.fori_loop(0, tokens // STRIP, strip, 0)
        dk_sc[...] = jnp.zeros_like(dk_sc)
        dv_sc[...] = jnp.zeros_like(dv_sc)

    segq = segq_ref[...]
    deltas = [
        jnp.sum(
            do_ref[head_rows(h), :].astype(f32) * o_ref[head_rows(h), :].astype(f32),
            axis=0,
            keepdims=True,
        )
        for h in range(heads)
    ]
    lo = lo_ref[i]
    dq_sc[...] = jnp.zeros_like(dq_sc)

    def step(j, _):
        off = pl.multiple_of(lo + j * tk, 128)
        cols = pl.ds(off, tk)
        same = segk_ref[cols, :][:, :1] == segq

        def products(h):
            rows = head_rows(h)
            return matmul(k_sc[h, cols, :], q_ref[rows, :]), matmul(v_sc[h, cols, :], do_ref[rows, :])

        ahead = products(0)
        for h in range(heads):
            rows = head_rows(h)
            s, dp = ahead
            if h + 1 < heads:
                ahead = products(h + 1)
            p = jnp.exp2(jnp.where(same, s * SCORE_LOG2 - lse_ref[h : h + 1, :], masked_score))
            ds = (p * (dp - deltas[h])).astype(bf16)
            dv_sc[rows, cols] += matmul(do_ref[rows, :], p.astype(bf16), 1, 1)
            dk_sc[rows, cols] += matmul(q_ref[rows, :], ds, 1, 1)
            dq_sc[rows, :] += matmul(k_ref[rows, cols], ds)
        return 0

    lax.fori_loop(0, n_ref[i], step, 0)
    cosine = cosq_ref[...] * SCORE_SCALE
    sine = sinq_ref[...] * SCORE_SCALE
    for h in range(heads):
        dq_ref[head_rows(h), :] = unrotate(dq_sc[head_rows(h), :], cosine, sine)

    @pl.when(i == pl.num_programs(0) - 1)
    def _():
        def strip(b, _):
            cols = pl.ds(pl.multiple_of(b * STRIP, STRIP), STRIP)
            c = cos_ref[:, cols] * SCORE_SCALE
            s = sin_ref[:, cols] * SCORE_SCALE
            for h in range(heads):
                dk_ref[head_rows(h), cols] = unrotate(dk_sc[head_rows(h), cols], c, s)
            dv_ref[:, cols] = dv_sc[:, cols].astype(bf16)
            return 0

        lax.fori_loop(0, tokens // STRIP, strip, 0)


def attend_back(
    q, k, v, o, do, lse, segments, positions, seg_rows, cosine, sine, tq=256, tk=512
):
    rows, tokens = q.shape
    heads = rows // HEAD_DIM
    lo, n = block_ranges(segments, positions, tq, tk)
    block = lambda r: pl.BlockSpec((r, tq), lambda i, lo, n: (0, i))
    whole = resident((rows, tokens))
    pairs = tokens * tokens * heads // 2
    return pl.pallas_call(
        partial(attend_back_kernel, heads=heads, tq=tq, tk=tk),
        out_shape=[jax.ShapeDtypeStruct((rows, tokens), bf16)] * 3,
        grid_spec=pltpu.PrefetchScalarGridSpec(
            num_scalar_prefetch=2,
            grid=(tokens // tq,),
            in_specs=[
                block(rows), whole, whole, block(rows), block(rows), block(heads),
                block(1), resident((1, tokens)), block(HALF), block(HALF),
                resident((HALF, tokens)), resident((HALF, tokens)),
            ],
            out_specs=[block(rows), whole, whole],
            scratch_shapes=[
                pltpu.VMEM((heads, tokens, HEAD_DIM), bf16),
                pltpu.VMEM((heads, tokens, HEAD_DIM), bf16),
                pltpu.VMEM((tokens, 128), jnp.int32),
                pltpu.VMEM((rows, tokens), f32),
                pltpu.VMEM((rows, tokens), f32),
                pltpu.VMEM((rows, tq), f32),
            ],
        ),
        compiler_params=pltpu.CompilerParams(vmem_limit_bytes=56 << 20),
        cost_estimate=pl.CostEstimate(
            flops=40 * HEAD_DIM * pairs, bytes_accessed=16 * rows * tokens, transcendentals=pairs
        ),
        name="attend_back",
    )(lo, n, q, k, v, o, do, lse, seg_rows, seg_rows, cosine, sine, cosine, sine)


def project_kernel(meta_ref, *refs, cols, rows, tt):
    x_refs = refs[:cols]
    w_ref, mod_ref, cos_ref, sin_ref, q_ref, k_ref, v_ref, mean_ref, inv_ref = refs[cols : cols + 9]
    w_sc, n_sc = refs[cols + 9 :]
    block = x_refs[0].shape[0]
    shard = D // rows

    @pl.when(pl.program_id(0) == 0)
    def _():
        for r in range(rows):
            start = pl.multiple_of(meta_ref[cols + 2 + r] * shard, shard)
            w_sc[:, r * shard : (r + 1) * shard] = w_ref[pl.ds(start, shard), :].T

    total = jnp.zeros((1, tt), f32)
    squares = jnp.zeros((1, tt), f32)
    for b in range(cols):
        x = x_refs[b][...].astype(f32)
        total = total + jnp.sum(x, axis=0, keepdims=True)
        squares = squares + jnp.sum(x * x, axis=0, keepdims=True)
    mean = total * (1.0 / D)
    inv = lax.rsqrt(squares * (1.0 / D) - mean * mean + norm_eps)
    mean_ref[...] = mean
    inv_ref[...] = inv
    for b in range(cols):
        own = slice(b * block, (b + 1) * block)
        n = (x_refs[b][...].astype(f32) - mean) * inv
        n_sc[own, :] = (n * (1.0 + mod_ref[own, 0:1]) + mod_ref[own, 1:2]).astype(bf16)
    out = matmul(w_sc[...], n_sc[...])
    cosine = cos_ref[...]
    sine = sin_ref[...]
    for j, ref in ((0, q_ref), (1, k_ref)):
        for h in range(block // HEAD_DIM):
            first = j * block + h * HEAD_DIM
            a = out[first : first + HALF]
            b = out[first + HALF : first + HEAD_DIM]
            ref[h * HEAD_DIM : h * HEAD_DIM + HALF, :] = (a * cosine - b * sine).astype(bf16)
            ref[h * HEAD_DIM + HALF : (h + 1) * HEAD_DIM, :] = (a * sine + b * cosine).astype(bf16)
    v_ref[...] = out[2 * block :].astype(bf16)


def project(rows, meta, pieces, w_qkv, mod, cosine, sine, tt=512):
    cols = len(pieces)
    block, tokens = pieces[0].shape
    strip = lambda r: pl.BlockSpec((r, tt), lambda t, order: (0, t))
    whole = lambda s: pl.BlockSpec(s, lambda t, order: (0, 0), pipeline_mode=pl.Buffered(1))
    return pl.pallas_call(
        partial(project_kernel, cols=cols, rows=rows, tt=tt),
        out_shape=[jax.ShapeDtypeStruct((block, tokens), bf16)] * 3
        + [jax.ShapeDtypeStruct((1, tokens), f32)] * 2,
        grid_spec=pltpu.PrefetchScalarGridSpec(
            num_scalar_prefetch=1,
            grid=(tokens // tt,),
            in_specs=[strip(block)] * cols
            + [whole(w_qkv.shape), whole(mod.shape), strip(HALF), strip(HALF)],
            out_specs=[strip(block)] * 3 + [strip(1)] * 2,
            scratch_shapes=[pltpu.VMEM((3 * block, D), bf16), pltpu.VMEM((D, tt), bf16)],
        ),
        compiler_params=pltpu.CompilerParams(vmem_limit_bytes=40 << 20),
        cost_estimate=pl.CostEstimate(
            flops=6 * D * block * tokens,
            bytes_accessed=2 * (D + 3 * block) * tokens,
            transcendentals=tokens,
        ),
        name="project",
    )(meta, *pieces, w_qkv, mod, cosine, sine)


def relative_rows(b, block):
    return slice(b * block, (b + 1) * block)


def feed_forward_kernel(meta_ref, *refs, cols, ff_local, tb, hb, sub):
    chips = cols // 2
    x_refs = refs[:cols]
    own_ref, recv_ref = refs[cols : cols + 2]
    cot_refs = refs[cols + 2 : 2 * cols + 2]
    up_refs = refs[2 * cols + 2 : 3 * cols + 2]
    down_refs = refs[3 * cols + 2 : 3 * cols + 2 + chips]
    (
        mod_ref, act_ref, du_ref, n_ref, cot_ref, mid_ref, mean_ref, inv_ref,
        keep_ref, send_ref, dn_ref, up_sc, down_sc, turned_sc, y_sc, dn_sc,
    ) = refs[3 * cols + 2 + chips :]
    block = x_refs[0].shape[0]
    h = pl.program_id(1)
    hs = pl.ds(pl.multiple_of(h * hb, hb), hb)

    @pl.when(pl.program_id(0) == 0)
    def _():
        for b in range(cols):
            up_sc[hs, relative_rows(b, block)] = up_refs[b][:, hs].T

    for i in range(chips):

        @pl.when(jnp.logical_and(pl.program_id(0) == 0, h * hb // ff_local == i))
        def _():
            from_cols = pl.ds(pl.multiple_of(h * hb - i * ff_local, hb), hb)
            for b in range(cols):
                start = pl.multiple_of(meta_ref[b] * block, block)
                weights = down_refs[i][pl.ds(start, block), from_cols]
                down_sc[relative_rows(b, block), hs] = weights
                turned_sc[hs, relative_rows(b, block)] = weights.T

    @pl.when(h == 0)
    def _():
        total = jnp.zeros((1, tb), f32)
        squares = jnp.zeros((1, tb), f32)
        for b in range(cols):
            rows = relative_rows(b, block)
            mid = (
                x_refs[b][...].astype(f32)
                + own_ref[rows, :].astype(f32)
                + recv_ref[relative_rows(b ^ 1, block), :].astype(f32)
            )
            mid_ref[rows, :] = mid
            total = total + jnp.sum(mid, axis=0, keepdims=True)
            squares = squares + jnp.sum(mid * mid, axis=0, keepdims=True)
            cot_ref[rows, :] = cot_refs[b][...]
        mean = total * (1.0 / D)
        inv = lax.rsqrt(squares * (1.0 / D) - mean * mean + norm_eps)
        mean_ref[...] = mean
        inv_ref[...] = inv
        for b in range(cols):
            rows = relative_rows(b, block)
            n = (mid_ref[rows, :] - mean) * inv
            n_ref[rows, :] = (n * (1.0 + mod_ref[rows, 2:3]) + mod_ref[rows, 3:4]).astype(bf16)
        y_sc[...] = jnp.zeros_like(y_sc)
        dn_sc[...] = jnp.zeros_like(dn_sc)

    def products(s):
        rows = pl.ds(pl.multiple_of(h * hb + s * sub, sub), sub)
        return matmul(up_sc[rows, :], n_ref[...]), matmul(turned_sc[rows, :], cot_ref[...])

    ahead = products(0)
    for s in range(hb // sub):
        up, grad_active = ahead
        if s + 1 < hb // sub:
            ahead = products(s + 1)
        cdf = 0.5 * (1.0 + lax.erf(up * math.sqrt(0.5)))
        density = jnp.exp(-0.5 * up * up) * (1.0 / math.sqrt(2.0 * math.pi))
        act_ref[s * sub : (s + 1) * sub, :] = (up * cdf).astype(bf16)
        du_ref[s * sub : (s + 1) * sub, :] = (grad_active * (cdf + up * density)).astype(bf16)
    for b in range(cols):
        rows = relative_rows(b, block)
        dn_sc[rows, :] += matmul(up_refs[b][:, hs], du_ref[...])
    y_sc[...] += matmul(down_sc[:, hs], act_ref[...])

    @pl.when(h == pl.num_programs(1) - 1)
    def _():
        dn_ref[...] = dn_sc[...].astype(bf16)
        for i in range(cols // 2):
            rows = relative_rows(2 * i, block)
            keep_ref[relative_rows(i, block), :] = mid_ref[rows, :] + y_sc[rows, :]
            send_ref[relative_rows(i, block), :] = y_sc[relative_rows(2 * i + 1, block), :].astype(
                bf16
            )


def feed_forward(meta, pieces, own, recv, cot_pieces, up_all, downs, mod, tb=512, hb=512):
    cols = len(pieces)
    ff_local = downs[0].shape[1]
    hidden = ff_local * len(downs)
    hb = min(hb, ff_local)
    block = pieces[0].shape[0]
    part = own.shape[1]
    tb = min(tb, part)
    strip = lambda r: pl.BlockSpec((r, tb), lambda t, h, meta: (0, t))
    tile = pl.BlockSpec((hb, tb), lambda t, h, meta: (h, t))

    def weight_rows(b):
        return pl.BlockSpec(
            (block, hidden), lambda t, h, meta: (meta[b], 0), pipeline_mode=pl.Buffered(1)
        )

    whole = lambda s: pl.BlockSpec(
        s, lambda t, h, meta: (0, 0), pipeline_mode=pl.Buffered(1)
    )

    shape = lambda r, kind: jax.ShapeDtypeStruct((r, part), kind)
    return pl.pallas_call(
        partial(feed_forward_kernel, cols=cols, ff_local=ff_local, tb=tb, hb=hb, sub=256),
        out_shape=[
            shape(hidden, bf16), shape(hidden, bf16), shape(D, bf16), shape(D, bf16),
            shape(D, f32), shape(1, f32), shape(1, f32), shape(D // 2, f32),
            shape(D // 2, bf16), shape(D, bf16),
        ],
        grid_spec=pltpu.PrefetchScalarGridSpec(
            num_scalar_prefetch=1,
            grid=(part // tb, hidden // hb),
            in_specs=[pl.BlockSpec((block, tb), lambda t, h, meta: (0, meta[cols] // tb + t))] * cols
            + [strip(D), strip(D)]
            + [strip(block)] * cols
            + [weight_rows(b) for b in range(cols)]
            + [whole(down.shape) for down in downs]
            + [whole(mod.shape)],
            out_specs=[
                tile, tile, strip(D), strip(D), strip(D), strip(1), strip(1),
                strip(D // 2), strip(D // 2), strip(D),
            ],
            scratch_shapes=[
                pltpu.VMEM((hidden, D), bf16),
                pltpu.VMEM((D, hidden), bf16),
                pltpu.VMEM((hidden, D), bf16),
                pltpu.VMEM((D, tb), f32),
                pltpu.VMEM((D, tb), f32),
            ],
        ),
        compiler_params=pltpu.CompilerParams(vmem_limit_bytes=58 << 20),
        cost_estimate=pl.CostEstimate(
            flops=8 * D * hidden * part,
            bytes_accessed=4 * D * hidden + 24 * D * part,
            transcendentals=2 * hidden * part,
        ),
        name="feed_forward",
    )(meta, *pieces, own, recv, *cot_pieces, *([up_all] * cols), *downs, mod)


def weight_grad_kernel(meta_ref, *refs, pairs, cols, starts):
    lefts = refs[:pairs]
    rights = refs[pairs : 2 * pairs]
    g_ref, g_sc = refs[-2:]
    block = D // cols
    j = pl.program_id(0)
    for p in range(pairs):

        @pl.when(jnp.logical_and(j >= starts[p], j < starts[p + 1]))
        def _():
            g_sc[...] = matmul(lefts[p][...], rights[p][...], 1, 1).astype(bf16)

    for b in range(cols):
        start = pl.multiple_of(meta_ref[b] * block, block)
        g_ref[pl.ds(start, block), :] = g_sc[relative_rows(b, block), :]


def weight_grads(cols, meta, pairs, places, width, into=None, step=512):
    sizes = [right.shape[0] for _, right in pairs]
    counts = [size // step for size in sizes]
    starts = [sum(counts[:p]) for p in range(len(pairs) + 1)]
    part = pairs[0][0].shape[1]

    def right_map(p):
        return lambda j, meta: (jnp.clip(j - starts[p], 0, counts[p] - 1), 0)

    def out_map(j, meta):
        column = places[0] // step + j
        for p in range(1, len(pairs)):
            column = jnp.where(j >= starts[p], places[p] // step + j - starts[p], column)
        return (0, column)

    lefts = [left for left, _ in pairs]
    rights = [right for _, right in pairs]
    whole = lambda s: pl.BlockSpec(s, lambda j, meta: (0, 0), pipeline_mode=pl.Buffered(1))
    more = [] if into is None else [into]
    return pl.pallas_call(
        partial(weight_grad_kernel, pairs=len(pairs), cols=cols, starts=starts),
        out_shape=jax.ShapeDtypeStruct((D, width), bf16),
        grid_spec=pltpu.PrefetchScalarGridSpec(
            num_scalar_prefetch=1,
            grid=(starts[-1],),
            in_specs=[whole((D, part))] * len(pairs)
            + [pl.BlockSpec((step, part), right_map(p)) for p in range(len(pairs))]
            + [pl.BlockSpec(memory_space=pl.ANY)] * len(more),
            out_specs=pl.BlockSpec((D, step), out_map),
            scratch_shapes=[pltpu.VMEM((D, step), bf16)],
        ),
        input_output_aliases={} if into is None else {1 + 2 * len(pairs): 0},
        compiler_params=pltpu.CompilerParams(vmem_limit_bytes=40 << 20),
        cost_estimate=pl.CostEstimate(
            flops=2 * D * part * sum(sizes),
            bytes_accessed=2 * (D * part * len(pairs) + (D + part) * sum(sizes)),
            transcendentals=0,
        ),
        name="weight_grads",
    )(meta, *lefts, *rights, *more)


def mid_back_kernel(meta_ref, *refs, cols):
    dn_ref, recv_ref, mid_ref, mean_ref, inv_ref, cot_ref, mod_ref = refs[:7]
    w_refs = refs[7 : 7 + cols]
    kept_ref, branch_ref, att_ref, sums_ref, r_sc, w_sc, sum_sc = refs[7 + cols :]
    block = w_refs[0].shape[0]
    tb = dn_ref.shape[1]
    t = pl.program_id(0)

    @pl.when(t == 0)
    def _():
        sum_sc[...] = jnp.zeros_like(sum_sc)
        for b in range(cols):
            w_sc[:, relative_rows(b, block)] = w_refs[b][...].T

    mean = mean_ref[...]
    inv = inv_ref[...]
    total = jnp.zeros((1, tb), f32)
    cross = jnp.zeros((1, tb), f32)
    for b in range(cols):
        rows = relative_rows(b, block)
        r = dn_ref[rows, :].astype(f32) + recv_ref[relative_rows(b ^ 1, block), :].astype(f32)
        n = (mid_ref[rows, :] - mean) * inv
        sum_sc[rows, 0:1] += jnp.sum(r * n, axis=1, keepdims=True)
        sum_sc[rows, 1:2] += jnp.sum(r, axis=1, keepdims=True)
        m = r * (1.0 + mod_ref[rows, 2:3])
        total = total + jnp.sum(m, axis=0, keepdims=True)
        cross = cross + jnp.sum(m * n, axis=0, keepdims=True)
        r_sc[rows, :] = m
    total = total * (1.0 / D)
    cross = cross * (1.0 / D)
    for b in range(cols):
        rows = relative_rows(b, block)
        n = (mid_ref[rows, :] - mean) * inv
        grad = cot_ref[rows, :].astype(f32) + inv * (r_sc[rows, :] - total - n * cross)
        if b % 2 == 0:
            kept_ref[relative_rows(b // 2, block), :] = grad
        branch_ref[rows, :] = grad.astype(bf16)
    att_ref[...] = matmul(w_sc[...], branch_ref[...]).astype(bf16)

    @pl.when(t == pl.num_programs(0) - 1)
    def _():
        sums_ref[...] = sum_sc[...]


def mid_back(cols, meta, own, recv, mid, mean, inv, cot, mod, up_all, hidden, tb=256):
    block = D // cols
    part = own.shape[1]
    tb = min(tb, part)
    width = up_all.shape[1] - hidden
    strip = lambda r: pl.BlockSpec((r, tb), lambda t, meta: (0, t))
    whole = lambda s: pl.BlockSpec(s, lambda t, meta: (0, 0), pipeline_mode=pl.Buffered(1))

    def weight_rows(b):
        return pl.BlockSpec(
            (block, width),
            lambda t, meta: (meta[b], hidden // width),
            pipeline_mode=pl.Buffered(1),
        )

    shape = lambda r, kind: jax.ShapeDtypeStruct((r, part), kind)
    return pl.pallas_call(
        partial(mid_back_kernel, cols=cols),
        out_shape=[
            shape(D // 2, f32), shape(D, bf16), shape(width, bf16),
            jax.ShapeDtypeStruct((D, 2), f32),
        ],
        grid_spec=pltpu.PrefetchScalarGridSpec(
            num_scalar_prefetch=1,
            grid=(part // tb,),
            in_specs=[strip(D), strip(D), strip(D), strip(1), strip(1), strip(D), whole(mod.shape)]
            + [weight_rows(b) for b in range(cols)],
            out_specs=[strip(D // 2), strip(D), strip(width), whole((D, 2))],
            scratch_shapes=[
                pltpu.VMEM((D, tb), f32),
                pltpu.VMEM((width, D), bf16),
                pltpu.VMEM((D, 2), f32),
            ],
        ),
        compiler_params=pltpu.CompilerParams(vmem_limit_bytes=40 << 20),
        cost_estimate=pl.CostEstimate(
            flops=2 * D * width * part, bytes_accessed=18 * D * part, transcendentals=0
        ),
        name="mid_back",
    )(meta, own, recv, mid, mean, inv, cot, mod, *([up_all] * cols))


def project_back_kernel(meta_ref, *refs, cols, rows, tt, middle):
    x_refs = refs[:cols]
    (
        mean_ref, inv_ref, dq_ref, dk_ref, dv_ref, w_ref, mod_ref, kept_ref,
        keep_early_ref, keep_late_ref, early_ref, late_ref, g_ref, sums_ref, w_sc, d_sc, n_sc, r_sc, g_sc, sum_sc,
    ) = refs[cols:]
    block = x_refs[0].shape[0]
    shard = D // rows
    t = pl.program_id(0)

    @pl.when(t == 0)
    def _():
        sum_sc[...] = jnp.zeros_like(sum_sc)
        g_sc[...] = jnp.zeros_like(g_sc)
        for r in range(rows):
            start = pl.multiple_of(meta_ref[cols + 2 + r] * shard, shard)
            w_sc[relative_rows(r, shard), :] = w_ref[pl.ds(start, shard), :]

    for j, ref in enumerate((dq_ref, dk_ref, dv_ref)):
        d_sc[j * block : (j + 1) * block, :] = ref[...]
    mean = mean_ref[...]
    inv = inv_ref[...]
    r_sc[...] = matmul(w_sc[...], d_sc[...])
    total = jnp.zeros((1, tt), f32)
    cross = jnp.zeros((1, tt), f32)
    for b in range(cols):
        own = relative_rows(b, block)
        n = (x_refs[b][...].astype(f32) - mean) * inv
        gain = 1.0 + mod_ref[own, 0:1]
        n_sc[own, :] = (n * gain + mod_ref[own, 1:2]).astype(bf16)
        r = r_sc[own, :]
        sum_sc[own, 0:1] += jnp.sum(r * n, axis=1, keepdims=True)
        sum_sc[own, 1:2] += jnp.sum(r, axis=1, keepdims=True)
        m = r * gain
        total = total + jnp.sum(m, axis=0, keepdims=True)
        cross = cross + jnp.sum(m * n, axis=0, keepdims=True)
    g_sc[...] += matmul(n_sc[...], d_sc[...], 1, 1)
    total = total * (1.0 / D)
    cross = cross * (1.0 / D)
    token = t * tt
    mine = jnp.where(
        jnp.logical_and(token >= meta_ref[cols], token < meta_ref[cols] + meta_ref[cols + 1]),
        1.0,
        0.0,
    )
    for b in range(cols):
        own = relative_rows(b, block)
        n = (x_refs[b][...].astype(f32) - mean) * inv
        grad = inv * (r_sc[own, :] * (1.0 + mod_ref[own, 0:1]) - total - n * cross)
        half = relative_rows(b // 2, block)
        if b % 2 == 0:
            value = grad + mine * kept_ref[half, :]
            early, late = keep_early_ref, keep_late_ref
        else:
            value = grad.astype(bf16)
            early, late = early_ref, late_ref

        @pl.when(t < middle)
        def _():
            early[half, :] = value

        @pl.when(t >= middle)
        def _():
            late[half, :] = value

    @pl.when(t == pl.num_programs(0) - 1)
    def _():
        sums_ref[...] = sum_sc[...]
        for r in range(rows):
            start = pl.multiple_of(meta_ref[cols + 2 + r] * shard, shard)
            g_ref[pl.ds(start, shard), :] = g_sc[relative_rows(r, shard), :].astype(g_ref.dtype)


def project_back(rows, meta, pieces, mean, inv, grads, w_qkv, mod, kept, tt=256):
    cols = len(pieces)
    block, tokens = pieces[0].shape
    part = kept.shape[1]
    tt = min(tt, part)
    width = w_qkv.shape[1]
    middle = tokens // tt // 2
    strip = lambda r: pl.BlockSpec((r, tt), lambda t, meta: (0, t))
    whole = lambda s: pl.BlockSpec(s, lambda t, meta: (0, 0), pipeline_mode=pl.Buffered(1))
    early = pl.BlockSpec((D // 2, tt), lambda t, meta: (0, jnp.minimum(t, middle - 1)))
    late = pl.BlockSpec((D // 2, tt), lambda t, meta: (0, jnp.maximum(t - middle, 0)))

    def kept_strip(t, meta):
        last = part // tt - 1
        return (0, jnp.clip(t - meta[cols] // tt, 0, last))

    half = jax.ShapeDtypeStruct((D // 2, tokens // 2), bf16)
    return pl.pallas_call(
        partial(project_back_kernel, cols=cols, rows=rows, tt=tt, middle=middle),
        out_shape=[
            jax.ShapeDtypeStruct((D // 2, tokens // 2), f32),
            jax.ShapeDtypeStruct((D // 2, tokens // 2), f32),
            half,
            half,
            jax.ShapeDtypeStruct((D, width), bf16),
            jax.ShapeDtypeStruct((D, 2), f32),
        ],
        grid_spec=pltpu.PrefetchScalarGridSpec(
            num_scalar_prefetch=1,
            grid=(tokens // tt,),
            in_specs=[strip(block)] * cols
            + [strip(1), strip(1)]
            + [strip(block)] * 3
            + [whole(w_qkv.shape), whole(mod.shape), pl.BlockSpec((D // 2, tt), kept_strip)],
            out_specs=[early, late, early, late, whole((D, width)), whole((D, 2))],
            scratch_shapes=[
                pltpu.VMEM((D, width), bf16),
                pltpu.VMEM((width, tt), bf16),
                pltpu.VMEM((D, tt), bf16),
                pltpu.VMEM((D, tt), f32),
                pltpu.VMEM((D, width), f32),
                pltpu.VMEM((D, 2), f32),
            ],
        ),
        compiler_params=pltpu.CompilerParams(vmem_limit_bytes=48 << 20),
        cost_estimate=pl.CostEstimate(
            flops=4 * D * width * tokens, bytes_accessed=8 * D * tokens, transcendentals=0
        ),
        name="project_back",
    )(meta, *pieces, mean, inv, *grads, w_qkv, mod, kept)


def time_features(time_steps, feature_count):
    half_dim = feature_count // 2
    frequency = jnp.exp(-math.log(10000.0) * jnp.arange(half_dim, dtype=f32) / half_dim)
    angles = time_steps.astype(f32)[:, None] * frequency[None, :]
    return jnp.concatenate([jnp.sin(angles), jnp.cos(angles)], axis=1)


def rotary_tables(places):
    inverse = jnp.exp(-math.log(10000.0) * jnp.arange(HALF, dtype=f32) * 2.0 / HEAD_DIM)
    angles = inverse[:, None] * places.astype(f32)[None, :]
    return jnp.cos(angles), jnp.sin(angles)


def local(
    chips,
    rows,
    hidden_in,
    query_key_value_weight,
    output_weight,
    up_weight,
    down_weight,
    w_time,
    segment_ids,
    positions,
    time_step,
    cotangent,
):
    cols = 2 * chips
    me = lax.axis_index("col")
    chip = me // 2
    core = me % 2
    row = lax.axis_index("row")
    block, tokens = hidden_in.shape
    part = tokens // chips

    def from_core(v):
        return lax.ppermute(v, "col", [(c, c ^ 1) for c in range(cols)])

    def from_chip(v, i):
        return lax.ppermute(v, "col", [(c, c ^ (2 * i)) for c in range(cols)])

    def from_col(v, b):
        return lax.ppermute(v, "col", [(c, c ^ b) for c in range(cols)])

    def from_row(v, a):
        return lax.ppermute(v, "row", [(r, r ^ a) for r in range(rows)])

    def gather_rows(v):
        return [v] + [from_row(v, a) for a in range(1, rows)]

    def gather_chips(v):
        return [v] + [from_chip(v, i) for i in range(1, chips)]

    def exchange_chips(pieces):
        return [pieces[0]] + [from_chip(pieces[i], i) for i in range(1, chips)]

    def token_part(v, i):
        return lax.dynamic_slice_in_dim(v, (chip ^ i) * part, part, axis=1)

    def place_parts(pieces):
        whole = jnp.zeros((pieces[0].shape[0], tokens), pieces[0].dtype)
        for i, piece in enumerate(pieces):
            whole = lax.dynamic_update_slice_in_dim(whole, piece, (chip ^ i) * part, axis=1)
        return whole

    def reorder(v):
        size = v.shape[0] // cols
        return jnp.concatenate(
            [lax.dynamic_slice_in_dim(v, (me ^ b) * size, size, axis=0) for b in range(cols)]
        )

    qkv_shard = jnp.transpose(query_key_value_weight, (1, 0, 2)).reshape(
        query_key_value_weight.shape[1], -1
    )
    qkv_width = qkv_shard.shape[1]
    ff_local = up_weight.shape[1]
    hidden = ff_local * chips
    first_shard = jnp.concatenate(
        [qkv_shard, w_time.reshape(-1, block), down_weight.T], axis=1
    )
    first_all = lax.all_gather(first_shard, "row", axis=0, tiled=True)
    w_qkv = first_all[:, :qkv_width]
    w_time_all = first_all[:, qkv_width : qkv_width + block].reshape(TEMB, 4, block)
    down_own = first_all[:, qkv_width + block :]
    order = me ^ jnp.arange(cols, dtype=jnp.int32)
    per_block = rows // cols
    shard_order = (
        order[:, None] * per_block + jnp.arange(per_block, dtype=jnp.int32)[None, :]
    ).reshape(rows)
    meta = jnp.concatenate([order, jnp.stack([chip * part, jnp.int32(part)]), shard_order])
    up_shards = gather_chips(jnp.concatenate([up_weight, output_weight.T], axis=1))
    up_packed = jnp.concatenate(
        [s[:, :ff_local] for s in up_shards] + [s[:, ff_local:] for s in up_shards], axis=1
    )
    up_all = lax.all_gather(up_packed, "row", axis=0, tiled=True)
    w_out = reorder(up_all[:, hidden:])

    pieces = []
    for piece in gather_chips(hidden_in):
        pieces += [piece, from_core(piece)]

    embedded = time_features(time_step, TEMB)[0]
    mod_own = jnp.sum(embedded[:, None, None] * w_time_all.astype(f32), axis=0)
    mod_all = jnp.stack([mod_own] + [from_col(mod_own, b) for b in range(1, cols)], axis=1)
    mod_columns = mod_all.reshape(4, D).T

    seg = segment_ids[0]
    pos = positions[0]
    cosine, sine = rotary_tables(pos)

    after, _ = lax.optimization_barrier((cotangent, pieces[-2]))
    cot_x = exchange_chips([token_part(after, i) for i in range(chips)])

    q, k, v, mean_one, inv_one = project(
        rows, meta, pieces, w_qkv, mod_columns, cosine, sine
    )
    down_own, _ = lax.optimization_barrier((down_own, cot_x[-1]))
    q, *cot_x = lax.optimization_barrier((q, *cot_x))
    downs = gather_chips(down_own)
    cot_pieces = []
    for piece in cot_x:
        cot_pieces += [piece, from_core(piece)]
    att_pieces = [None] * chips
    lse_pieces = [None] * chips
    for i in list(range(1, chips)) + [0]:
        att_pieces[i], lse_pieces[i] = attend(
            (chip ^ i) * part, part, q, k, v, seg, pos, segment_ids
        )
        if i + 1 == chips:
            q, cot_pieces, downs, att_pieces[1:] = lax.optimization_barrier(
                (q, cot_pieces, downs, att_pieces[1:])
            )
    att_part = jnp.concatenate(exchange_chips(att_pieces))
    attended = place_parts(att_pieces)
    lse = place_parts(lse_pieces)
    mid_share = matmul(w_out, att_part).astype(bf16)

    active, grad_up_b, normed_two, cot, middle, mean_two, inv_two, done_keep, done_send, dn_two = (
        feed_forward(
            meta, pieces, mid_share, from_core(mid_share), cot_pieces, up_all, downs, mod_columns
        )
    )
    dn_recv = from_core(dn_two)

    def rows_total(shares):
        return lax.psum_scatter(shares, "row", scatter_dimension=0, tiled=True)

    width = 2 * hidden + chips * block
    shares_ff = weight_grads(cols, meta, [(cot, active)], [hidden], width)
    done = (done_keep + from_core(done_send).astype(f32)).astype(bf16)
    done = done.reshape(chips, block, part)
    dn_recv, shares_ff, done = lax.optimization_barrier((dn_recv, shares_ff, done))
    grad_mid_kept, grad_branch, grad_att_part, sums_two = mid_back(
        cols, meta, dn_two, dn_recv, middle, mean_two, inv_two, cot, mod_columns, up_all, hidden
    )
    grad_att_part = grad_att_part.reshape(chips, block, part)
    grad_attended = exchange_chips([grad_att_part[i] for i in range(chips)])
    shares_ff = weight_grads(
        cols, meta, [(normed_two, grad_up_b), (grad_branch, att_part)], [0, 2 * hidden],
        width, shares_ff,
    )
    grad_attended, shares_ff = lax.optimization_barrier((grad_attended, shares_ff))
    grads_ff = rows_total(shares_ff)
    grad_attended = place_parts(grad_attended)
    done_pieces = exchange_chips([done[i] for i in range(chips)])

    dq, dk, dv = attend_back(
        q, k, v, attended, grad_attended, lse, seg, pos, segment_ids, cosine, sine
    )
    dq, dk, dv, done_pieces = lax.optimization_barrier((dq, dk, dv, done_pieces))
    layer_result = place_parts(done_pieces)
    keep_early, keep_late, send_early, send_late, shares_qkv, sums_one = project_back(
        rows, meta, pieces, mean_one, inv_one, (dq, dk, dv), w_qkv, mod_columns, grad_mid_kept
    )

    def core_total(keep, recv):
        total = (keep + recv.astype(f32)).reshape(chips, block, -1)
        return total[0], [total[i].astype(bf16) for i in range(1, chips)]

    def chip_total(total, away):
        for i in range(1, chips):
            total = total + from_chip(away[i - 1], i).astype(f32)
        return total.astype(bf16)

    recv_early, recv_late = from_core(send_early), from_core(send_late)
    total_early, away_early = core_total(keep_early, recv_early)
    recv_late, away_early = lax.optimization_barrier((recv_late, away_early))
    total_late, away_late = core_total(keep_late, recv_late)
    grad_hidden = jnp.concatenate(
        [chip_total(total_early, away_early), chip_total(total_late, away_late)], axis=1
    )

    once = (core == 0).astype(f32)
    grad_mod = jnp.concatenate([sums_one, sums_two * once], axis=1).T.reshape(4, cols, block)
    mod_total = grad_mod[:, 0]
    for b in range(1, cols):
        mod_total = mod_total + from_col(grad_mod[:, b], b)

    high = mod_total.astype(bf16)
    low = (mod_total - high.astype(f32)).astype(bf16)
    step = time_step[0]
    numbers = jnp.stack([step // 256, step % 256]).astype(bf16)
    extra = jnp.concatenate([high, low], axis=0)
    extra = jnp.concatenate(
        [extra, jnp.broadcast_to(jnp.tile(numbers, 4)[:, None], (8, qkv_width - block))], axis=1
    )
    shares = jnp.concatenate(
        [
            shares_qkv.reshape(rows, -1, qkv_width),
            jnp.broadcast_to(extra[None], (rows, 8, qkv_width)),
        ],
        axis=1,
    )
    row_shares = lax.all_to_all(shares, "row", split_axis=0, concat_axis=0, tiled=True)
    shard = D // rows
    grads_qkv = jnp.sum(row_shares[:, :shard].astype(f32), axis=0)
    extras = row_shares[:, shard:].astype(f32)
    mod_rows = extras[:, :4, :block] + extras[:, 4:, :block]
    steps = extras[:, 0, block] * 256.0 + extras[:, 1, block]

    pieces_ff = [
        jnp.concatenate(
            [
                grads_ff[:, i * ff_local : (i + 1) * ff_local],
                grads_ff[:, hidden + i * ff_local : hidden + (i + 1) * ff_local],
                grads_ff[:, 2 * hidden + i * block : 2 * hidden + (i + 1) * block],
            ],
            axis=1,
        )
        for i in range(chips)
    ]
    summed = pieces_ff[0].astype(f32)
    for piece in exchange_chips(pieces_ff)[1:]:
        summed = summed + piece.astype(f32)
    summed_up = summed[:, :ff_local]
    summed_down = summed[:, ff_local : 2 * ff_local].T
    summed_out = summed[:, 2 * ff_local :].T
    summed_qkv = jnp.transpose(grads_qkv.reshape(-1, 3, block), (1, 0, 2))

    temb_share = w_time.shape[0]
    embed_rows = time_features(steps, TEMB)
    embed_share = lax.dynamic_slice_in_dim(embed_rows, row * temb_share, temb_share, axis=1)
    grad_time = jnp.einsum("st,skc->tkc", embed_share, mod_rows, precision=highest_precision)
    return (layer_result, grad_hidden, summed_qkv, summed_out, summed_up, summed_down, grad_time)


def solution(mesh):
    in_specs = (
        P("col", "row"),
        P(None, "row", "col"),
        P("col", "row"),
        P("row", "col"),
        P("col", "row"),
        P("row", None, "col"),
        P("row", None),
        P("row", None),
        P("row"),
        P("col", "row"),
    )
    out_specs = (
        P("col", "row"),
        P("col", "row"),
        P(None, "row", "col"),
        P("col", "row"),
        P("row", "col"),
        P("col", "row"),
        P("row", None, "col"),
    )
    return jax.shard_map(
        partial(local, mesh.shape["col"] // 2, mesh.shape["row"]),
        mesh=mesh,
        in_specs=in_specs,
        out_specs=out_specs,
        check_vma=False,
    )
```

```python
from functools import partial
import math

import jax
import jax.numpy as jnp
from jax import lax
from jax.experimental import pallas as pl
from jax.experimental.pallas import tpu as pltpu
from jax.sharding import PartitionSpec as P

D = 1024
HEAD_DIM = 64
TEMB = 256
HALF = HEAD_DIM // 2
SCORE_SCALE = HEAD_DIM**-0.5
SCORE_LOG2 = SCORE_SCALE * math.log2(math.e)
SAFE_LOG2 = 60.0
STRIP = 512
SEGMENTS = 16
DEPTH = 128
AWAY = 2.0**100
EXTRA = 16
VMEM_LIMIT = 60 << 20

norm_eps = 1e-05
masked_score = -1e30
highest_precision = lax.Precision.HIGHEST
f32 = jnp.float32
bf16 = jnp.bfloat16


def matmul(a, b, ca=1, cb=0):
    return lax.dot_general(a, b, (((ca,), (cb,)), ((), ())), preferred_element_type=f32)


def head_rows(h):
    return slice(h * HEAD_DIM, (h + 1) * HEAD_DIM)


def attend_kernel(
    lo_ref, n_ref, base_ref, q_ref, k_ref, v_ref, segq_ref, segs_ref, o_ref, lse_ref,
    k_sc, v_sc, q_sc, acc_sc, kmax_sc, *, heads, tq, tk,
):
    i = pl.program_id(0)
    tokens = k_ref.shape[1]
    rest = DEPTH - HEAD_DIM - SEGMENTS

    @pl.when(i == 0)
    def _():
        number = lax.broadcasted_iota(jnp.int32, (SEGMENTS, STRIP), 0)

        def strip(b, most):
            cols = pl.ds(pl.multiple_of(b * STRIP, STRIP), STRIP)
            member = jnp.where(number == segs_ref[:, cols], 1.0, 0.0).astype(bf16)
            for h in range(heads):
                kk = k_ref[head_rows(h), cols]
                k_sc[h, cols, :] = jnp.concatenate(
                    [kk, member, jnp.zeros((rest, STRIP), bf16)], axis=0
                ).T
                kf = kk.astype(f32)
                most = jnp.maximum(most, jnp.sum(kf * kf, axis=0, keepdims=True))
                v_sc[h, :HEAD_DIM, cols] = v_ref[head_rows(h), cols]
                v_sc[h, HEAD_DIM:, cols] = jnp.ones((8, STRIP), bf16)
            return most

        most = lax.fori_loop(0, tokens // STRIP, strip, jnp.zeros((1, STRIP), f32))
        kmax_sc[0] = jnp.max(most)

    number = lax.broadcasted_iota(jnp.int32, (SEGMENTS, tq), 0)
    away = jnp.where(number == segq_ref[...], 0.0, -AWAY).astype(bf16)
    qmost = jnp.zeros((1, tq), f32)
    for h in range(heads):
        qq = q_ref[head_rows(h), :]
        qf = qq.astype(f32)
        qmost = jnp.maximum(qmost, jnp.sum(qf * qf, axis=0, keepdims=True))
        q_sc[h, :HEAD_DIM, :] = qq
        q_sc[h, HEAD_DIM : HEAD_DIM + SEGMENTS, :] = away
        q_sc[h, HEAD_DIM + SEGMENTS :, :] = jnp.zeros((rest, tq), bf16)
    small = jnp.max(qmost) * kmax_sc[0] * (SCORE_LOG2 * SCORE_LOG2) <= SAFE_LOG2 * SAFE_LOG2
    lo = lo_ref[base_ref[0] + i]
    n = n_ref[base_ref[0] + i]
    acc_sc[...] = jnp.zeros_like(acc_sc)

    def finish(tops):
        for h in range(heads):
            total = acc_sc[h, HEAD_DIM : HEAD_DIM + 1, :]
            o_ref[head_rows(h), :] = (acc_sc[h, :HEAD_DIM, :] / total).astype(bf16)
            lse_ref[h : h + 1, :] = tops[h] + jnp.log2(total)

    @pl.when(small)
    def _():
        def step(j, _):
            off = pl.multiple_of(lo + j * tk, 128)
            scores = lambda h: matmul(k_sc[h, pl.ds(off, tk), :], q_sc[h])
            ahead = scores(0)
            for h in range(heads):
                s = ahead
                if h + 1 < heads:
                    ahead = scores(h + 1)
                p = jnp.exp2(s * SCORE_LOG2).astype(bf16)
                acc_sc[h] += matmul(v_sc[h, :, pl.ds(off, tk)], p)
            return 0

        lax.fori_loop(0, n, step, 0)
        finish([jnp.zeros((1, tq), f32)] * heads)

    @pl.when(jnp.logical_not(small))
    def _():
        def step(j, tops):
            off = pl.multiple_of(lo + j * tk, 128)
            grown = []
            for h in range(heads):
                s = matmul(k_sc[h, pl.ds(off, tk), :], q_sc[h]) * SCORE_LOG2
                top = jnp.maximum(tops[h], jnp.max(s, axis=0, keepdims=True))
                p = jnp.exp2(s - top).astype(bf16)
                acc_sc[h] = acc_sc[h] * jnp.exp2(tops[h] - top) + matmul(
                    v_sc[h, :, pl.ds(off, tk)], p
                )
                grown.append(top)
            return tuple(grown)

        start = tuple(jnp.full((1, tq), masked_score, f32) for _ in range(heads))
        finish(lax.fori_loop(0, n, step, start))


def block_ranges(segments, positions, tq, tk):
    tokens = segments.shape[0]
    blocks = tokens // tq
    firsts = jnp.arange(blocks, dtype=jnp.int32) * tq
    lo = ((firsts - positions[::tq]) // 128) * 128
    last = segments.reshape(blocks, tq)[:, -1]
    end = jnp.sum((segments[None, :] <= last[:, None]).astype(jnp.int32), axis=1)
    n = (end - lo + tk - 1) // tk
    lo = jnp.maximum(jnp.minimum(lo, tokens - n * tk), 0)
    return lo.astype(jnp.int32), n.astype(jnp.int32)


def attend(first, part, q, k, v, segments, positions, seg_rows, tq=512, tk=512):
    rows, tokens = q.shape
    heads = rows // HEAD_DIM
    lo, n = block_ranges(segments, positions, tq, tk)
    block = lambda r: pl.BlockSpec((r, tq), lambda i, lo, n, base: (0, base[0] + i))
    out = lambda r: pl.BlockSpec((r, tq), lambda i, lo, n, base: (0, i))
    whole = lambda s: pl.BlockSpec(
        s, lambda i, lo, n, base: (0, 0), pipeline_mode=pl.Buffered(1)
    )
    pairs = tokens * part * heads // 2
    return pl.pallas_call(
        partial(attend_kernel, heads=heads, tq=tq, tk=tk),
        out_shape=(
            jax.ShapeDtypeStruct((rows, part), bf16),
            jax.ShapeDtypeStruct((heads, part), f32),
        ),
        grid_spec=pltpu.PrefetchScalarGridSpec(
            num_scalar_prefetch=3,
            grid=(part // tq,),
            in_specs=[
                block(rows), whole((rows, tokens)), whole((rows, tokens)),
                block(1), whole((1, tokens)),
            ],
            out_specs=(out(rows), out(heads)),
            scratch_shapes=[
                pltpu.VMEM((heads, tokens, DEPTH), bf16),
                pltpu.VMEM((heads, HEAD_DIM + 8, tokens), bf16),
                pltpu.VMEM((heads, DEPTH, tq), bf16),
                pltpu.VMEM((heads, HEAD_DIM + 8, tq), f32),
                pltpu.SMEM((1,), f32),
            ],
        ),
        compiler_params=pltpu.CompilerParams(vmem_limit_bytes=VMEM_LIMIT),
        cost_estimate=pl.CostEstimate(
            flops=16 * HEAD_DIM * pairs, bytes_accessed=8 * rows * tokens, transcendentals=pairs
        ),
        name="attend",
    )(lo, n, jnp.reshape(first // tq, (1,)).astype(jnp.int32), q, k, v, seg_rows, seg_rows)


def unrotate(g, cosine, sine):
    a = g[:HALF]
    b = g[HALF:]
    return jnp.concatenate([a * cosine + b * sine, b * cosine - a * sine], axis=0).astype(bf16)


def attend_back_kernel(lo_ref, n_ref, start_ref, *refs, chips, heads, tq, tk):
    q_ref, k_ref, v_ref = refs[:3]
    o_refs = refs[3 : 3 + chips]
    do_refs = refs[3 + chips : 3 + 2 * chips]
    lse_refs = refs[3 + 2 * chips : 3 + 3 * chips]
    (
        segq_ref, segs_ref, cosq_ref, sinq_ref, cos_ref, sin_ref, dq_ref, dk_ref, dv_ref,
        k_sc, v_sc, segk_ref, dk_sc, dv_sc, dq_sc, do_ref, lse_ref,
    ) = refs[3 + 3 * chips :]
    i = pl.program_id(0)

    def of_block(parts):
        value = parts[0][...]
        for p in range(1, chips):
            value = jnp.where(i >= start_ref[p], jnp.where(i < start_ref[p] + start_ref[chips], parts[p][...], value), value)
        return value

    tokens = k_ref.shape[1]

    @pl.when(i == 0)
    def _():
        def strip(b, _):
            cols = pl.ds(pl.multiple_of(b * STRIP, STRIP), STRIP)
            segk_ref[cols, :] = jnp.broadcast_to(segs_ref[:, cols], (128, STRIP)).T
            for h in range(heads):
                k_sc[h, cols, :] = k_ref[head_rows(h), cols].T
                v_sc[h, cols, :] = v_ref[head_rows(h), cols].T
            return 0

        lax.fori_loop(0, tokens // STRIP, strip, 0)
        dk_sc[...] = jnp.zeros_like(dk_sc)
        dv_sc[...] = jnp.zeros_like(dv_sc)

    segq = segq_ref[...]
    do_ref[...] = of_block(do_refs)
    lse_ref[...] = of_block(lse_refs)
    both = do_ref[...].astype(f32) * of_block(o_refs).astype(f32)
    deltas = [jnp.sum(both[head_rows(h)], axis=0, keepdims=True) for h in range(heads)]
    lo = lo_ref[i]
    dq_sc[...] = jnp.zeros_like(dq_sc)

    def step(j, _):
        off = pl.multiple_of(lo + j * tk, 128)
        cols = pl.ds(off, tk)
        same = segk_ref[cols, :][:, :1] == segq

        def products(h):
            rows = head_rows(h)
            return matmul(k_sc[h, cols, :], q_ref[rows, :]), matmul(v_sc[h, cols, :], do_ref[rows, :])

        ahead = products(0)
        for h in range(heads):
            rows = head_rows(h)
            s, dp = ahead
            if h + 1 < heads:
                ahead = products(h + 1)
            p = jnp.exp2(jnp.where(same, s * SCORE_LOG2 - lse_ref[h : h + 1, :], masked_score))
            ds = (p * (dp - deltas[h])).astype(bf16)
            dv_sc[rows, cols] += matmul(do_ref[rows, :], p.astype(bf16), 1, 1)
            dk_sc[rows, cols] += matmul(q_ref[rows, :], ds, 1, 1)
            dq_sc[rows, :] += matmul(k_ref[rows, cols], ds)
        return 0

    lax.fori_loop(0, n_ref[i], step, 0)
    cosine = cosq_ref[...] * SCORE_SCALE
    sine = sinq_ref[...] * SCORE_SCALE
    for h in range(heads):
        dq_ref[head_rows(h), :] = unrotate(dq_sc[head_rows(h), :], cosine, sine)

    @pl.when(i == pl.num_programs(0) - 1)
    def _():
        def strip(b, _):
            cols = pl.ds(pl.multiple_of(b * STRIP, STRIP), STRIP)
            c = cos_ref[:, cols] * SCORE_SCALE
            s = sin_ref[:, cols] * SCORE_SCALE
            for h in range(heads):
                dk_ref[head_rows(h), cols] = unrotate(dk_sc[head_rows(h), cols], c, s)
            dv_ref[:, cols] = dv_sc[:, cols].astype(bf16)
            return 0

        lax.fori_loop(0, tokens // STRIP, strip, 0)


def attend_back(
    chip, q, k, v, o, do, lse, segments, positions, seg_rows, cosine, sine, tq=256, tk=512
):
    rows, tokens = q.shape
    heads = rows // HEAD_DIM
    lo, n = block_ranges(segments, positions, tq, tk)
    chips = len(o)
    per_part = tokens // chips // tq
    starts = jnp.concatenate(
        [
            (chip ^ jnp.arange(chips, dtype=jnp.int32)) * per_part,
            jnp.full((1,), per_part, jnp.int32),
        ]
    )
    block = lambda r: pl.BlockSpec((r, tq), lambda i, lo, n, start: (0, i))
    resident = lambda s: pl.BlockSpec(
        s, lambda i, lo, n, start: (0, 0), pipeline_mode=pl.Buffered(1)
    )
    whole = resident((rows, tokens))

    def part_block(r, p):
        return pl.BlockSpec(
            (r, tq), lambda i, lo, n, start: (0, jnp.clip(i - start[p], 0, per_part - 1))
        )

    part_blocks = lambda r: [part_block(r, p) for p in range(chips)]
    pairs = tokens * tokens * heads // 2
    return pl.pallas_call(
        partial(attend_back_kernel, chips=chips, heads=heads, tq=tq, tk=tk),
        out_shape=[jax.ShapeDtypeStruct((rows, tokens), bf16)] * 3,
        grid_spec=pltpu.PrefetchScalarGridSpec(
            num_scalar_prefetch=3,
            grid=(tokens // tq,),
            in_specs=[
                block(rows), whole, whole,
                *part_blocks(rows), *part_blocks(rows), *part_blocks(heads),
                block(1), resident((1, tokens)), block(HALF), block(HALF),
                resident((HALF, tokens)), resident((HALF, tokens)),
            ],
            out_specs=[block(rows), whole, whole],
            scratch_shapes=[
                pltpu.VMEM((heads, tokens, HEAD_DIM), bf16),
                pltpu.VMEM((heads, tokens, HEAD_DIM), bf16),
                pltpu.VMEM((tokens, 128), jnp.int32),
                pltpu.VMEM((rows, tokens), f32),
                pltpu.VMEM((rows, tokens), f32),
                pltpu.VMEM((rows, tq), f32),
                pltpu.VMEM((rows, tq), bf16),
                pltpu.VMEM((heads, tq), f32),
            ],
        ),
        compiler_params=pltpu.CompilerParams(vmem_limit_bytes=VMEM_LIMIT),
        cost_estimate=pl.CostEstimate(
            flops=40 * HEAD_DIM * pairs, bytes_accessed=16 * rows * tokens, transcendentals=pairs
        ),
        name="attend_back",
    )(
        lo, n, starts, q, k, v, *o, *do, *lse, seg_rows, seg_rows, cosine, sine, cosine, sine
    )


def project_kernel(meta_ref, *refs, cols, rows, tt):
    x_refs = refs[:cols]
    w_ref, mod_ref, cos_ref, sin_ref, q_ref, k_ref, v_ref, mean_ref, inv_ref = refs[cols : cols + 9]
    w_sc, n_sc = refs[cols + 9 :]
    block = x_refs[0].shape[0]
    shard = D // rows

    @pl.when(pl.program_id(0) == 0)
    def _():
        for r in range(rows):
            start = pl.multiple_of(meta_ref[cols + 2 + r] * shard, shard)
            w_sc[:, r * shard : (r + 1) * shard] = w_ref[pl.ds(start, shard), :].T

    total = jnp.zeros((1, tt), f32)
    squares = jnp.zeros((1, tt), f32)
    for b in range(cols):
        x = x_refs[b][...].astype(f32)
        total = total + jnp.sum(x, axis=0, keepdims=True)
        squares = squares + jnp.sum(x * x, axis=0, keepdims=True)
    mean = total * (1.0 / D)
    inv = lax.rsqrt(squares * (1.0 / D) - mean * mean + norm_eps)
    mean_ref[...] = mean
    inv_ref[...] = inv
    for b in range(cols):
        own = slice(b * block, (b + 1) * block)
        n = (x_refs[b][...].astype(f32) - mean) * inv
        n_sc[own, :] = (n * (1.0 + mod_ref[own, 0:1]) + mod_ref[own, 1:2]).astype(bf16)
    out = matmul(w_sc[...], n_sc[...])
    cosine = cos_ref[...]
    sine = sin_ref[...]
    for j, ref in ((0, q_ref), (1, k_ref)):
        for h in range(block // HEAD_DIM):
            first = j * block + h * HEAD_DIM
            a = out[first : first + HALF]
            b = out[first + HALF : first + HEAD_DIM]
            ref[h * HEAD_DIM : h * HEAD_DIM + HALF, :] = (a * cosine - b * sine).astype(bf16)
            ref[h * HEAD_DIM + HALF : (h + 1) * HEAD_DIM, :] = (a * sine + b * cosine).astype(bf16)
    v_ref[...] = out[2 * block :].astype(bf16)


def project(rows, meta, pieces, w_qkv, mod, cosine, sine, tt=512):
    cols = len(pieces)
    block, tokens = pieces[0].shape
    strip = lambda r: pl.BlockSpec((r, tt), lambda t, order: (0, t))
    whole = lambda s: pl.BlockSpec(s, lambda t, order: (0, 0), pipeline_mode=pl.Buffered(1))
    return pl.pallas_call(
        partial(project_kernel, cols=cols, rows=rows, tt=tt),
        out_shape=[jax.ShapeDtypeStruct((block, tokens), bf16)] * 3
        + [jax.ShapeDtypeStruct((1, tokens), f32)] * 2,
        grid_spec=pltpu.PrefetchScalarGridSpec(
            num_scalar_prefetch=1,
            grid=(tokens // tt,),
            in_specs=[strip(block)] * cols
            + [whole(w_qkv.shape), whole(mod.shape), strip(HALF), strip(HALF)],
            out_specs=[strip(block)] * 3 + [strip(1)] * 2,
            scratch_shapes=[pltpu.VMEM((3 * block, D), bf16), pltpu.VMEM((D, tt), bf16)],
        ),
        compiler_params=pltpu.CompilerParams(vmem_limit_bytes=VMEM_LIMIT),
        cost_estimate=pl.CostEstimate(
            flops=6 * D * block * tokens,
            bytes_accessed=2 * (D + 3 * block) * tokens,
            transcendentals=tokens,
        ),
        name="project",
    )(meta, *pieces, w_qkv, mod, cosine, sine)


def out_project_kernel(meta_ref, *refs, cols):
    chips = cols // 2
    att_refs = refs[:chips]
    w_refs = refs[chips : chips + cols]
    share_ref, att_ref = refs[chips + cols :]
    block = att_refs[0].shape[0]
    for i in range(chips):
        att_ref[i * block : (i + 1) * block, :] = att_refs[i][...]
    for b in range(cols):
        share_ref[b * block : (b + 1) * block, :] = matmul(w_refs[b][...], att_ref[...]).astype(
            bf16
        )


def out_project(cols, meta, att, up_all, hidden, tb=512):
    block, part = att[0].shape
    tb = min(tb, part)
    width = up_all.shape[1] - hidden
    strip = lambda r: pl.BlockSpec((r, tb), lambda t, meta: (0, t))

    def weight_rows(b):
        return pl.BlockSpec(
            (block, width),
            lambda t, meta: (meta[b], hidden // width),
            pipeline_mode=pl.Buffered(1),
        )

    return pl.pallas_call(
        partial(out_project_kernel, cols=cols),
        out_shape=[
            jax.ShapeDtypeStruct((D, part), bf16), jax.ShapeDtypeStruct((width, part), bf16)
        ],
        grid_spec=pltpu.PrefetchScalarGridSpec(
            num_scalar_prefetch=1,
            grid=(part // tb,),
            in_specs=[strip(block)] * len(att) + [weight_rows(b) for b in range(cols)],
            out_specs=[strip(D), strip(width)],
        ),
        compiler_params=pltpu.CompilerParams(vmem_limit_bytes=VMEM_LIMIT),
        cost_estimate=pl.CostEstimate(
            flops=2 * D * width * part, bytes_accessed=2 * (D + 2 * width) * part, transcendentals=0
        ),
        name="out_project",
    )(meta, *att, *([up_all] * cols))


def relative_rows(b, block):
    return slice(b * block, (b + 1) * block)


def feed_forward_kernel(meta_ref, *refs, cols, ff_local, tb, sub):
    chips = cols // 2
    hidden = chips * ff_local
    x_refs = refs[:cols]
    own_ref, recv_ref = refs[cols : cols + 2]
    cot_refs = refs[cols + 2 : 2 * cols + 2]
    up_refs = refs[2 * cols + 2 : 3 * cols + 2]
    down_refs = refs[3 * cols + 2 : 3 * cols + 2 + chips]
    (
        mod_ref, act_ref, du_ref, n_ref, cot_ref, unit_ref,  inv_ref,
        keep_ref, send_ref, dn_ref, up_sc, down_sc, turned_sc, mid_sc,
    ) = refs[3 * cols + 2 + chips :]
    block = x_refs[0].shape[0]

    @pl.when(pl.program_id(0) == 0)
    def _():
        for b in range(cols):
            rows = relative_rows(b, block)
            start = pl.multiple_of(meta_ref[b] * block, block)
            for c in range(hidden // sub):
                up_sc[c * sub : (c + 1) * sub, rows] = up_refs[b][:, c * sub : (c + 1) * sub].T
            for i in range(chips):
                for c in range(ff_local // sub):
                    first = i * ff_local + c * sub
                    weights = down_refs[i][pl.ds(start, block), c * sub : (c + 1) * sub]
                    down_sc[rows, first : first + sub] = weights
                    turned_sc[first : first + sub, rows] = weights.T

    total = jnp.zeros((1, tb), f32)
    squares = jnp.zeros((1, tb), f32)
    for b in range(cols):
        rows = relative_rows(b, block)
        mid = (
            x_refs[b][...].astype(f32)
            + own_ref[rows, :].astype(f32)
            + recv_ref[relative_rows(b ^ 1, block), :].astype(f32)
        )
        mid_sc[rows, :] = mid
        total = total + jnp.sum(mid, axis=0, keepdims=True)
        squares = squares + jnp.sum(mid * mid, axis=0, keepdims=True)
        cot_ref[rows, :] = cot_refs[b][...]
    mean = total * (1.0 / D)
    inv = lax.rsqrt(squares * (1.0 / D) - mean * mean + norm_eps)
    inv_ref[...] = inv
    for b in range(cols):
        rows = relative_rows(b, block)
        n = (mid_sc[rows, :] - mean) * inv
        unit_ref[rows, :] = n.astype(bf16)
        n_ref[rows, :] = (n * (1.0 + mod_ref[rows, 2:3]) + mod_ref[rows, 3:4]).astype(bf16)

    def products(s):
        rows = slice(s * sub, (s + 1) * sub)
        return matmul(up_sc[rows, :], n_ref[...]), matmul(turned_sc[rows, :], cot_ref[...])

    ahead = products(0)
    for s in range(hidden // sub):
        up, grad_active = ahead
        if s + 1 < hidden // sub:
            ahead = products(s + 1)
        cdf = 0.5 * (1.0 + lax.erf(up * math.sqrt(0.5)))
        density = jnp.exp(-0.5 * up * up) * (1.0 / math.sqrt(2.0 * math.pi))
        act_ref[s * sub : (s + 1) * sub, :] = (up * cdf).astype(bf16)
        du_ref[s * sub : (s + 1) * sub, :] = (grad_active * (cdf + up * density)).astype(bf16)
    for b in range(cols):
        rows = relative_rows(b, block)
        dn_ref[rows, :] = matmul(up_refs[b][...], du_ref[...]).astype(bf16)
        y = matmul(down_sc[rows, :], act_ref[...])
        half = relative_rows(b // 2, block)
        if b % 2 == 0:
            keep_ref[half, :] = mid_sc[rows, :] + y
        else:
            send_ref[half, :] = y.astype(bf16)


def feed_forward(meta, pieces, own, recv, cot_pieces, up_all, downs, mod, tb=512):
    cols = len(pieces)
    ff_local = downs[0].shape[1]
    hidden = ff_local * len(downs)
    block = pieces[0].shape[0]
    part = own.shape[1]
    tb = min(tb, part)
    strip = lambda r: pl.BlockSpec((r, tb), lambda t, meta: (0, t))
    whole = lambda s: pl.BlockSpec(s, lambda t, meta: (0, 0), pipeline_mode=pl.Buffered(1))

    def weight_rows(b):
        return pl.BlockSpec(
            (block, hidden), lambda t, meta: (meta[b], 0), pipeline_mode=pl.Buffered(1)
        )

    shape = lambda r, kind: jax.ShapeDtypeStruct((r, part), kind)
    return pl.pallas_call(
        partial(feed_forward_kernel, cols=cols, ff_local=ff_local, tb=tb, sub=256),
        out_shape=[
            shape(hidden, bf16), shape(hidden, bf16), shape(D, bf16), shape(D, bf16),
            shape(D, bf16), shape(1, f32), shape(D // 2, f32), shape(D // 2, bf16),
            shape(D, bf16),
        ],
        grid_spec=pltpu.PrefetchScalarGridSpec(
            num_scalar_prefetch=1,
            grid=(part // tb,),
            in_specs=[pl.BlockSpec((block, tb), lambda t, meta: (0, meta[cols] // tb + t))] * cols
            + [strip(D), strip(D)]
            + [strip(block)] * cols
            + [weight_rows(b) for b in range(cols)]
            + [whole(down.shape) for down in downs]
            + [whole(mod.shape)],
            out_specs=[
                strip(hidden), strip(hidden), strip(D), strip(D), strip(D), strip(1),
                strip(D // 2), strip(D // 2), strip(D),
            ],
            scratch_shapes=[
                pltpu.VMEM((hidden, D), bf16),
                pltpu.VMEM((D, hidden), bf16),
                pltpu.VMEM((hidden, D), bf16),
                pltpu.VMEM((D, tb), f32),
            ],
        ),
        compiler_params=pltpu.CompilerParams(vmem_limit_bytes=VMEM_LIMIT),
        cost_estimate=pl.CostEstimate(
            flops=8 * D * hidden * part,
            bytes_accessed=4 * D * hidden + 24 * D * part,
            transcendentals=2 * hidden * part,
        ),
        name="feed_forward",
    )(meta, *pieces, own, recv, *cot_pieces, *([up_all] * cols), *downs, mod)


def weight_grad_kernel(meta_ref, *refs, pairs, cols, starts):
    lefts = refs[:pairs]
    rights = refs[pairs : 2 * pairs]
    g_ref, g_sc = refs[-2:]
    block = D // cols
    j = pl.program_id(0)
    for p in range(pairs):

        @pl.when(jnp.logical_and(j >= starts[p], j < starts[p + 1]))
        def _():
            g_sc[...] = matmul(lefts[p][...], rights[p][...], 1, 1).astype(bf16)

    for b in range(cols):
        start = pl.multiple_of(meta_ref[b] * block, block)
        g_ref[pl.ds(start, block), :] = g_sc[relative_rows(b, block), :]


def weight_grads(cols, meta, pairs, places, width, into=None, step=512):
    sizes = [right.shape[0] for _, right in pairs]
    counts = [size // step for size in sizes]
    starts = [sum(counts[:p]) for p in range(len(pairs) + 1)]
    part = pairs[0][0].shape[1]

    def right_map(p):
        return lambda j, meta: (jnp.clip(j - starts[p], 0, counts[p] - 1), 0)

    def out_map(j, meta):
        column = places[0] // step + j
        for p in range(1, len(pairs)):
            column = jnp.where(j >= starts[p], places[p] // step + j - starts[p], column)
        return (0, column)

    lefts = [left for left, _ in pairs]
    rights = [right for _, right in pairs]
    whole = lambda s: pl.BlockSpec(s, lambda j, meta: (0, 0), pipeline_mode=pl.Buffered(1))
    more = [] if into is None else [into]
    return pl.pallas_call(
        partial(weight_grad_kernel, pairs=len(pairs), cols=cols, starts=starts),
        out_shape=jax.ShapeDtypeStruct((D, width), bf16),
        grid_spec=pltpu.PrefetchScalarGridSpec(
            num_scalar_prefetch=1,
            grid=(starts[-1],),
            in_specs=[whole((D, part))] * len(pairs)
            + [pl.BlockSpec((step, part), right_map(p)) for p in range(len(pairs))]
            + [pl.BlockSpec(memory_space=pl.ANY)] * len(more),
            out_specs=pl.BlockSpec((D, step), out_map),
            scratch_shapes=[pltpu.VMEM((D, step), bf16)],
        ),
        input_output_aliases={} if into is None else {1 + 2 * len(pairs): 0},
        compiler_params=pltpu.CompilerParams(vmem_limit_bytes=VMEM_LIMIT),
        cost_estimate=pl.CostEstimate(
            flops=2 * D * part * sum(sizes),
            bytes_accessed=2 * (D * part * len(pairs) + (D + part) * sum(sizes)),
            transcendentals=0,
        ),
        name="weight_grads",
    )(meta, *lefts, *rights, *more)


def mid_back_kernel(meta_ref, *refs, cols):
    dn_ref, recv_ref, unit_ref, inv_ref, cot_ref, mod_ref = refs[:6]
    w_refs = refs[6 : 6 + cols]
    kept_ref, branch_ref, att_ref, sums_ref, r_sc, w_sc, sum_sc = refs[6 + cols :]
    block = w_refs[0].shape[0]
    tb = dn_ref.shape[1]
    t = pl.program_id(0)

    @pl.when(t == 0)
    def _():
        sum_sc[...] = jnp.zeros_like(sum_sc)
        for b in range(cols):
            w_sc[:, relative_rows(b, block)] = w_refs[b][...].T

    inv = inv_ref[...]
    total = jnp.zeros((1, tb), f32)
    cross = jnp.zeros((1, tb), f32)
    for b in range(cols):
        rows = relative_rows(b, block)
        r = dn_ref[rows, :].astype(f32) + recv_ref[relative_rows(b ^ 1, block), :].astype(f32)
        n = unit_ref[rows, :].astype(f32)
        sum_sc[rows, 0:1] += jnp.sum(r * n, axis=1, keepdims=True)
        sum_sc[rows, 1:2] += jnp.sum(r, axis=1, keepdims=True)
        m = r * (1.0 + mod_ref[rows, 2:3])
        total = total + jnp.sum(m, axis=0, keepdims=True)
        cross = cross + jnp.sum(m * n, axis=0, keepdims=True)
        r_sc[rows, :] = m
    total = total * (1.0 / D)
    cross = cross * (1.0 / D)
    for b in range(cols):
        rows = relative_rows(b, block)
        n = unit_ref[rows, :].astype(f32)
        grad = cot_ref[rows, :].astype(f32) + inv * (r_sc[rows, :] - total - n * cross)
        if b % 2 == 0:
            kept_ref[relative_rows(b // 2, block), :] = grad
        branch_ref[rows, :] = grad.astype(bf16)
    att_ref[...] = matmul(w_sc[...], branch_ref[...]).astype(bf16)

    @pl.when(t == pl.num_programs(0) - 1)
    def _():
        sums_ref[...] = sum_sc[...]


def mid_back(cols, meta, own, recv, unit, inv, cot, mod, up_all, hidden, tb=512):
    block = D // cols
    part = own.shape[1]
    tb = min(tb, part)
    width = up_all.shape[1] - hidden
    strip = lambda r: pl.BlockSpec((r, tb), lambda t, meta: (0, t))
    whole = lambda s: pl.BlockSpec(s, lambda t, meta: (0, 0), pipeline_mode=pl.Buffered(1))

    def weight_rows(b):
        return pl.BlockSpec(
            (block, width),
            lambda t, meta: (meta[b], hidden // width),
            pipeline_mode=pl.Buffered(1),
        )

    shape = lambda r, kind: jax.ShapeDtypeStruct((r, part), kind)
    return pl.pallas_call(
        partial(mid_back_kernel, cols=cols),
        out_shape=[
            shape(D // 2, f32), shape(D, bf16), shape(width, bf16),
            jax.ShapeDtypeStruct((D, 2), f32),
        ],
        grid_spec=pltpu.PrefetchScalarGridSpec(
            num_scalar_prefetch=1,
            grid=(part // tb,),
            in_specs=[strip(D), strip(D), strip(D), strip(1), strip(D), whole(mod.shape)]
            + [weight_rows(b) for b in range(cols)],
            out_specs=[strip(D // 2), strip(D), strip(width), whole((D, 2))],
            scratch_shapes=[
                pltpu.VMEM((D, tb), f32),
                pltpu.VMEM((width, D), bf16),
                pltpu.VMEM((D, 2), f32),
            ],
        ),
        compiler_params=pltpu.CompilerParams(vmem_limit_bytes=VMEM_LIMIT),
        cost_estimate=pl.CostEstimate(
            flops=2 * D * width * part, bytes_accessed=18 * D * part, transcendentals=0
        ),
        name="mid_back",
    )(meta, own, recv, unit, inv, cot, mod, *([up_all] * cols))


def project_back_kernel(meta_ref, *refs, cols, rows, tt):
    x_refs = refs[:cols]
    (
        mean_ref, inv_ref, dq_ref, dk_ref, dv_ref, w_ref, mod_ref, kept_ref,
        keep_ref, send_ref, g_ref, sums_ref, w_sc, d_sc, n_sc, r_sc, g_sc,
    ) = refs[cols:]
    block = x_refs[0].shape[0]
    shard = D // rows
    t = pl.program_id(0)

    @pl.when(t == 0)
    def _():
        g_sc[...] = jnp.zeros_like(g_sc)
        n_sc[D:, :] = jnp.ones((EXTRA, tt), bf16)
        column = jnp.zeros((1, w_sc.shape[1]), f32)
        for r in range(rows):
            start = pl.multiple_of(meta_ref[cols + 2 + r] * shard, shard)
            own = relative_rows(r, shard)
            weights = w_ref[pl.ds(start, shard), :]
            w_sc[own, :] = weights
            column = column + jnp.sum(
                weights.astype(f32) * (1.0 + mod_ref[own, 0:1]), axis=0, keepdims=True
            )
        number = lax.broadcasted_iota(jnp.int32, (EXTRA, w_sc.shape[1]), 0)
        terms = jnp.zeros((EXTRA, w_sc.shape[1]), f32)
        for i in range(3):
            term = column.astype(bf16).astype(f32)
            terms = jnp.where(number == i, term, terms)
            column = column - term
        w_sc[D:, :] = terms.astype(bf16)

    for j, ref in enumerate((dq_ref, dk_ref, dv_ref)):
        d_sc[j * block : (j + 1) * block, :] = ref[...]
    r_sc[...] = matmul(w_sc[...], d_sc[...])
    token = t * tt
    mine = jnp.where(
        jnp.logical_and(token >= meta_ref[cols], token < meta_ref[cols] + meta_ref[cols + 1]),
        1.0,
        0.0,
    )
    mean = mean_ref[...]
    inv = inv_ref[...]
    cross = jnp.zeros((1, tt), f32)
    for b in range(cols):
        own = relative_rows(b, block)
        n = (x_refs[b][...].astype(f32) - mean) * inv
        n_sc[own, :] = n.astype(bf16)
        m = r_sc[own, :] * (1.0 + mod_ref[own, 0:1])
        r_sc[own, :] = m
        cross = cross + jnp.sum(m * n, axis=0, keepdims=True)
    g_sc[...] += matmul(n_sc[...], d_sc[...], 1, 1)
    total = r_sc[D : D + 1, :] + r_sc[D + 1 : D + 2, :] + r_sc[D + 2 : D + 3, :]
    slope = inv * inv * cross * (1.0 / D)
    level = inv * total * (1.0 / D) - mean * slope
    for b in range(cols):
        own = relative_rows(b, block)
        grad = r_sc[own, :] * inv - x_refs[b][...].astype(f32) * slope - level
        half = relative_rows(b // 2, block)
        if b % 2 == 0:
            keep_ref[half, :] = grad + mine * kept_ref[half, :]
        else:
            send_ref[half, :] = grad.astype(bf16)

    @pl.when(t == pl.num_programs(0) - 1)
    def _():
        sums = g_sc[D : D + 1, :]
        for r in range(rows):
            start = pl.multiple_of(meta_ref[cols + 2 + r] * shard, shard)
            own = relative_rows(r, shard)
            weights = w_sc[own, :].astype(f32)
            products = g_sc[own, :]
            sums_ref[own, 0:1] = jnp.sum(weights * products, axis=1, keepdims=True)
            sums_ref[own, 1:2] = jnp.sum(weights * sums, axis=1, keepdims=True)
            gains = products * (1.0 + mod_ref[own, 0:1]) + mod_ref[own, 1:2] * sums
            g_ref[pl.ds(start, shard), :] = gains.astype(bf16)


def project_back(rows, meta, pieces, mean, inv, grads, w_qkv, mod, kept, tt=512):
    cols = len(pieces)
    block, tokens = pieces[0].shape
    part = kept.shape[1]
    tt = min(tt, part)
    width = w_qkv.shape[1]
    middle = tokens // tt // 2
    strip = lambda r: pl.BlockSpec((r, tt), lambda t, meta: (0, t))
    whole = lambda s: pl.BlockSpec(s, lambda t, meta: (0, 0), pipeline_mode=pl.Buffered(1))
    halves = pl.BlockSpec(
        (pl.Squeezed(), D // 2, tt), lambda t, meta: (t // middle, 0, t % middle)
    )

    def kept_strip(t, meta):
        last = part // tt - 1
        return (0, jnp.clip(t - meta[cols] // tt, 0, last))

    return pl.pallas_call(
        partial(project_back_kernel, cols=cols, rows=rows, tt=tt),
        out_shape=[
            jax.ShapeDtypeStruct((2, D // 2, tokens // 2), f32),
            jax.ShapeDtypeStruct((2, D // 2, tokens // 2), bf16),
            jax.ShapeDtypeStruct((D, width), bf16),
            jax.ShapeDtypeStruct((D, 2), f32),
        ],
        grid_spec=pltpu.PrefetchScalarGridSpec(
            num_scalar_prefetch=1,
            grid=(tokens // tt,),
            in_specs=[strip(block)] * cols
            + [strip(1), strip(1)]
            + [strip(block)] * 3
            + [whole(w_qkv.shape), whole(mod.shape), pl.BlockSpec((D // 2, tt), kept_strip)],
            out_specs=[halves, halves, whole((D, width)), whole((D, 2))],
            scratch_shapes=[
                pltpu.VMEM((D + EXTRA, width), bf16),
                pltpu.VMEM((width, tt), bf16),
                pltpu.VMEM((D + EXTRA, tt), bf16),
                pltpu.VMEM((D + EXTRA, tt), f32),
                pltpu.VMEM((D + EXTRA, width), f32),
            ],
        ),
        compiler_params=pltpu.CompilerParams(vmem_limit_bytes=VMEM_LIMIT),
        cost_estimate=pl.CostEstimate(
            flops=4 * D * width * tokens, bytes_accessed=8 * D * tokens, transcendentals=0
        ),
        name="project_back",
    )(meta, *pieces, mean, inv, *grads, w_qkv, mod, kept)


def time_features(time_steps, feature_count):
    half_dim = feature_count // 2
    frequency = jnp.exp(-math.log(10000.0) * jnp.arange(half_dim, dtype=f32) / half_dim)
    angles = time_steps.astype(f32)[:, None] * frequency[None, :]
    return jnp.concatenate([jnp.sin(angles), jnp.cos(angles)], axis=1)


def rotary_tables(places):
    inverse = jnp.exp(-math.log(10000.0) * jnp.arange(HALF, dtype=f32) * 2.0 / HEAD_DIM)
    angles = inverse[:, None] * places.astype(f32)[None, :]
    return jnp.cos(angles), jnp.sin(angles)


def local(
    chips,
    rows,
    hidden_in,
    query_key_value_weight,
    output_weight,
    up_weight,
    down_weight,
    w_time,
    segment_ids,
    positions,
    time_step,
    cotangent,
):
    cols = 2 * chips
    me = lax.axis_index("col")
    chip = me // 2
    core = me % 2
    row = lax.axis_index("row")
    block, tokens = hidden_in.shape
    part = tokens // chips

    def from_core(v):
        return lax.ppermute(v, "col", [(c, c ^ 1) for c in range(cols)])

    def from_chip(v, i):
        return lax.ppermute(v, "col", [(c, c ^ (2 * i)) for c in range(cols)])

    def from_col(v, b):
        return lax.ppermute(v, "col", [(c, c ^ b) for c in range(cols)])

    def from_row(v, a):
        return lax.ppermute(v, "row", [(r, r ^ a) for r in range(rows)])

    def gather_rows(v):
        return [v] + [from_row(v, a) for a in range(1, rows)]

    def gather_chips(v):
        return [v] + [from_chip(v, i) for i in range(1, chips)]

    def exchange_chips(pieces):
        return [pieces[0]] + [from_chip(pieces[i], i) for i in range(1, chips)]

    def token_part(v, i):
        return lax.dynamic_slice_in_dim(v, (chip ^ i) * part, part, axis=1)

    def place_parts(pieces):
        whole = jnp.zeros((pieces[0].shape[0], tokens), pieces[0].dtype)
        for i, piece in enumerate(pieces):
            whole = lax.dynamic_update_slice_in_dim(whole, piece, (chip ^ i) * part, axis=1)
        return whole

    qkv_shard = jnp.transpose(query_key_value_weight, (1, 0, 2)).reshape(
        query_key_value_weight.shape[1], -1
    )
    qkv_width = qkv_shard.shape[1]
    ff_local = up_weight.shape[1]
    hidden = ff_local * chips
    first_shard = jnp.concatenate(
        [qkv_shard, w_time.reshape(-1, block), down_weight.T], axis=1
    )
    first_all = lax.all_gather(first_shard, "row", axis=0, tiled=True)
    w_qkv = first_all[:, :qkv_width]
    w_time_all = first_all[:, qkv_width : qkv_width + block].reshape(TEMB, 4, block)
    down_own = first_all[:, qkv_width + block :]
    order = me ^ jnp.arange(cols, dtype=jnp.int32)
    per_block = rows // cols
    shard_order = (
        order[:, None] * per_block + jnp.arange(per_block, dtype=jnp.int32)[None, :]
    ).reshape(rows)
    meta = jnp.concatenate([order, jnp.stack([chip * part, jnp.int32(part)]), shard_order])
    up_shards = gather_chips(jnp.concatenate([up_weight, output_weight.T], axis=1))
    up_packed = jnp.concatenate(
        [s[:, :ff_local] for s in up_shards] + [s[:, ff_local:] for s in up_shards], axis=1
    )
    up_all = lax.all_gather(up_packed, "row", axis=0, tiled=True)

    pieces = []
    for piece in gather_chips(hidden_in):
        pieces += [piece, from_core(piece)]

    embedded = time_features(time_step, TEMB)[0]
    mod_own = jnp.sum(embedded[:, None, None] * w_time_all.astype(f32), axis=0)
    mod_all = jnp.stack([mod_own] + [from_col(mod_own, b) for b in range(1, cols)], axis=1)
    mod_columns = mod_all.reshape(4, D).T

    seg = segment_ids[0]
    pos = positions[0]
    cosine, sine = rotary_tables(pos)

    after, _ = lax.optimization_barrier((cotangent, pieces[-2]))
    cot_x = exchange_chips([token_part(after, i) for i in range(chips)])

    q, k, v, mean_one, inv_one = project(
        rows, meta, pieces, w_qkv, mod_columns, cosine, sine
    )
    q, *cot_x = lax.optimization_barrier((q, *cot_x))
    downs = gather_chips(down_own)
    cot_pieces = []
    for piece in cot_x:
        cot_pieces += [piece, from_core(piece)]
    att_pieces = [None] * chips
    lse_pieces = [None] * chips
    for i in list(range(1, chips)) + [0]:
        att_pieces[i], lse_pieces[i] = attend(
            (chip ^ i) * part, part, q, k, v, seg, pos, segment_ids
        )
        if i + 1 == chips:
            q, cot_pieces, downs, att_pieces[1:] = lax.optimization_barrier(
                (q, cot_pieces, downs, att_pieces[1:])
            )
    mid_share, att_part = out_project(
        cols, meta, exchange_chips(att_pieces), up_all, hidden
    )

    active, grad_up_b, normed_two, cot, unit_two, inv_two, done_keep, done_send, dn_two = (
        feed_forward(
            meta, pieces, mid_share, from_core(mid_share), cot_pieces, up_all, downs, mod_columns
        )
    )
    dn_recv = from_core(dn_two)

    def rows_total(shares):
        return lax.psum_scatter(shares, "row", scatter_dimension=0, tiled=True)

    width = 2 * hidden + chips * block
    shares_ff = weight_grads(cols, meta, [(cot, active)], [hidden], width)
    done = (done_keep + from_core(done_send).astype(f32)).astype(bf16)
    done = done.reshape(chips, block, part)
    dn_recv, shares_ff, done = lax.optimization_barrier((dn_recv, shares_ff, done))
    grad_mid_kept, grad_branch, grad_att_part, sums_two = mid_back(
        cols, meta, dn_two, dn_recv, unit_two, inv_two, cot, mod_columns, up_all, hidden
    )
    grad_att_part = grad_att_part.reshape(chips, block, part)
    grad_attended = exchange_chips([grad_att_part[i] for i in range(chips)])
    shares_ff = weight_grads(
        cols, meta, [(normed_two, grad_up_b), (grad_branch, att_part)], [0, 2 * hidden],
        width, shares_ff,
    )
    grad_attended, shares_ff = lax.optimization_barrier((grad_attended, shares_ff))
    grads_ff = rows_total(shares_ff)
    done_pieces = exchange_chips([done[i] for i in range(chips)])

    dq, dk, dv = attend_back(
        chip, q, k, v, att_pieces, grad_attended, lse_pieces, seg, pos, segment_ids, cosine, sine
    )
    dq, dk, dv, done_pieces = lax.optimization_barrier((dq, dk, dv, done_pieces))
    layer_result = place_parts(done_pieces)
    keep, send, shares_qkv, sums_one = project_back(
        rows, meta, pieces, mean_one, inv_one, (dq, dk, dv), w_qkv, mod_columns, grad_mid_kept
    )

    def core_total(keep, recv):
        total = (keep + recv.astype(f32)).reshape(chips, block, -1)
        return total[0], [total[i].astype(bf16) for i in range(1, chips)]

    def chip_total(total, away):
        for i in range(1, chips):
            total = total + from_chip(away[i - 1], i).astype(f32)
        return total.astype(bf16)

    recv = from_core(send)
    total_early, away_early = core_total(keep[0], recv[0])
    keep, away_early = lax.optimization_barrier((keep, away_early))
    total_late, away_late = core_total(keep[1], recv[1])
    shares_qkv, grads_ff, away_late = lax.optimization_barrier((shares_qkv, grads_ff, away_late))
    grad_hidden = jnp.concatenate(
        [chip_total(total_early, away_early), chip_total(total_late, away_late)], axis=1
    )

    once = (core == 0).astype(f32)
    grad_mod = jnp.concatenate([sums_one, sums_two * once], axis=1).T.reshape(4, cols, block)
    mod_total = grad_mod[:, 0]
    for b in range(1, cols):
        mod_total = mod_total + from_col(grad_mod[:, b], b)

    high = mod_total.astype(bf16)
    low = (mod_total - high.astype(f32)).astype(bf16)
    step = time_step[0]
    numbers = jnp.stack([step // 256, step % 256]).astype(bf16)
    extra = jnp.concatenate([high, low], axis=0)
    extra = jnp.concatenate(
        [extra, jnp.broadcast_to(jnp.tile(numbers, 4)[:, None], (8, qkv_width - block))], axis=1
    )
    shares = jnp.concatenate(
        [
            shares_qkv.reshape(rows, -1, qkv_width),
            jnp.broadcast_to(extra[None], (rows, 8, qkv_width)),
        ],
        axis=1,
    )
    row_shares = lax.all_to_all(shares, "row", split_axis=0, concat_axis=0, tiled=True)
    shard = D // rows
    grads_qkv = jnp.sum(row_shares[:, :shard].astype(f32), axis=0)
    extras = row_shares[:, shard:].astype(f32)
    mod_rows = extras[:, :4, :block] + extras[:, 4:, :block]
    steps = extras[:, 0, block] * 256.0 + extras[:, 1, block]

    pieces_ff = [
        jnp.concatenate(
            [
                grads_ff[:, i * ff_local : (i + 1) * ff_local],
                grads_ff[:, hidden + i * ff_local : hidden + (i + 1) * ff_local],
                grads_ff[:, 2 * hidden + i * block : 2 * hidden + (i + 1) * block],
            ],
            axis=1,
        )
        for i in range(chips)
    ]
    summed = pieces_ff[0].astype(f32)
    for piece in exchange_chips(pieces_ff)[1:]:
        summed = summed + piece.astype(f32)
    summed_up = summed[:, :ff_local]
    summed_down = summed[:, ff_local : 2 * ff_local].T
    summed_out = summed[:, 2 * ff_local :].T
    summed_qkv = jnp.transpose(grads_qkv.reshape(-1, 3, block), (1, 0, 2))

    temb_share = w_time.shape[0]
    embed_rows = time_features(steps, TEMB)
    embed_share = lax.dynamic_slice_in_dim(embed_rows, row * temb_share, temb_share, axis=1)
    grad_time = jnp.einsum("st,skc->tkc", embed_share, mod_rows, precision=highest_precision)
    return (layer_result, grad_hidden, summed_qkv, summed_out, summed_up, summed_down, grad_time)


def solution(mesh):
    in_specs = (
        P("col", "row"),
        P(None, "row", "col"),
        P("col", "row"),
        P("row", "col"),
        P("col", "row"),
        P("row", None, "col"),
        P("row", None),
        P("row", None),
        P("row"),
        P("col", "row"),
    )
    out_specs = (
        P("col", "row"),
        P("col", "row"),
        P(None, "row", "col"),
        P("col", "row"),
        P("row", "col"),
        P("col", "row"),
        P("row", None, "col"),
    )
    return jax.shard_map(
        partial(local, mesh.shape["col"] // 2, mesh.shape["row"]),
        mesh=mesh,
        in_specs=in_specs,
        out_specs=out_specs,
        check_vma=False,
    )
```

```python
from functools import partial
import math

import jax
import jax.numpy as jnp
from jax import lax
from jax.experimental import pallas as pl
from jax.experimental.pallas import tpu as pltpu
from jax.sharding import PartitionSpec as P

D = 1024
HEAD_DIM = 64
TEMB = 256
HALF = HEAD_DIM // 2
SCORE_SCALE = HEAD_DIM**-0.5
SCORE_LOG2 = SCORE_SCALE * math.log2(math.e)
SAFE_LOG2 = 60.0
STRIP = 512
SEGMENTS = 16
DEPTH = 128
AWAY = 2.0**100
EXTRA = 16
VMEM_LIMIT = 60 << 20

norm_eps = 1e-05
masked_score = -1e30
highest_precision = lax.Precision.HIGHEST
f32 = jnp.float32
bf16 = jnp.bfloat16


def matmul(a, b, ca=1, cb=0):
    return lax.dot_general(a, b, (((ca,), (cb,)), ((), ())), preferred_element_type=f32)


def head_rows(h):
    return slice(h * HEAD_DIM, (h + 1) * HEAD_DIM)


def attend_kernel(
    lo_ref, n_ref, base_ref, q_ref, k_ref, v_ref, segq_ref, segs_ref, o_ref, lse_ref,
    k_sc, v_sc, q_sc, acc_sc, kmax_sc, *, heads, tq, tk,
):
    i = pl.program_id(0)
    tokens = k_ref.shape[1]
    rest = DEPTH - HEAD_DIM - SEGMENTS

    @pl.when(i == 0)
    def _():
        number = lax.broadcasted_iota(jnp.int32, (SEGMENTS, STRIP), 0)

        def strip(b, most):
            cols = pl.ds(pl.multiple_of(b * STRIP, STRIP), STRIP)
            member = jnp.where(number == segs_ref[:, cols], 1.0, 0.0).astype(bf16)
            for h in range(heads):
                kk = k_ref[head_rows(h), cols]
                k_sc[h, cols, :] = jnp.concatenate(
                    [kk, member, jnp.zeros((rest, STRIP), bf16)], axis=0
                ).T
                kf = kk.astype(f32)
                most = jnp.maximum(most, jnp.sum(kf * kf, axis=0, keepdims=True))
                v_sc[h, :HEAD_DIM, cols] = v_ref[head_rows(h), cols]
                v_sc[h, HEAD_DIM:, cols] = jnp.ones((8, STRIP), bf16)
            return most

        most = lax.fori_loop(0, tokens // STRIP, strip, jnp.zeros((1, STRIP), f32))
        kmax_sc[0] = jnp.max(most)

    number = lax.broadcasted_iota(jnp.int32, (SEGMENTS, tq), 0)
    away = jnp.where(number == segq_ref[...], 0.0, -AWAY).astype(bf16)
    qmost = jnp.zeros((1, tq), f32)
    for h in range(heads):
        qq = q_ref[head_rows(h), :]
        qf = qq.astype(f32)
        qmost = jnp.maximum(qmost, jnp.sum(qf * qf, axis=0, keepdims=True))
        q_sc[h, :HEAD_DIM, :] = qq
        q_sc[h, HEAD_DIM : HEAD_DIM + SEGMENTS, :] = away
        q_sc[h, HEAD_DIM + SEGMENTS :, :] = jnp.zeros((rest, tq), bf16)
    small = jnp.max(qmost) * kmax_sc[0] * (SCORE_LOG2 * SCORE_LOG2) <= SAFE_LOG2 * SAFE_LOG2
    lo = lo_ref[base_ref[0] + i]
    n = n_ref[base_ref[0] + i]
    more = n_ref[tokens // tq + base_ref[0] + i]
    acc_sc[...] = jnp.zeros_like(acc_sc)

    def finish(tops):
        for h in range(heads):
            total = acc_sc[h, HEAD_DIM : HEAD_DIM + 1, :]
            o_ref[head_rows(h), :] = (acc_sc[h, :HEAD_DIM, :] / total).astype(bf16)
            lse_ref[h : h + 1, :] = tops[h] + jnp.log2(total)

    @pl.when(small)
    def _():
        def tile(off, keys):
            off = pl.multiple_of(off, 128)
            scores = lambda h: matmul(k_sc[h, pl.ds(off, keys), :], q_sc[h])
            ahead = scores(0)
            for h in range(heads):
                s = ahead
                if h + 1 < heads:
                    ahead = scores(h + 1)
                p = jnp.exp2(s * SCORE_LOG2).astype(bf16)
                acc_sc[h] += matmul(v_sc[h, :, pl.ds(off, keys)], p)

        def step(j, _):
            tile(lo + j * tk, tk)
            return 0

        lax.fori_loop(0, n, step, 0)

        @pl.when(more > 0)
        def _():
            tile(lo + n * tk, tk // 2)

        finish([jnp.zeros((1, tq), f32)] * heads)

    @pl.when(jnp.logical_not(small))
    def _():
        def step(j, tops):
            off = pl.multiple_of(lo + j * (tk // 2), 128)
            grown = []
            for h in range(heads):
                s = matmul(k_sc[h, pl.ds(off, tk // 2), :], q_sc[h]) * SCORE_LOG2
                top = jnp.maximum(tops[h], jnp.max(s, axis=0, keepdims=True))
                p = jnp.exp2(s - top).astype(bf16)
                acc_sc[h] = acc_sc[h] * jnp.exp2(tops[h] - top) + matmul(
                    v_sc[h, :, pl.ds(off, tk // 2)], p
                )
                grown.append(top)
            return tuple(grown)

        start = tuple(jnp.full((1, tq), masked_score, f32) for _ in range(heads))
        finish(lax.fori_loop(0, 2 * n + more, step, start))


def block_ranges(segments, positions, tq, tk):
    tokens = segments.shape[0]
    blocks = tokens // tq
    firsts = jnp.arange(blocks, dtype=jnp.int32) * tq
    lo = ((firsts - positions[::tq]) // 128) * 128
    last = segments.reshape(blocks, tq)[:, -1]
    end = jnp.sum((segments[None, :] <= last[:, None]).astype(jnp.int32), axis=1)
    halves = (end - lo + tk // 2 - 1) // (tk // 2)
    lo = jnp.minimum(lo, tokens - halves * (tk // 2))
    n = jnp.concatenate([halves // 2, halves % 2])
    return lo.astype(jnp.int32), n.astype(jnp.int32)


def attend(first, part, q, k, v, segments, positions, seg_rows, tq=512, tk=512):
    rows, tokens = q.shape
    heads = rows // HEAD_DIM
    lo, n = block_ranges(segments, positions, tq, tk)
    block = lambda r: pl.BlockSpec((r, tq), lambda i, lo, n, base: (0, base[0] + i))
    out = lambda r: pl.BlockSpec((r, tq), lambda i, lo, n, base: (0, i))
    whole = lambda s: pl.BlockSpec(
        s, lambda i, lo, n, base: (0, 0), pipeline_mode=pl.Buffered(1)
    )
    pairs = tokens * part * heads // 2
    return pl.pallas_call(
        partial(attend_kernel, heads=heads, tq=tq, tk=tk),
        out_shape=(
            jax.ShapeDtypeStruct((rows, part), bf16),
            jax.ShapeDtypeStruct((heads, part), f32),
        ),
        grid_spec=pltpu.PrefetchScalarGridSpec(
            num_scalar_prefetch=3,
            grid=(part // tq,),
            in_specs=[
                block(rows), whole((rows, tokens)), whole((rows, tokens)),
                block(1), whole((1, tokens)),
            ],
            out_specs=(out(rows), out(heads)),
            scratch_shapes=[
                pltpu.VMEM((heads, tokens, DEPTH), bf16),
                pltpu.VMEM((heads, HEAD_DIM + 8, tokens), bf16),
                pltpu.VMEM((heads, DEPTH, tq), bf16),
                pltpu.VMEM((heads, HEAD_DIM + 8, tq), f32),
                pltpu.SMEM((1,), f32),
            ],
        ),
        compiler_params=pltpu.CompilerParams(vmem_limit_bytes=VMEM_LIMIT),
        cost_estimate=pl.CostEstimate(
            flops=16 * HEAD_DIM * pairs, bytes_accessed=8 * rows * tokens, transcendentals=pairs
        ),
        name="attend",
    )(lo, n, jnp.reshape(first // tq, (1,)).astype(jnp.int32), q, k, v, seg_rows, seg_rows)


def unrotate(g, cosine, sine):
    a = g[:HALF]
    b = g[HALF:]
    return jnp.concatenate([a * cosine + b * sine, b * cosine - a * sine], axis=0).astype(bf16)


def attend_back_kernel(lo_ref, n_ref, start_ref, *refs, chips, heads, tq, tk):
    q_ref, k_ref, v_ref = refs[:3]
    o_refs = refs[3 : 3 + chips]
    do_refs = refs[3 + chips : 3 + 2 * chips]
    lse_refs = refs[3 + 2 * chips : 3 + 3 * chips]
    (
        segq_ref, segs_ref, cosq_ref, sinq_ref, cos_ref, sin_ref, dq_ref, dk_ref, dv_ref,
        k_sc, v_sc, segk_ref, dk_sc, dv_sc, dq_sc, do_ref, lse_ref,
    ) = refs[3 + 3 * chips :]
    i = pl.program_id(0)

    def of_block(parts):
        value = parts[0][...]
        for p in range(1, chips):
            value = jnp.where(i >= start_ref[p], jnp.where(i < start_ref[p] + start_ref[chips], parts[p][...], value), value)
        return value

    tokens = k_ref.shape[1]

    @pl.when(i == 0)
    def _():
        def strip(b, _):
            cols = pl.ds(pl.multiple_of(b * STRIP, STRIP), STRIP)
            segk_ref[cols, :] = jnp.broadcast_to(segs_ref[:, cols], (128, STRIP)).T
            for h in range(heads):
                k_sc[h, cols, :] = k_ref[head_rows(h), cols].T
                v_sc[h, cols, :] = v_ref[head_rows(h), cols].T
            return 0

        lax.fori_loop(0, tokens // STRIP, strip, 0)
        dk_sc[...] = jnp.zeros_like(dk_sc)
        dv_sc[...] = jnp.zeros_like(dv_sc)

    segq = segq_ref[...]
    do_ref[...] = of_block(do_refs)
    lse_ref[...] = of_block(lse_refs)
    both = do_ref[...].astype(f32) * of_block(o_refs).astype(f32)
    deltas = [jnp.sum(both[head_rows(h)], axis=0, keepdims=True) for h in range(heads)]
    lo = lo_ref[i]
    dq_sc[...] = jnp.zeros_like(dq_sc)

    def tile(off, keys):
        off = pl.multiple_of(off, 128)
        cols = pl.ds(off, keys)
        same = segk_ref[cols, :][:, :1] == segq

        def products(h):
            rows = head_rows(h)
            return matmul(k_sc[h, cols, :], q_ref[rows, :]), matmul(v_sc[h, cols, :], do_ref[rows, :])

        ahead = products(0)
        for h in range(heads):
            rows = head_rows(h)
            s, dp = ahead
            if h + 1 < heads:
                ahead = products(h + 1)
            p = jnp.exp2(jnp.where(same, s * SCORE_LOG2 - lse_ref[h : h + 1, :], masked_score))
            ds = (p * (dp - deltas[h])).astype(bf16)
            dv_sc[rows, cols] += matmul(do_ref[rows, :], p.astype(bf16), 1, 1)
            dk_sc[rows, cols] += matmul(q_ref[rows, :], ds, 1, 1)
            dq_sc[rows, :] += matmul(k_ref[rows, cols], ds)

    def step(j, _):
        tile(lo + j * tk, tk)
        return 0

    lax.fori_loop(0, n_ref[i], step, 0)

    @pl.when(n_ref[tokens // tq + i] > 0)
    def _():
        tile(lo + n_ref[i] * tk, tk // 2)

    cosine = cosq_ref[...] * SCORE_SCALE
    sine = sinq_ref[...] * SCORE_SCALE
    for h in range(heads):
        dq_ref[head_rows(h), :] = unrotate(dq_sc[head_rows(h), :], cosine, sine)

    @pl.when(i == pl.num_programs(0) - 1)
    def _():
        def strip(b, _):
            cols = pl.ds(pl.multiple_of(b * STRIP, STRIP), STRIP)
            c = cos_ref[:, cols] * SCORE_SCALE
            s = sin_ref[:, cols] * SCORE_SCALE
            for h in range(heads):
                dk_ref[head_rows(h), cols] = unrotate(dk_sc[head_rows(h), cols], c, s)
            dv_ref[:, cols] = dv_sc[:, cols].astype(bf16)
            return 0

        lax.fori_loop(0, tokens // STRIP, strip, 0)


def attend_back(
    chip, q, k, v, o, do, lse, segments, positions, seg_rows, cosine, sine, tq=256, tk=512
):
    rows, tokens = q.shape
    heads = rows // HEAD_DIM
    lo, n = block_ranges(segments, positions, tq, tk)
    chips = len(o)
    per_part = tokens // chips // tq
    starts = jnp.concatenate(
        [
            (chip ^ jnp.arange(chips, dtype=jnp.int32)) * per_part,
            jnp.full((1,), per_part, jnp.int32),
        ]
    )
    block = lambda r: pl.BlockSpec((r, tq), lambda i, lo, n, start: (0, i))
    resident = lambda s: pl.BlockSpec(
        s, lambda i, lo, n, start: (0, 0), pipeline_mode=pl.Buffered(1)
    )
    whole = resident((rows, tokens))

    def part_block(r, p):
        return pl.BlockSpec(
            (r, tq), lambda i, lo, n, start: (0, jnp.clip(i - start[p], 0, per_part - 1))
        )

    part_blocks = lambda r: [part_block(r, p) for p in range(chips)]
    pairs = tokens * tokens * heads // 2
    return pl.pallas_call(
        partial(attend_back_kernel, chips=chips, heads=heads, tq=tq, tk=tk),
        out_shape=[jax.ShapeDtypeStruct((rows, tokens), bf16)] * 3,
        grid_spec=pltpu.PrefetchScalarGridSpec(
            num_scalar_prefetch=3,
            grid=(tokens // tq,),
            in_specs=[
                block(rows), whole, whole,
                *part_blocks(rows), *part_blocks(rows), *part_blocks(heads),
                block(1), resident((1, tokens)), block(HALF), block(HALF),
                resident((HALF, tokens)), resident((HALF, tokens)),
            ],
            out_specs=[block(rows), whole, whole],
            scratch_shapes=[
                pltpu.VMEM((heads, tokens, HEAD_DIM), bf16),
                pltpu.VMEM((heads, tokens, HEAD_DIM), bf16),
                pltpu.VMEM((tokens, 128), jnp.int32),
                pltpu.VMEM((rows, tokens), f32),
                pltpu.VMEM((rows, tokens), f32),
                pltpu.VMEM((rows, tq), f32),
                pltpu.VMEM((rows, tq), bf16),
                pltpu.VMEM((heads, tq), f32),
            ],
        ),
        compiler_params=pltpu.CompilerParams(vmem_limit_bytes=VMEM_LIMIT),
        cost_estimate=pl.CostEstimate(
            flops=40 * HEAD_DIM * pairs, bytes_accessed=16 * rows * tokens, transcendentals=pairs
        ),
        name="attend_back",
    )(
        lo, n, starts, q, k, v, *o, *do, *lse, seg_rows, seg_rows, cosine, sine, cosine, sine
    )


def project_kernel(meta_ref, *refs, cols, rows, tt):
    x_refs = refs[:cols]
    w_ref, mod_ref, cos_ref, sin_ref, q_ref, k_ref, v_ref, mean_ref, inv_ref = refs[cols : cols + 9]
    w_sc, n_sc = refs[cols + 9 :]
    block = x_refs[0].shape[0]
    shard = D // rows

    @pl.when(pl.program_id(0) == 0)
    def _():
        for r in range(rows):
            start = pl.multiple_of(meta_ref[cols + 2 + r] * shard, shard)
            w_sc[:, r * shard : (r + 1) * shard] = w_ref[pl.ds(start, shard), :].T

    total = jnp.zeros((1, tt), f32)
    squares = jnp.zeros((1, tt), f32)
    for b in range(cols):
        x = x_refs[b][...].astype(f32)
        total = total + jnp.sum(x, axis=0, keepdims=True)
        squares = squares + jnp.sum(x * x, axis=0, keepdims=True)
    mean = total * (1.0 / D)
    inv = lax.rsqrt(squares * (1.0 / D) - mean * mean + norm_eps)
    mean_ref[...] = mean
    inv_ref[...] = inv
    for b in range(cols):
        own = slice(b * block, (b + 1) * block)
        n = (x_refs[b][...].astype(f32) - mean) * inv
        n_sc[own, :] = (n * (1.0 + mod_ref[own, 0:1]) + mod_ref[own, 1:2]).astype(bf16)
    out = matmul(w_sc[...], n_sc[...])
    cosine = cos_ref[...]
    sine = sin_ref[...]
    for j, ref in ((0, q_ref), (1, k_ref)):
        for h in range(block // HEAD_DIM):
            first = j * block + h * HEAD_DIM
            a = out[first : first + HALF]
            b = out[first + HALF : first + HEAD_DIM]
            ref[h * HEAD_DIM : h * HEAD_DIM + HALF, :] = (a * cosine - b * sine).astype(bf16)
            ref[h * HEAD_DIM + HALF : (h + 1) * HEAD_DIM, :] = (a * sine + b * cosine).astype(bf16)
    v_ref[...] = out[2 * block :].astype(bf16)


def project(rows, meta, pieces, w_qkv, mod, cosine, sine, tt=1024):
    cols = len(pieces)
    block, tokens = pieces[0].shape
    strip = lambda r: pl.BlockSpec((r, tt), lambda t, order: (0, t))
    whole = lambda s: pl.BlockSpec(s, lambda t, order: (0, 0), pipeline_mode=pl.Buffered(1))
    return pl.pallas_call(
        partial(project_kernel, cols=cols, rows=rows, tt=tt),
        out_shape=[jax.ShapeDtypeStruct((block, tokens), bf16)] * 3
        + [jax.ShapeDtypeStruct((1, tokens), f32)] * 2,
        grid_spec=pltpu.PrefetchScalarGridSpec(
            num_scalar_prefetch=1,
            grid=(tokens // tt,),
            in_specs=[strip(block)] * cols
            + [whole(w_qkv.shape), whole(mod.shape), strip(HALF), strip(HALF)],
            out_specs=[strip(block)] * 3 + [strip(1)] * 2,
            scratch_shapes=[pltpu.VMEM((3 * block, D), bf16), pltpu.VMEM((D, tt), bf16)],
        ),
        compiler_params=pltpu.CompilerParams(vmem_limit_bytes=VMEM_LIMIT),
        cost_estimate=pl.CostEstimate(
            flops=6 * D * block * tokens,
            bytes_accessed=2 * (D + 3 * block) * tokens,
            transcendentals=tokens,
        ),
        name="project",
    )(meta, *pieces, w_qkv, mod, cosine, sine)


def out_project_kernel(meta_ref, *refs, cols):
    chips = cols // 2
    att_refs = refs[:chips]
    w_refs = refs[chips : chips + cols]
    share_ref, att_ref = refs[chips + cols :]
    block = att_refs[0].shape[0]
    for i in range(chips):
        att_ref[i * block : (i + 1) * block, :] = att_refs[i][...]
    for b in range(cols):
        share_ref[b * block : (b + 1) * block, :] = matmul(w_refs[b][...], att_ref[...]).astype(
            bf16
        )


def out_project(cols, meta, att, up_all, hidden, tb=512):
    block, part = att[0].shape
    tb = min(tb, part)
    width = up_all.shape[1] - hidden
    strip = lambda r: pl.BlockSpec((r, tb), lambda t, meta: (0, t))

    def weight_rows(b):
        return pl.BlockSpec(
            (block, width),
            lambda t, meta: (meta[b], hidden // width),
            pipeline_mode=pl.Buffered(1),
        )

    return pl.pallas_call(
        partial(out_project_kernel, cols=cols),
        out_shape=[
            jax.ShapeDtypeStruct((D, part), bf16), jax.ShapeDtypeStruct((width, part), bf16)
        ],
        grid_spec=pltpu.PrefetchScalarGridSpec(
            num_scalar_prefetch=1,
            grid=(part // tb,),
            in_specs=[strip(block)] * len(att) + [weight_rows(b) for b in range(cols)],
            out_specs=[strip(D), strip(width)],
        ),
        compiler_params=pltpu.CompilerParams(vmem_limit_bytes=VMEM_LIMIT),
        cost_estimate=pl.CostEstimate(
            flops=2 * D * width * part, bytes_accessed=2 * (D + 2 * width) * part, transcendentals=0
        ),
        name="out_project",
    )(meta, *att, *([up_all] * cols))


def relative_rows(b, block):
    return slice(b * block, (b + 1) * block)


def feed_forward_kernel(meta_ref, *refs, cols, ff_local, tb, sub):
    chips = cols // 2
    hidden = chips * ff_local
    x_refs = refs[:cols]
    own_ref, recv_ref = refs[cols : cols + 2]
    cot_refs = refs[cols + 2 : 2 * cols + 2]
    up_refs = refs[2 * cols + 2 : 3 * cols + 2]
    down_refs = refs[3 * cols + 2 : 3 * cols + 2 + chips]
    (
        mod_ref, act_ref, du_ref, n_ref, cot_ref, unit_ref,  inv_ref,
        keep_ref, send_ref, dn_ref, up_sc, down_sc, mid_sc,
    ) = refs[3 * cols + 2 + chips :]
    block = x_refs[0].shape[0]

    @pl.when(pl.program_id(0) == 0)
    def _():
        for b in range(cols):
            rows = relative_rows(b, block)
            start = pl.multiple_of(meta_ref[b] * block, block)
            up_sc[rows, :] = up_refs[b][...]
            for i in range(chips):
                for c in range(ff_local // sub):
                    first = i * ff_local + c * sub
                    weights = down_refs[i][pl.ds(start, block), c * sub : (c + 1) * sub]
                    down_sc[rows, first : first + sub] = weights

    total = jnp.zeros((1, tb), f32)
    squares = jnp.zeros((1, tb), f32)
    for b in range(cols):
        rows = relative_rows(b, block)
        mid = (
            x_refs[b][...].astype(f32)
            + own_ref[rows, :].astype(f32)
            + recv_ref[relative_rows(b ^ 1, block), :].astype(f32)
        )
        mid_sc[rows, :] = mid
        total = total + jnp.sum(mid, axis=0, keepdims=True)
        squares = squares + jnp.sum(mid * mid, axis=0, keepdims=True)
        cot_ref[rows, :] = cot_refs[b][...]
    mean = total * (1.0 / D)
    inv = lax.rsqrt(squares * (1.0 / D) - mean * mean + norm_eps)
    inv_ref[...] = inv
    for b in range(cols):
        rows = relative_rows(b, block)
        n = (mid_sc[rows, :] - mean) * inv
        unit_ref[rows, :] = n.astype(bf16)
        n_ref[rows, :] = (n * (1.0 + mod_ref[rows, 2:3]) + mod_ref[rows, 3:4]).astype(bf16)

    def products(s):
        rows = slice(s * sub, (s + 1) * sub)
        return matmul(up_sc[:, rows], n_ref[...], 0, 0), matmul(
            down_sc[:, rows], cot_ref[...], 0, 0
        )

    ahead = products(0)
    for s in range(hidden // sub):
        up, grad_active = ahead
        if s + 1 < hidden // sub:
            ahead = products(s + 1)
        cdf = 0.5 * (1.0 + lax.erf(up * math.sqrt(0.5)))
        density = jnp.exp(-0.5 * up * up) * (1.0 / math.sqrt(2.0 * math.pi))
        act_ref[s * sub : (s + 1) * sub, :] = (up * cdf).astype(bf16)
        du_ref[s * sub : (s + 1) * sub, :] = (grad_active * (cdf + up * density)).astype(bf16)
    for b in range(cols):
        rows = relative_rows(b, block)
        dn_ref[rows, :] = matmul(up_sc[rows, :], du_ref[...]).astype(bf16)
        y = matmul(down_sc[rows, :], act_ref[...])
        half = relative_rows(b // 2, block)
        if b % 2 == 0:
            keep_ref[half, :] = mid_sc[rows, :] + y
        else:
            send_ref[half, :] = y.astype(bf16)


def feed_forward(meta, pieces, own, recv, cot_pieces, up_all, downs, mod, tb=512):
    cols = len(pieces)
    ff_local = downs[0].shape[1]
    hidden = ff_local * len(downs)
    block = pieces[0].shape[0]
    part = own.shape[1]
    tb = min(tb, part)
    strip = lambda r: pl.BlockSpec((r, tb), lambda t, meta: (0, t))
    whole = lambda s: pl.BlockSpec(s, lambda t, meta: (0, 0), pipeline_mode=pl.Buffered(1))

    def weight_rows(b):
        return pl.BlockSpec(
            (block, hidden), lambda t, meta: (meta[b], 0), pipeline_mode=pl.Buffered(1)
        )

    shape = lambda r, kind: jax.ShapeDtypeStruct((r, part), kind)
    return pl.pallas_call(
        partial(feed_forward_kernel, cols=cols, ff_local=ff_local, tb=tb, sub=128),
        out_shape=[
            shape(hidden, bf16), shape(hidden, bf16), shape(D, bf16), shape(D, bf16),
            shape(D, bf16), shape(1, f32), shape(D // 2, f32), shape(D // 2, bf16),
            shape(D, bf16),
        ],
        grid_spec=pltpu.PrefetchScalarGridSpec(
            num_scalar_prefetch=1,
            grid=(part // tb,),
            in_specs=[pl.BlockSpec((block, tb), lambda t, meta: (0, meta[cols] // tb + t))] * cols
            + [strip(D), strip(D)]
            + [strip(block)] * cols
            + [weight_rows(b) for b in range(cols)]
            + [whole(down.shape) for down in downs]
            + [whole(mod.shape)],
            out_specs=[
                strip(hidden), strip(hidden), strip(D), strip(D), strip(D), strip(1),
                strip(D // 2), strip(D // 2), strip(D),
            ],
            scratch_shapes=[
                pltpu.VMEM((D, hidden), bf16),
                pltpu.VMEM((D, hidden), bf16),
                pltpu.VMEM((D, tb), f32),
            ],
        ),
        compiler_params=pltpu.CompilerParams(vmem_limit_bytes=VMEM_LIMIT),
        cost_estimate=pl.CostEstimate(
            flops=8 * D * hidden * part,
            bytes_accessed=4 * D * hidden + 24 * D * part,
            transcendentals=2 * hidden * part,
        ),
        name="feed_forward",
    )(meta, *pieces, own, recv, *cot_pieces, *([up_all] * cols), *downs, mod)


def weight_grad_kernel(meta_ref, *refs, pairs, cols, starts):
    lefts = refs[:pairs]
    rights = refs[pairs : 2 * pairs]
    g_ref, g_sc = refs[-2:]
    block = D // cols
    j = pl.program_id(0)
    for p in range(pairs):

        @pl.when(jnp.logical_and(j >= starts[p], j < starts[p + 1]))
        def _():
            g_sc[...] = matmul(lefts[p][...], rights[p][...], 1, 1).astype(bf16)

    for b in range(cols):
        start = pl.multiple_of(meta_ref[b] * block, block)
        g_ref[pl.ds(start, block), :] = g_sc[relative_rows(b, block), :]


def weight_grads(cols, meta, pairs, places, width, into=None, step=512):
    sizes = [right.shape[0] for _, right in pairs]
    counts = [size // step for size in sizes]
    starts = [sum(counts[:p]) for p in range(len(pairs) + 1)]
    part = pairs[0][0].shape[1]

    def right_map(p):
        return lambda j, meta: (jnp.clip(j - starts[p], 0, counts[p] - 1), 0)

    def out_map(j, meta):
        column = places[0] // step + j
        for p in range(1, len(pairs)):
            column = jnp.where(j >= starts[p], places[p] // step + j - starts[p], column)
        return (0, column)

    lefts = [left for left, _ in pairs]
    rights = [right for _, right in pairs]
    whole = lambda s: pl.BlockSpec(s, lambda j, meta: (0, 0), pipeline_mode=pl.Buffered(1))
    more = [] if into is None else [into]
    return pl.pallas_call(
        partial(weight_grad_kernel, pairs=len(pairs), cols=cols, starts=starts),
        out_shape=jax.ShapeDtypeStruct((D, width), bf16),
        grid_spec=pltpu.PrefetchScalarGridSpec(
            num_scalar_prefetch=1,
            grid=(starts[-1],),
            in_specs=[whole((D, part))] * len(pairs)
            + [pl.BlockSpec((step, part), right_map(p)) for p in range(len(pairs))]
            + [pl.BlockSpec(memory_space=pl.ANY)] * len(more),
            out_specs=pl.BlockSpec((D, step), out_map),
            scratch_shapes=[pltpu.VMEM((D, step), bf16)],
        ),
        input_output_aliases={} if into is None else {1 + 2 * len(pairs): 0},
        compiler_params=pltpu.CompilerParams(vmem_limit_bytes=VMEM_LIMIT),
        cost_estimate=pl.CostEstimate(
            flops=2 * D * part * sum(sizes),
            bytes_accessed=2 * (D * part * len(pairs) + (D + part) * sum(sizes)),
            transcendentals=0,
        ),
        name="weight_grads",
    )(meta, *lefts, *rights, *more)


def mid_back_kernel(meta_ref, *refs, cols):
    dn_ref, recv_ref, unit_ref, inv_ref, cot_ref, mod_ref = refs[:6]
    w_refs = refs[6 : 6 + cols]
    kept_ref, branch_ref = refs[6 + cols : 8 + cols]
    att_refs = refs[8 + cols : 8 + cols + cols // 2]
    sums_ref, r_sc, w_sc, sum_sc = refs[8 + cols + cols // 2 :]
    block = w_refs[0].shape[0]
    tb = dn_ref.shape[1]
    t = pl.program_id(0)

    @pl.when(t == 0)
    def _():
        sum_sc[...] = jnp.zeros_like(sum_sc)
        for b in range(cols):
            w_sc[:, relative_rows(b, block)] = w_refs[b][...].T

    inv = inv_ref[...]
    total = jnp.zeros((1, tb), f32)
    cross = jnp.zeros((1, tb), f32)
    for b in range(cols):
        rows = relative_rows(b, block)
        r = dn_ref[rows, :].astype(f32) + recv_ref[relative_rows(b ^ 1, block), :].astype(f32)
        n = unit_ref[rows, :].astype(f32)
        sum_sc[rows, 0:1] += jnp.sum(r * n, axis=1, keepdims=True)
        sum_sc[rows, 1:2] += jnp.sum(r, axis=1, keepdims=True)
        m = r * (1.0 + mod_ref[rows, 2:3])
        total = total + jnp.sum(m, axis=0, keepdims=True)
        cross = cross + jnp.sum(m * n, axis=0, keepdims=True)
        r_sc[rows, :] = m
    total = total * (1.0 / D)
    cross = cross * (1.0 / D)
    for b in range(cols):
        rows = relative_rows(b, block)
        n = unit_ref[rows, :].astype(f32)
        grad = cot_ref[rows, :].astype(f32) + inv * (r_sc[rows, :] - total - n * cross)
        if b % 2 == 0:
            kept_ref[relative_rows(b // 2, block), :] = grad
        branch_ref[rows, :] = grad.astype(bf16)
    att = matmul(w_sc[...], branch_ref[...]).astype(bf16)
    for i in range(cols // 2):
        att_refs[i][...] = att[i * block : (i + 1) * block]

    @pl.when(t == pl.num_programs(0) - 1)
    def _():
        sums_ref[...] = sum_sc[...]


def mid_back(cols, meta, own, recv, unit, inv, cot, mod, up_all, hidden, tb=512):
    block = D // cols
    part = own.shape[1]
    tb = min(tb, part)
    width = up_all.shape[1] - hidden
    strip = lambda r: pl.BlockSpec((r, tb), lambda t, meta: (0, t))
    whole = lambda s: pl.BlockSpec(s, lambda t, meta: (0, 0), pipeline_mode=pl.Buffered(1))

    def weight_rows(b):
        return pl.BlockSpec(
            (block, width),
            lambda t, meta: (meta[b], hidden // width),
            pipeline_mode=pl.Buffered(1),
        )

    shape = lambda r, kind: jax.ShapeDtypeStruct((r, part), kind)
    return pl.pallas_call(
        partial(mid_back_kernel, cols=cols),
        out_shape=[
            shape(D // 2, f32), shape(D, bf16), *[shape(block, bf16)] * (cols // 2),
            jax.ShapeDtypeStruct((D, 2), f32),
        ],
        grid_spec=pltpu.PrefetchScalarGridSpec(
            num_scalar_prefetch=1,
            grid=(part // tb,),
            in_specs=[strip(D), strip(D), strip(D), strip(1), strip(D), whole(mod.shape)]
            + [weight_rows(b) for b in range(cols)],
            out_specs=[strip(D // 2), strip(D), *[strip(block)] * (cols // 2), whole((D, 2))],
            scratch_shapes=[
                pltpu.VMEM((D, tb), f32),
                pltpu.VMEM((width, D), bf16),
                pltpu.VMEM((D, 2), f32),
            ],
        ),
        compiler_params=pltpu.CompilerParams(vmem_limit_bytes=VMEM_LIMIT),
        cost_estimate=pl.CostEstimate(
            flops=2 * D * width * part, bytes_accessed=18 * D * part, transcendentals=0
        ),
        name="mid_back",
    )(meta, own, recv, unit, inv, cot, mod, *([up_all] * cols))


def project_back_kernel(meta_ref, *refs, cols, rows, tt):
    x_refs = refs[:cols]
    (
        mean_ref, inv_ref, dq_ref, dk_ref, dv_ref, w_ref, mod_ref, kept_ref,
        keep_ref, send_ref, g_ref, sums_ref, w_sc, d_sc, n_sc, r_sc, g_sc,
    ) = refs[cols:]
    block = x_refs[0].shape[0]
    shard = D // rows
    t = pl.program_id(0)

    @pl.when(t == 0)
    def _():
        g_sc[...] = jnp.zeros_like(g_sc)
        n_sc[D:, :] = jnp.ones((EXTRA, tt), bf16)
        column = jnp.zeros((1, w_sc.shape[1]), f32)
        for r in range(rows):
            start = pl.multiple_of(meta_ref[cols + 2 + r] * shard, shard)
            own = relative_rows(r, shard)
            weights = w_ref[pl.ds(start, shard), :]
            w_sc[own, :] = weights
            column = column + jnp.sum(
                weights.astype(f32) * (1.0 + mod_ref[own, 0:1]), axis=0, keepdims=True
            )
        number = lax.broadcasted_iota(jnp.int32, (EXTRA, w_sc.shape[1]), 0)
        terms = jnp.zeros((EXTRA, w_sc.shape[1]), f32)
        for i in range(3):
            term = column.astype(bf16).astype(f32)
            terms = jnp.where(number == i, term, terms)
            column = column - term
        w_sc[D:, :] = terms.astype(bf16)

    for j, ref in enumerate((dq_ref, dk_ref, dv_ref)):
        d_sc[j * block : (j + 1) * block, :] = ref[...]
    r_sc[...] = matmul(w_sc[...], d_sc[...])
    token = t * tt
    mine = jnp.where(
        jnp.logical_and(token >= meta_ref[cols], token < meta_ref[cols] + meta_ref[cols + 1]),
        1.0,
        0.0,
    )
    mean = mean_ref[...]
    inv = inv_ref[...]
    cross = jnp.zeros((1, tt), f32)
    for b in range(cols):
        own = relative_rows(b, block)
        n = (x_refs[b][...].astype(f32) - mean) * inv
        n_sc[own, :] = n.astype(bf16)
        m = r_sc[own, :] * (1.0 + mod_ref[own, 0:1])
        r_sc[own, :] = m
        cross = cross + jnp.sum(m * n, axis=0, keepdims=True)
    g_sc[...] += matmul(n_sc[...], d_sc[...], 1, 1)
    total = r_sc[D : D + 1, :] + r_sc[D + 1 : D + 2, :] + r_sc[D + 2 : D + 3, :]
    slope = inv * inv * cross * (1.0 / D)
    level = inv * total * (1.0 / D) - mean * slope
    for b in range(cols):
        own = relative_rows(b, block)
        grad = r_sc[own, :] * inv - x_refs[b][...].astype(f32) * slope - level
        half = relative_rows(b // 2, block)
        if b % 2 == 0:
            keep_ref[half, :] = grad + mine * kept_ref[half, :]
        else:
            send_ref[half, :] = grad.astype(bf16)

    @pl.when(t == pl.num_programs(0) - 1)
    def _():
        sums = g_sc[D : D + 1, :]
        for r in range(rows):
            start = pl.multiple_of(meta_ref[cols + 2 + r] * shard, shard)
            own = relative_rows(r, shard)
            weights = w_sc[own, :].astype(f32)
            products = g_sc[own, :]
            sums_ref[own, 0:1] = jnp.sum(weights * products, axis=1, keepdims=True)
            sums_ref[own, 1:2] = jnp.sum(weights * sums, axis=1, keepdims=True)
            gains = products * (1.0 + mod_ref[own, 0:1]) + mod_ref[own, 1:2] * sums
            g_ref[pl.ds(start, shard), :] = gains.astype(bf16)


def project_back(rows, meta, pieces, mean, inv, grads, w_qkv, mod, kept, tt=512):
    cols = len(pieces)
    block, tokens = pieces[0].shape
    part = kept.shape[1]
    tt = min(tt, part)
    width = w_qkv.shape[1]
    middle = tokens // tt // 2
    strip = lambda r: pl.BlockSpec((r, tt), lambda t, meta: (0, t))
    whole = lambda s: pl.BlockSpec(s, lambda t, meta: (0, 0), pipeline_mode=pl.Buffered(1))
    halves = pl.BlockSpec(
        (pl.Squeezed(), D // 2, tt), lambda t, meta: (t // middle, 0, t % middle)
    )

    def kept_strip(t, meta):
        last = part // tt - 1
        return (0, jnp.clip(t - meta[cols] // tt, 0, last))

    return pl.pallas_call(
        partial(project_back_kernel, cols=cols, rows=rows, tt=tt),
        out_shape=[
            jax.ShapeDtypeStruct((2, D // 2, tokens // 2), f32),
            jax.ShapeDtypeStruct((2, D // 2, tokens // 2), bf16),
            jax.ShapeDtypeStruct((D, width), bf16),
            jax.ShapeDtypeStruct((D, 2), f32),
        ],
        grid_spec=pltpu.PrefetchScalarGridSpec(
            num_scalar_prefetch=1,
            grid=(tokens // tt,),
            in_specs=[strip(block)] * cols
            + [strip(1), strip(1)]
            + [strip(block)] * 3
            + [whole(w_qkv.shape), whole(mod.shape), pl.BlockSpec((D // 2, tt), kept_strip)],
            out_specs=[halves, halves, whole((D, width)), whole((D, 2))],
            scratch_shapes=[
                pltpu.VMEM((D + EXTRA, width), bf16),
                pltpu.VMEM((width, tt), bf16),
                pltpu.VMEM((D + EXTRA, tt), bf16),
                pltpu.VMEM((D + EXTRA, tt), f32),
                pltpu.VMEM((D + EXTRA, width), f32),
            ],
        ),
        compiler_params=pltpu.CompilerParams(vmem_limit_bytes=VMEM_LIMIT),
        cost_estimate=pl.CostEstimate(
            flops=4 * D * width * tokens, bytes_accessed=8 * D * tokens, transcendentals=0
        ),
        name="project_back",
    )(meta, *pieces, mean, inv, *grads, w_qkv, mod, kept)


def time_features(time_steps, feature_count):
    half_dim = feature_count // 2
    frequency = jnp.exp(-math.log(10000.0) * jnp.arange(half_dim, dtype=f32) / half_dim)
    angles = time_steps.astype(f32)[:, None] * frequency[None, :]
    return jnp.concatenate([jnp.sin(angles), jnp.cos(angles)], axis=1)


def rotary_tables(places):
    inverse = jnp.exp(-math.log(10000.0) * jnp.arange(HALF, dtype=f32) * 2.0 / HEAD_DIM)
    angles = inverse[:, None] * places.astype(f32)[None, :]
    return jnp.cos(angles), jnp.sin(angles)


def local(
    chips,
    rows,
    hidden_in,
    query_key_value_weight,
    output_weight,
    up_weight,
    down_weight,
    w_time,
    segment_ids,
    positions,
    time_step,
    cotangent,
):
    cols = 2 * chips
    me = lax.axis_index("col")
    chip = me // 2
    core = me % 2
    row = lax.axis_index("row")
    block, tokens = hidden_in.shape
    part = tokens // chips

    def from_core(v):
        return lax.ppermute(v, "col", [(c, c ^ 1) for c in range(cols)])

    def from_chip(v, i):
        return lax.ppermute(v, "col", [(c, c ^ (2 * i)) for c in range(cols)])

    def from_col(v, b):
        return lax.ppermute(v, "col", [(c, c ^ b) for c in range(cols)])

    def from_row(v, a):
        return lax.ppermute(v, "row", [(r, r ^ a) for r in range(rows)])

    def gather_rows(v):
        return [v] + [from_row(v, a) for a in range(1, rows)]

    def gather_chips(v):
        return [v] + [from_chip(v, i) for i in range(1, chips)]

    def exchange_chips(pieces):
        return [pieces[0]] + [from_chip(pieces[i], i) for i in range(1, chips)]

    def token_part(v, i):
        return lax.dynamic_slice_in_dim(v, (chip ^ i) * part, part, axis=1)

    def place_parts(pieces):
        whole = jnp.zeros((pieces[0].shape[0], tokens), pieces[0].dtype)
        for i, piece in enumerate(pieces):
            whole = lax.dynamic_update_slice_in_dim(whole, piece, (chip ^ i) * part, axis=1)
        return whole

    qkv_shard = jnp.transpose(query_key_value_weight, (1, 0, 2)).reshape(
        query_key_value_weight.shape[1], -1
    )
    qkv_width = qkv_shard.shape[1]
    ff_local = up_weight.shape[1]
    hidden = ff_local * chips
    first_shard = jnp.concatenate(
        [qkv_shard, w_time.reshape(-1, block), down_weight.T], axis=1
    )
    first_all = lax.all_gather(first_shard, "row", axis=0, tiled=True)
    w_qkv = first_all[:, :qkv_width]
    w_time_all = first_all[:, qkv_width : qkv_width + block].reshape(TEMB, 4, block)
    down_own = first_all[:, qkv_width + block :]
    order = me ^ jnp.arange(cols, dtype=jnp.int32)
    per_block = rows // cols
    shard_order = (
        order[:, None] * per_block + jnp.arange(per_block, dtype=jnp.int32)[None, :]
    ).reshape(rows)
    meta = jnp.concatenate([order, jnp.stack([chip * part, jnp.int32(part)]), shard_order])
    up_shards = gather_chips(jnp.concatenate([up_weight, output_weight.T], axis=1))
    up_packed = jnp.concatenate(
        [s[:, :ff_local] for s in up_shards] + [s[:, ff_local:] for s in up_shards], axis=1
    )
    up_all = lax.all_gather(up_packed, "row", axis=0, tiled=True)

    pieces = []
    for piece in gather_chips(hidden_in):
        pieces += [piece, from_core(piece)]

    embedded = time_features(time_step, TEMB)[0]
    mod_own = jnp.sum(embedded[:, None, None] * w_time_all.astype(f32), axis=0)
    mod_all = jnp.stack([mod_own] + [from_col(mod_own, b) for b in range(1, cols)], axis=1)
    mod_columns = mod_all.reshape(4, D).T

    seg = segment_ids[0]
    pos = positions[0]
    cosine, sine = rotary_tables(pos)

    after, _ = lax.optimization_barrier((cotangent, pieces[-2]))
    cot_x = exchange_chips([token_part(after, i) for i in range(chips)])

    q, k, v, mean_one, inv_one = project(
        rows, meta, pieces, w_qkv, mod_columns, cosine, sine
    )
    q, *cot_x = lax.optimization_barrier((q, *cot_x))
    downs = gather_chips(down_own)
    cot_pieces = []
    for piece in cot_x:
        cot_pieces += [piece, from_core(piece)]
    att_pieces = [None] * chips
    lse_pieces = [None] * chips
    for i in list(range(1, chips)) + [0]:
        att_pieces[i], lse_pieces[i] = attend(
            (chip ^ i) * part, part, q, k, v, seg, pos, segment_ids
        )
        if i + 1 == chips:
            q, cot_pieces, downs, att_pieces[1:] = lax.optimization_barrier(
                (q, cot_pieces, downs, att_pieces[1:])
            )
    mid_share, att_part = out_project(
        cols, meta, exchange_chips(att_pieces), up_all, hidden
    )

    active, grad_up_b, normed_two, cot, unit_two, inv_two, done_keep, done_send, dn_two = (
        feed_forward(
            meta, pieces, mid_share, from_core(mid_share), cot_pieces, up_all, downs, mod_columns
        )
    )
    dn_recv = from_core(dn_two)

    def rows_total(shares):
        return lax.psum_scatter(shares, "row", scatter_dimension=0, tiled=True)

    width = 2 * hidden + chips * block
    shares_ff = weight_grads(cols, meta, [(cot, active)], [hidden], width)
    done = (done_keep + from_core(done_send).astype(f32)).astype(bf16)
    done = done.reshape(chips, block, part)
    dn_recv, shares_ff, done = lax.optimization_barrier((dn_recv, shares_ff, done))
    grad_mid_kept, grad_branch, *grad_att_parts, sums_two = mid_back(
        cols, meta, dn_two, dn_recv, unit_two, inv_two, cot, mod_columns, up_all, hidden
    )
    grad_attended = exchange_chips(grad_att_parts)
    shares_ff = weight_grads(
        cols, meta, [(normed_two, grad_up_b), (grad_branch, att_part)], [0, 2 * hidden],
        width, shares_ff,
    )
    grad_attended, shares_ff = lax.optimization_barrier((grad_attended, shares_ff))
    grads_ff = rows_total(shares_ff)
    done_pieces = exchange_chips([done[i] for i in range(chips)])

    dq, dk, dv = attend_back(
        chip, q, k, v, att_pieces, grad_attended, lse_pieces, seg, pos, segment_ids, cosine, sine
    )
    dq, dk, dv, done_pieces = lax.optimization_barrier((dq, dk, dv, done_pieces))
    layer_result = place_parts(done_pieces)
    keep, send, shares_qkv, sums_one = project_back(
        rows, meta, pieces, mean_one, inv_one, (dq, dk, dv), w_qkv, mod_columns, grad_mid_kept
    )

    def core_total(keep, recv):
        total = (keep + recv.astype(f32)).reshape(chips, block, -1)
        return total[0], [total[i].astype(bf16) for i in range(1, chips)]

    def chip_total(total, away):
        for i in range(1, chips):
            total = total + from_chip(away[i - 1], i).astype(f32)
        return total.astype(bf16)

    recv = from_core(send)
    total_early, away_early = core_total(keep[0], recv[0])
    keep, away_early = lax.optimization_barrier((keep, away_early))
    total_late, away_late = core_total(keep[1], recv[1])
    shares_qkv, grads_ff, away_late = lax.optimization_barrier((shares_qkv, grads_ff, away_late))
    grad_hidden = jnp.concatenate(
        [chip_total(total_early, away_early), chip_total(total_late, away_late)], axis=1
    )

    once = (core == 0).astype(f32)
    grad_mod = jnp.concatenate([sums_one, sums_two * once], axis=1).T.reshape(4, cols, block)
    mod_total = grad_mod[:, 0]
    for b in range(1, cols):
        mod_total = mod_total + from_col(grad_mod[:, b], b)

    high = mod_total.astype(bf16)
    low = (mod_total - high.astype(f32)).astype(bf16)
    step = time_step[0]
    numbers = jnp.stack([step // 256, step % 256]).astype(bf16)
    extra = jnp.concatenate([high, low], axis=0)
    extra = jnp.concatenate(
        [extra, jnp.broadcast_to(jnp.tile(numbers, 4)[:, None], (8, qkv_width - block))], axis=1
    )
    shares = jnp.concatenate(
        [
            shares_qkv.reshape(rows, -1, qkv_width),
            jnp.broadcast_to(extra[None], (rows, 8, qkv_width)),
        ],
        axis=1,
    )
    row_shares = lax.all_to_all(shares, "row", split_axis=0, concat_axis=0, tiled=True)
    shard = D // rows
    grads_qkv = jnp.sum(row_shares[:, :shard].astype(f32), axis=0)
    extras = row_shares[:, shard:].astype(f32)
    mod_rows = extras[:, :4, :block] + extras[:, 4:, :block]
    steps = extras[:, 0, block] * 256.0 + extras[:, 1, block]

    pieces_ff = [
        jnp.concatenate(
            [
                grads_ff[:, i * ff_local : (i + 1) * ff_local],
                grads_ff[:, hidden + i * ff_local : hidden + (i + 1) * ff_local],
                grads_ff[:, 2 * hidden + i * block : 2 * hidden + (i + 1) * block],
            ],
            axis=1,
        )
        for i in range(chips)
    ]
    summed = pieces_ff[0].astype(f32)
    for piece in exchange_chips(pieces_ff)[1:]:
        summed = summed + piece.astype(f32)
    summed_up = summed[:, :ff_local]
    summed_down = summed[:, ff_local : 2 * ff_local].T
    summed_out = summed[:, 2 * ff_local :].T
    summed_qkv = jnp.transpose(grads_qkv.reshape(-1, 3, block), (1, 0, 2))

    temb_share = w_time.shape[0]
    embed_rows = time_features(steps, TEMB)
    embed_share = lax.dynamic_slice_in_dim(embed_rows, row * temb_share, temb_share, axis=1)
    grad_time = jnp.einsum("st,skc->tkc", embed_share, mod_rows, precision=highest_precision)
    return (layer_result, grad_hidden, summed_qkv, summed_out, summed_up, summed_down, grad_time)


def solution(mesh):
    in_specs = (
        P("col", "row"),
        P(None, "row", "col"),
        P("col", "row"),
        P("row", "col"),
        P("col", "row"),
        P("row", None, "col"),
        P("row", None),
        P("row", None),
        P("row"),
        P("col", "row"),
    )
    out_specs = (
        P("col", "row"),
        P("col", "row"),
        P(None, "row", "col"),
        P("col", "row"),
        P("row", "col"),
        P("col", "row"),
        P("row", None, "col"),
    )
    return jax.shard_map(
        partial(local, mesh.shape["col"] // 2, mesh.shape["row"]),
        mesh=mesh,
        in_specs=in_specs,
        out_specs=out_specs,
        check_vma=False,
    )
```

```python
from functools import partial
import math

import jax
import jax.numpy as jnp
from jax import lax
from jax.experimental import pallas as pl
from jax.experimental.pallas import tpu as pltpu
from jax.sharding import PartitionSpec as P

D = 1024
HEAD_DIM = 64
TEMB = 256
HALF = HEAD_DIM // 2
SCORE_SCALE = HEAD_DIM**-0.5
SCORE_LOG2 = SCORE_SCALE * math.log2(math.e)
SAFE_LOG2 = 60.0
STRIP = 512
TQ_FORWARD = 512
TQ_BACKWARD = 256
TK = 512
SEGMENTS = 16
DEPTH = 128
AWAY = 2.0**100
EXTRA = 16
VMEM_LIMIT = 60 << 20

norm_eps = 1e-05
masked_score = -1e30
highest_precision = lax.Precision.HIGHEST
f32 = jnp.float32
bf16 = jnp.bfloat16


def matmul(a, b, ca=1, cb=0):
    return lax.dot_general(a, b, (((ca,), (cb,)), ((), ())), preferred_element_type=f32)


def head_rows(h):
    return slice(h * HEAD_DIM, (h + 1) * HEAD_DIM)


def attend_kernel(
    lo_ref, n_ref, base_ref, q_ref, k_ref, v_ref, segq_ref, segs_ref, o_ref, lse_ref,
    k_sc, v_sc, q_sc, acc_sc, kmax_sc, *, heads, tq, tk,
):
    i = pl.program_id(0)
    tokens = k_ref.shape[1]
    rest = DEPTH - HEAD_DIM - SEGMENTS

    @pl.when(i == 0)
    def _():
        number = lax.broadcasted_iota(jnp.int32, (SEGMENTS, STRIP), 0)

        def strip(b, most):
            cols = pl.ds(pl.multiple_of(b * STRIP, STRIP), STRIP)
            member = jnp.where(number == segs_ref[:, cols], 1.0, 0.0).astype(bf16)
            for h in range(heads):
                kk = k_ref[head_rows(h), cols]
                k_sc[h, cols, :] = jnp.concatenate(
                    [kk, member, jnp.zeros((rest, STRIP), bf16)], axis=0
                ).T
                kf = kk.astype(f32)
                most = jnp.maximum(most, jnp.sum(kf * kf, axis=0, keepdims=True))
                v_sc[h, :HEAD_DIM, cols] = v_ref[head_rows(h), cols]
                v_sc[h, HEAD_DIM:, cols] = jnp.ones((8, STRIP), bf16)
            return most

        most = lax.fori_loop(0, tokens // STRIP, strip, jnp.zeros((1, STRIP), f32))
        kmax_sc[0] = jnp.max(most)

    number = lax.broadcasted_iota(jnp.int32, (SEGMENTS, tq), 0)
    away = jnp.where(number == segq_ref[...], 0.0, -AWAY).astype(bf16)
    qmost = jnp.zeros((1, tq), f32)
    for h in range(heads):
        qq = q_ref[head_rows(h), :]
        qf = qq.astype(f32)
        qmost = jnp.maximum(qmost, jnp.sum(qf * qf, axis=0, keepdims=True))
        q_sc[h, :HEAD_DIM, :] = qq
        q_sc[h, HEAD_DIM : HEAD_DIM + SEGMENTS, :] = away
        q_sc[h, HEAD_DIM + SEGMENTS :, :] = jnp.zeros((rest, tq), bf16)
    small = jnp.max(qmost) * kmax_sc[0] * (SCORE_LOG2 * SCORE_LOG2) <= SAFE_LOG2 * SAFE_LOG2
    lo = lo_ref[base_ref[0] + i]
    n = n_ref[base_ref[0] + i]
    more = n_ref[tokens // tq + base_ref[0] + i]
    acc_sc[...] = jnp.zeros_like(acc_sc)

    def finish(tops):
        for h in range(heads):
            total = acc_sc[h, HEAD_DIM : HEAD_DIM + 1, :]
            o_ref[head_rows(h), :] = (acc_sc[h, :HEAD_DIM, :] / total).astype(bf16)
            lse_ref[h : h + 1, :] = tops[h] + jnp.log2(total)

    @pl.when(small)
    def _():
        def tile(off, keys):
            off = pl.multiple_of(off, 128)
            scores = lambda h: matmul(k_sc[h, pl.ds(off, keys), :], q_sc[h])
            ahead = scores(0)
            for h in range(heads):
                s = ahead
                if h + 1 < heads:
                    ahead = scores(h + 1)
                p = jnp.exp2(s * SCORE_LOG2).astype(bf16)
                acc_sc[h] += matmul(v_sc[h, :, pl.ds(off, keys)], p)

        def step(j, _):
            tile(lo + j * tk, tk)
            return 0

        lax.fori_loop(0, n, step, 0)

        @pl.when(more > 0)
        def _():
            tile(lo + n * tk, tk // 2)

        finish([jnp.zeros((1, tq), f32)] * heads)

    @pl.when(jnp.logical_not(small))
    def _():
        def step(j, tops):
            off = pl.multiple_of(lo + j * (tk // 2), 128)
            grown = []
            for h in range(heads):
                s = matmul(k_sc[h, pl.ds(off, tk // 2), :], q_sc[h]) * SCORE_LOG2
                top = jnp.maximum(tops[h], jnp.max(s, axis=0, keepdims=True))
                p = jnp.exp2(s - top).astype(bf16)
                acc_sc[h] = acc_sc[h] * jnp.exp2(tops[h] - top) + matmul(
                    v_sc[h, :, pl.ds(off, tk // 2)], p
                )
                grown.append(top)
            return tuple(grown)

        start = tuple(jnp.full((1, tq), masked_score, f32) for _ in range(heads))
        finish(lax.fori_loop(0, 2 * n + more, step, start))


def block_ranges(segments, positions, tq, tk):
    tokens = segments.shape[0]
    blocks = tokens // tq
    firsts = jnp.arange(blocks, dtype=jnp.int32) * tq
    lo = ((firsts - positions[::tq]) // 128) * 128
    last = segments.reshape(blocks, tq)[:, -1]
    end = jnp.sum((segments[None, :] <= last[:, None]).astype(jnp.int32), axis=1)
    halves = (end - lo + tk // 2 - 1) // (tk // 2)
    lo = jnp.minimum(lo, tokens - halves * (tk // 2))
    n = jnp.concatenate([halves // 2, halves % 2])
    return lo.astype(jnp.int32), n.astype(jnp.int32)


def attend(first, part, q, k, v, ranges, seg_rows, tq=TQ_FORWARD, tk=TK):
    rows, tokens = q.shape
    heads = rows // HEAD_DIM
    lo, n = ranges
    block = lambda r: pl.BlockSpec((r, tq), lambda i, lo, n, base: (0, base[0] + i))
    out = lambda r: pl.BlockSpec((r, tq), lambda i, lo, n, base: (0, i))
    whole = lambda s: pl.BlockSpec(
        s, lambda i, lo, n, base: (0, 0), pipeline_mode=pl.Buffered(1)
    )
    pairs = tokens * part * heads // 2
    return pl.pallas_call(
        partial(attend_kernel, heads=heads, tq=tq, tk=tk),
        out_shape=(
            jax.ShapeDtypeStruct((rows, part), bf16),
            jax.ShapeDtypeStruct((heads, part), f32),
        ),
        grid_spec=pltpu.PrefetchScalarGridSpec(
            num_scalar_prefetch=3,
            grid=(part // tq,),
            in_specs=[
                block(rows), whole((rows, tokens)), whole((rows, tokens)),
                block(1), whole((1, tokens)),
            ],
            out_specs=(out(rows), out(heads)),
            scratch_shapes=[
                pltpu.VMEM((heads, tokens, DEPTH), bf16),
                pltpu.VMEM((heads, HEAD_DIM + 8, tokens), bf16),
                pltpu.VMEM((heads, DEPTH, tq), bf16),
                pltpu.VMEM((heads, HEAD_DIM + 8, tq), f32),
                pltpu.SMEM((1,), f32),
            ],
        ),
        compiler_params=pltpu.CompilerParams(vmem_limit_bytes=VMEM_LIMIT),
        cost_estimate=pl.CostEstimate(
            flops=16 * HEAD_DIM * pairs, bytes_accessed=8 * rows * tokens, transcendentals=pairs
        ),
        name="attend",
    )(lo, n, jnp.reshape(first // tq, (1,)).astype(jnp.int32), q, k, v, seg_rows, seg_rows)


def unrotate(g, cosine, sine):
    a = g[:HALF]
    b = g[HALF:]
    return jnp.concatenate([a * cosine + b * sine, b * cosine - a * sine], axis=0).astype(bf16)


def attend_back_kernel(lo_ref, n_ref, start_ref, *refs, chips, heads, tq, tk):
    q_ref, k_ref, v_ref = refs[:3]
    o_refs = refs[3 : 3 + chips]
    do_refs = refs[3 + chips : 3 + 2 * chips]
    lse_refs = refs[3 + 2 * chips : 3 + 3 * chips]
    (
        segq_ref, segs_ref, cosq_ref, sinq_ref, cos_ref, sin_ref, dq_ref, dk_ref, dv_ref,
        k_sc, v_sc, segk_ref, dk_sc, dv_sc, dq_sc, do_ref, lse_ref,
    ) = refs[3 + 3 * chips :]
    i = pl.program_id(0)

    def of_block(parts):
        value = parts[0][...]
        for p in range(1, chips):
            value = jnp.where(i >= start_ref[p], jnp.where(i < start_ref[p] + start_ref[chips], parts[p][...], value), value)
        return value

    tokens = k_ref.shape[1]

    @pl.when(i == 0)
    def _():
        def strip(b, _):
            cols = pl.ds(pl.multiple_of(b * STRIP, STRIP), STRIP)
            segk_ref[cols, :] = jnp.broadcast_to(segs_ref[:, cols], (128, STRIP)).T
            for h in range(heads):
                k_sc[h, cols, :] = k_ref[head_rows(h), cols].T
                v_sc[h, cols, :] = v_ref[head_rows(h), cols].T
            return 0

        lax.fori_loop(0, tokens // STRIP, strip, 0)
        dk_sc[...] = jnp.zeros_like(dk_sc)
        dv_sc[...] = jnp.zeros_like(dv_sc)

    segq = segq_ref[...]
    do_ref[...] = of_block(do_refs)
    lse_ref[...] = of_block(lse_refs)
    both = do_ref[...].astype(f32) * of_block(o_refs).astype(f32)
    deltas = [jnp.sum(both[head_rows(h)], axis=0, keepdims=True) for h in range(heads)]
    lo = lo_ref[i]
    dq_sc[...] = jnp.zeros_like(dq_sc)

    def tile(off, keys):
        off = pl.multiple_of(off, 128)
        cols = pl.ds(off, keys)
        same = segk_ref[cols, :][:, :1] == segq

        def products(h):
            rows = head_rows(h)
            return matmul(k_sc[h, cols, :], q_ref[rows, :]), matmul(v_sc[h, cols, :], do_ref[rows, :])

        ahead = products(0)
        for h in range(heads):
            rows = head_rows(h)
            s, dp = ahead
            if h + 1 < heads:
                ahead = products(h + 1)
            p = jnp.exp2(jnp.where(same, s * SCORE_LOG2 - lse_ref[h : h + 1, :], masked_score))
            ds = (p * (dp - deltas[h])).astype(bf16)
            dv_sc[rows, cols] += matmul(do_ref[rows, :], p.astype(bf16), 1, 1)
            dk_sc[rows, cols] += matmul(q_ref[rows, :], ds, 1, 1)
            dq_sc[rows, :] += matmul(k_ref[rows, cols], ds)

    def step(j, _):
        tile(lo + j * tk, tk)
        return 0

    lax.fori_loop(0, n_ref[i], step, 0)

    @pl.when(n_ref[tokens // tq + i] > 0)
    def _():
        tile(lo + n_ref[i] * tk, tk // 2)

    cosine = cosq_ref[...] * SCORE_SCALE
    sine = sinq_ref[...] * SCORE_SCALE
    for h in range(heads):
        dq_ref[head_rows(h), :] = unrotate(dq_sc[head_rows(h), :], cosine, sine)

    @pl.when(i == pl.num_programs(0) - 1)
    def _():
        def strip(b, _):
            cols = pl.ds(pl.multiple_of(b * STRIP, STRIP), STRIP)
            c = cos_ref[:, cols] * SCORE_SCALE
            s = sin_ref[:, cols] * SCORE_SCALE
            for h in range(heads):
                dk_ref[head_rows(h), cols] = unrotate(dk_sc[head_rows(h), cols], c, s)
            dv_ref[:, cols] = dv_sc[:, cols].astype(bf16)
            return 0

        lax.fori_loop(0, tokens // STRIP, strip, 0)


def attend_back(
    chip, q, k, v, o, do, lse, ranges, seg_rows, cosine, sine, tq=TQ_BACKWARD, tk=TK
):
    rows, tokens = q.shape
    heads = rows // HEAD_DIM
    lo, n = ranges
    chips = len(o)
    per_part = tokens // chips // tq
    starts = jnp.concatenate(
        [
            (chip ^ jnp.arange(chips, dtype=jnp.int32)) * per_part,
            jnp.full((1,), per_part, jnp.int32),
        ]
    )
    block = lambda r: pl.BlockSpec((r, tq), lambda i, lo, n, start: (0, i))
    resident = lambda s: pl.BlockSpec(
        s, lambda i, lo, n, start: (0, 0), pipeline_mode=pl.Buffered(1)
    )
    whole = resident((rows, tokens))

    def part_block(r, p):
        return pl.BlockSpec(
            (r, tq), lambda i, lo, n, start: (0, jnp.clip(i - start[p], 0, per_part - 1))
        )

    part_blocks = lambda r: [part_block(r, p) for p in range(chips)]
    pairs = tokens * tokens * heads // 2
    return pl.pallas_call(
        partial(attend_back_kernel, chips=chips, heads=heads, tq=tq, tk=tk),
        out_shape=[jax.ShapeDtypeStruct((rows, tokens), bf16)] * 3,
        grid_spec=pltpu.PrefetchScalarGridSpec(
            num_scalar_prefetch=3,
            grid=(tokens // tq,),
            in_specs=[
                block(rows), whole, whole,
                *part_blocks(rows), *part_blocks(rows), *part_blocks(heads),
                block(1), resident((1, tokens)), block(HALF), block(HALF),
                resident((HALF, tokens)), resident((HALF, tokens)),
            ],
            out_specs=[block(rows), whole, whole],
            scratch_shapes=[
                pltpu.VMEM((heads, tokens, HEAD_DIM), bf16),
                pltpu.VMEM((heads, tokens, HEAD_DIM), bf16),
                pltpu.VMEM((tokens, 128), jnp.int32),
                pltpu.VMEM((rows, tokens), f32),
                pltpu.VMEM((rows, tokens), f32),
                pltpu.VMEM((rows, tq), f32),
                pltpu.VMEM((rows, tq), bf16),
                pltpu.VMEM((heads, tq), f32),
            ],
        ),
        compiler_params=pltpu.CompilerParams(vmem_limit_bytes=VMEM_LIMIT),
        cost_estimate=pl.CostEstimate(
            flops=40 * HEAD_DIM * pairs, bytes_accessed=16 * rows * tokens, transcendentals=pairs
        ),
        name="attend_back",
    )(
        lo, n, starts, q, k, v, *o, *do, *lse, seg_rows, seg_rows, cosine, sine, cosine, sine
    )


def project_kernel(meta_ref, *refs, cols, rows, tt):
    x_refs = refs[:cols]
    w_ref, mod_ref, cos_ref, sin_ref, q_ref, k_ref, v_ref, mean_ref, inv_ref = refs[cols : cols + 9]
    w_sc, n_sc = refs[cols + 9 :]
    block = x_refs[0].shape[0]
    shard = D // rows

    @pl.when(pl.program_id(0) == 0)
    def _():
        for r in range(rows):
            start = pl.multiple_of(meta_ref[cols + 2 + r] * shard, shard)
            w_sc[:, r * shard : (r + 1) * shard] = w_ref[pl.ds(start, shard), :].T

    total = jnp.zeros((1, tt), f32)
    squares = jnp.zeros((1, tt), f32)
    for b in range(cols):
        x = x_refs[b][...].astype(f32)
        total = total + jnp.sum(x, axis=0, keepdims=True)
        squares = squares + jnp.sum(x * x, axis=0, keepdims=True)
    mean = total * (1.0 / D)
    inv = lax.rsqrt(squares * (1.0 / D) - mean * mean + norm_eps)
    mean_ref[...] = mean
    inv_ref[...] = inv
    for b in range(cols):
        own = slice(b * block, (b + 1) * block)
        n = (x_refs[b][...].astype(f32) - mean) * inv
        n_sc[own, :] = (n * (1.0 + mod_ref[own, 0:1]) + mod_ref[own, 1:2]).astype(bf16)
    out = matmul(w_sc[...], n_sc[...])
    cosine = cos_ref[...]
    sine = sin_ref[...]
    for j, ref in ((0, q_ref), (1, k_ref)):
        for h in range(block // HEAD_DIM):
            first = j * block + h * HEAD_DIM
            a = out[first : first + HALF]
            b = out[first + HALF : first + HEAD_DIM]
            ref[h * HEAD_DIM : h * HEAD_DIM + HALF, :] = (a * cosine - b * sine).astype(bf16)
            ref[h * HEAD_DIM + HALF : (h + 1) * HEAD_DIM, :] = (a * sine + b * cosine).astype(bf16)
    v_ref[...] = out[2 * block :].astype(bf16)


def project(rows, meta, pieces, w_qkv, mod, cosine, sine, tt=1024):
    cols = len(pieces)
    block, tokens = pieces[0].shape
    strip = lambda r: pl.BlockSpec((r, tt), lambda t, order: (0, t))
    whole = lambda s: pl.BlockSpec(s, lambda t, order: (0, 0), pipeline_mode=pl.Buffered(1))
    return pl.pallas_call(
        partial(project_kernel, cols=cols, rows=rows, tt=tt),
        out_shape=[jax.ShapeDtypeStruct((block, tokens), bf16)] * 3
        + [jax.ShapeDtypeStruct((1, tokens), f32)] * 2,
        grid_spec=pltpu.PrefetchScalarGridSpec(
            num_scalar_prefetch=1,
            grid=(tokens // tt,),
            in_specs=[strip(block)] * cols
            + [whole(w_qkv.shape), whole(mod.shape), strip(HALF), strip(HALF)],
            out_specs=[strip(block)] * 3 + [strip(1)] * 2,
            scratch_shapes=[pltpu.VMEM((3 * block, D), bf16), pltpu.VMEM((D, tt), bf16)],
        ),
        compiler_params=pltpu.CompilerParams(vmem_limit_bytes=VMEM_LIMIT),
        cost_estimate=pl.CostEstimate(
            flops=6 * D * block * tokens,
            bytes_accessed=2 * (D + 3 * block) * tokens,
            transcendentals=tokens,
        ),
        name="project",
    )(meta, *pieces, w_qkv, mod, cosine, sine)


def out_project_kernel(meta_ref, *refs, cols):
    chips = cols // 2
    att_refs = refs[:chips]
    w_refs = refs[chips : chips + cols]
    share_ref, att_ref = refs[chips + cols :]
    block = att_refs[0].shape[0]
    for i in range(chips):
        att_ref[i * block : (i + 1) * block, :] = att_refs[i][...]
    for b in range(cols):
        share_ref[b * block : (b + 1) * block, :] = matmul(w_refs[b][...], att_ref[...]).astype(
            bf16
        )


def out_project(cols, meta, att, up_all, hidden, tb=512):
    block, part = att[0].shape
    tb = min(tb, part)
    width = up_all.shape[1] - hidden
    strip = lambda r: pl.BlockSpec((r, tb), lambda t, meta: (0, t))

    def weight_rows(b):
        return pl.BlockSpec(
            (block, width),
            lambda t, meta: (meta[b], hidden // width),
            pipeline_mode=pl.Buffered(1),
        )

    return pl.pallas_call(
        partial(out_project_kernel, cols=cols),
        out_shape=[
            jax.ShapeDtypeStruct((D, part), bf16), jax.ShapeDtypeStruct((width, part), bf16)
        ],
        grid_spec=pltpu.PrefetchScalarGridSpec(
            num_scalar_prefetch=1,
            grid=(part // tb,),
            in_specs=[strip(block)] * len(att) + [weight_rows(b) for b in range(cols)],
            out_specs=[strip(D), strip(width)],
        ),
        compiler_params=pltpu.CompilerParams(vmem_limit_bytes=VMEM_LIMIT),
        cost_estimate=pl.CostEstimate(
            flops=2 * D * width * part, bytes_accessed=2 * (D + 2 * width) * part, transcendentals=0
        ),
        name="out_project",
    )(meta, *att, *([up_all] * cols))


def relative_rows(b, block):
    return slice(b * block, (b + 1) * block)


def feed_forward_kernel(meta_ref, *refs, cols, ff_local, tb, sub):
    chips = cols // 2
    hidden = chips * ff_local
    x_refs = refs[:cols]
    own_ref, recv_ref = refs[cols : cols + 2]
    cot_refs = refs[cols + 2 : 2 * cols + 2]
    up_refs = refs[2 * cols + 2 : 3 * cols + 2]
    down_refs = refs[3 * cols + 2 : 3 * cols + 2 + chips]
    (
        mod_ref, act_ref, du_ref, n_ref, cot_ref, unit_ref,  inv_ref,
        keep_ref, send_ref, dn_ref, up_sc, down_sc, mid_sc,
    ) = refs[3 * cols + 2 + chips :]
    block = x_refs[0].shape[0]

    @pl.when(pl.program_id(0) == 0)
    def _():
        for b in range(cols):
            rows = relative_rows(b, block)
            start = pl.multiple_of(meta_ref[b] * block, block)
            up_sc[rows, :] = up_refs[b][...]
            for i in range(chips):
                for c in range(ff_local // sub):
                    first = i * ff_local + c * sub
                    weights = down_refs[i][pl.ds(start, block), c * sub : (c + 1) * sub]
                    down_sc[rows, first : first + sub] = weights

    total = jnp.zeros((1, tb), f32)
    squares = jnp.zeros((1, tb), f32)
    for b in range(cols):
        rows = relative_rows(b, block)
        mid = (
            x_refs[b][...].astype(f32)
            + own_ref[rows, :].astype(f32)
            + recv_ref[relative_rows(b ^ 1, block), :].astype(f32)
        )
        mid_sc[rows, :] = mid
        total = total + jnp.sum(mid, axis=0, keepdims=True)
        squares = squares + jnp.sum(mid * mid, axis=0, keepdims=True)
        cot_ref[rows, :] = cot_refs[b][...]
    mean = total * (1.0 / D)
    inv = lax.rsqrt(squares * (1.0 / D) - mean * mean + norm_eps)
    inv_ref[...] = inv
    for b in range(cols):
        rows = relative_rows(b, block)
        n = (mid_sc[rows, :] - mean) * inv
        unit_ref[rows, :] = n.astype(bf16)
        n_ref[rows, :] = (n * (1.0 + mod_ref[rows, 2:3]) + mod_ref[rows, 3:4]).astype(bf16)

    def products(s):
        rows = slice(s * sub, (s + 1) * sub)
        return matmul(up_sc[:, rows], n_ref[...], 0, 0), matmul(
            down_sc[:, rows], cot_ref[...], 0, 0
        )

    ahead = products(0)
    for s in range(hidden // sub):
        up, grad_active = ahead
        if s + 1 < hidden // sub:
            ahead = products(s + 1)
        cdf = 0.5 * (1.0 + lax.erf(up * math.sqrt(0.5)))
        density = jnp.exp(-0.5 * up * up) * (1.0 / math.sqrt(2.0 * math.pi))
        act_ref[s * sub : (s + 1) * sub, :] = (up * cdf).astype(bf16)
        du_ref[s * sub : (s + 1) * sub, :] = (grad_active * (cdf + up * density)).astype(bf16)
    for b in range(cols):
        rows = relative_rows(b, block)
        dn_ref[rows, :] = matmul(up_sc[rows, :], du_ref[...]).astype(bf16)
        y = matmul(down_sc[rows, :], act_ref[...])
        half = relative_rows(b // 2, block)
        if b % 2 == 0:
            keep_ref[half, :] = mid_sc[rows, :] + y
        else:
            send_ref[half, :] = y.astype(bf16)


def feed_forward(meta, pieces, own, recv, cot_pieces, up_all, downs, mod, tb=512):
    cols = len(pieces)
    ff_local = downs[0].shape[1]
    hidden = ff_local * len(downs)
    block = pieces[0].shape[0]
    part = own.shape[1]
    tb = min(tb, part)
    strip = lambda r: pl.BlockSpec((r, tb), lambda t, meta: (0, t))
    whole = lambda s: pl.BlockSpec(s, lambda t, meta: (0, 0), pipeline_mode=pl.Buffered(1))

    def weight_rows(b):
        return pl.BlockSpec(
            (block, hidden), lambda t, meta: (meta[b], 0), pipeline_mode=pl.Buffered(1)
        )

    shape = lambda r, kind: jax.ShapeDtypeStruct((r, part), kind)
    return pl.pallas_call(
        partial(feed_forward_kernel, cols=cols, ff_local=ff_local, tb=tb, sub=128),
        out_shape=[
            shape(hidden, bf16), shape(hidden, bf16), shape(D, bf16), shape(D, bf16),
            shape(D, bf16), shape(1, f32), shape(D // 2, f32), shape(D // 2, bf16),
            shape(D, bf16),
        ],
        grid_spec=pltpu.PrefetchScalarGridSpec(
            num_scalar_prefetch=1,
            grid=(part // tb,),
            in_specs=[pl.BlockSpec((block, tb), lambda t, meta: (0, meta[cols] // tb + t))] * cols
            + [strip(D), strip(D)]
            + [strip(block)] * cols
            + [weight_rows(b) for b in range(cols)]
            + [whole(down.shape) for down in downs]
            + [whole(mod.shape)],
            out_specs=[
                strip(hidden), strip(hidden), strip(D), strip(D), strip(D), strip(1),
                strip(D // 2), strip(D // 2), strip(D),
            ],
            scratch_shapes=[
                pltpu.VMEM((D, hidden), bf16),
                pltpu.VMEM((D, hidden), bf16),
                pltpu.VMEM((D, tb), f32),
            ],
        ),
        compiler_params=pltpu.CompilerParams(vmem_limit_bytes=VMEM_LIMIT),
        cost_estimate=pl.CostEstimate(
            flops=8 * D * hidden * part,
            bytes_accessed=4 * D * hidden + 24 * D * part,
            transcendentals=2 * hidden * part,
        ),
        name="feed_forward",
    )(meta, *pieces, own, recv, *cot_pieces, *([up_all] * cols), *downs, mod)


def weight_grad_kernel(meta_ref, *refs, pairs, cols, starts):
    lefts = refs[:pairs]
    rights = refs[pairs : 2 * pairs]
    g_ref, g_sc = refs[-2:]
    block = D // cols
    j = pl.program_id(0)
    for p in range(pairs):

        @pl.when(jnp.logical_and(j >= starts[p], j < starts[p + 1]))
        def _():
            g_sc[...] = matmul(lefts[p][...], rights[p][...], 1, 1).astype(bf16)

    for b in range(cols):
        start = pl.multiple_of(meta_ref[b] * block, block)
        g_ref[pl.ds(start, block), :] = g_sc[relative_rows(b, block), :]


def weight_grads(cols, meta, pairs, places, width, into=None, step=512):
    sizes = [right.shape[0] for _, right in pairs]
    counts = [size // step for size in sizes]
    starts = [sum(counts[:p]) for p in range(len(pairs) + 1)]
    part = pairs[0][0].shape[1]

    def right_map(p):
        return lambda j, meta: (jnp.clip(j - starts[p], 0, counts[p] - 1), 0)

    def out_map(j, meta):
        column = places[0] // step + j
        for p in range(1, len(pairs)):
            column = jnp.where(j >= starts[p], places[p] // step + j - starts[p], column)
        return (0, column)

    lefts = [left for left, _ in pairs]
    rights = [right for _, right in pairs]
    whole = lambda s: pl.BlockSpec(s, lambda j, meta: (0, 0), pipeline_mode=pl.Buffered(1))
    more = [] if into is None else [into]
    return pl.pallas_call(
        partial(weight_grad_kernel, pairs=len(pairs), cols=cols, starts=starts),
        out_shape=jax.ShapeDtypeStruct((D, width), bf16),
        grid_spec=pltpu.PrefetchScalarGridSpec(
            num_scalar_prefetch=1,
            grid=(starts[-1],),
            in_specs=[whole((D, part))] * len(pairs)
            + [pl.BlockSpec((step, part), right_map(p)) for p in range(len(pairs))]
            + [pl.BlockSpec(memory_space=pl.ANY)] * len(more),
            out_specs=pl.BlockSpec((D, step), out_map),
            scratch_shapes=[pltpu.VMEM((D, step), bf16)],
        ),
        input_output_aliases={} if into is None else {1 + 2 * len(pairs): 0},
        compiler_params=pltpu.CompilerParams(vmem_limit_bytes=VMEM_LIMIT),
        cost_estimate=pl.CostEstimate(
            flops=2 * D * part * sum(sizes),
            bytes_accessed=2 * (D * part * len(pairs) + (D + part) * sum(sizes)),
            transcendentals=0,
        ),
        name="weight_grads",
    )(meta, *lefts, *rights, *more)


def mid_back_kernel(meta_ref, *refs, cols):
    dn_ref, recv_ref, unit_ref, inv_ref, cot_ref, mod_ref = refs[:6]
    w_refs = refs[6 : 6 + cols]
    kept_ref, branch_ref = refs[6 + cols : 8 + cols]
    att_refs = refs[8 + cols : 8 + cols + cols // 2]
    sums_ref, r_sc, w_sc, sum_sc = refs[8 + cols + cols // 2 :]
    block = w_refs[0].shape[0]
    tb = dn_ref.shape[1]
    t = pl.program_id(0)

    @pl.when(t == 0)
    def _():
        sum_sc[...] = jnp.zeros_like(sum_sc)
        for b in range(cols):
            w_sc[:, relative_rows(b, block)] = w_refs[b][...].T

    inv = inv_ref[...]
    total = jnp.zeros((1, tb), f32)
    cross = jnp.zeros((1, tb), f32)
    for b in range(cols):
        rows = relative_rows(b, block)
        r = dn_ref[rows, :].astype(f32) + recv_ref[relative_rows(b ^ 1, block), :].astype(f32)
        n = unit_ref[rows, :].astype(f32)
        sum_sc[rows, 0:1] += jnp.sum(r * n, axis=1, keepdims=True)
        sum_sc[rows, 1:2] += jnp.sum(r, axis=1, keepdims=True)
        m = r * (1.0 + mod_ref[rows, 2:3])
        total = total + jnp.sum(m, axis=0, keepdims=True)
        cross = cross + jnp.sum(m * n, axis=0, keepdims=True)
        r_sc[rows, :] = m
    total = total * (1.0 / D)
    cross = cross * (1.0 / D)
    for b in range(cols):
        rows = relative_rows(b, block)
        n = unit_ref[rows, :].astype(f32)
        grad = cot_ref[rows, :].astype(f32) + inv * (r_sc[rows, :] - total - n * cross)
        if b % 2 == 0:
            kept_ref[relative_rows(b // 2, block), :] = grad
        branch_ref[rows, :] = grad.astype(bf16)
    att = matmul(w_sc[...], branch_ref[...]).astype(bf16)
    for i in range(cols // 2):
        att_refs[i][...] = att[i * block : (i + 1) * block]

    @pl.when(t == pl.num_programs(0) - 1)
    def _():
        sums_ref[...] = sum_sc[...]


def mid_back(cols, meta, own, recv, unit, inv, cot, mod, up_all, hidden, tb=512):
    block = D // cols
    part = own.shape[1]
    tb = min(tb, part)
    width = up_all.shape[1] - hidden
    strip = lambda r: pl.BlockSpec((r, tb), lambda t, meta: (0, t))
    whole = lambda s: pl.BlockSpec(s, lambda t, meta: (0, 0), pipeline_mode=pl.Buffered(1))

    def weight_rows(b):
        return pl.BlockSpec(
            (block, width),
            lambda t, meta: (meta[b], hidden // width),
            pipeline_mode=pl.Buffered(1),
        )

    shape = lambda r, kind: jax.ShapeDtypeStruct((r, part), kind)
    return pl.pallas_call(
        partial(mid_back_kernel, cols=cols),
        out_shape=[
            shape(D // 2, f32), shape(D, bf16), *[shape(block, bf16)] * (cols // 2),
            jax.ShapeDtypeStruct((D, 2), f32),
        ],
        grid_spec=pltpu.PrefetchScalarGridSpec(
            num_scalar_prefetch=1,
            grid=(part // tb,),
            in_specs=[strip(D), strip(D), strip(D), strip(1), strip(D), whole(mod.shape)]
            + [weight_rows(b) for b in range(cols)],
            out_specs=[strip(D // 2), strip(D), *[strip(block)] * (cols // 2), whole((D, 2))],
            scratch_shapes=[
                pltpu.VMEM((D, tb), f32),
                pltpu.VMEM((width, D), bf16),
                pltpu.VMEM((D, 2), f32),
            ],
        ),
        compiler_params=pltpu.CompilerParams(vmem_limit_bytes=VMEM_LIMIT),
        cost_estimate=pl.CostEstimate(
            flops=2 * D * width * part, bytes_accessed=18 * D * part, transcendentals=0
        ),
        name="mid_back",
    )(meta, own, recv, unit, inv, cot, mod, *([up_all] * cols))


def project_back_kernel(meta_ref, *refs, cols, rows, tt):
    x_refs = refs[:cols]
    (
        mean_ref, inv_ref, dq_ref, dk_ref, dv_ref, w_ref, mod_ref, kept_ref,
        keep_ref, send_ref, g_ref, sums_ref, w_sc, d_sc, n_sc, r_sc, g_sc,
    ) = refs[cols:]
    block = x_refs[0].shape[0]
    shard = D // rows
    t = pl.program_id(0)

    @pl.when(t == 0)
    def _():
        g_sc[...] = jnp.zeros_like(g_sc)
        n_sc[D:, :] = jnp.ones((EXTRA, tt), bf16)
        column = jnp.zeros((1, w_sc.shape[1]), f32)
        for r in range(rows):
            start = pl.multiple_of(meta_ref[cols + 2 + r] * shard, shard)
            own = relative_rows(r, shard)
            weights = w_ref[pl.ds(start, shard), :]
            w_sc[own, :] = weights
            column = column + jnp.sum(
                weights.astype(f32) * (1.0 + mod_ref[own, 0:1]), axis=0, keepdims=True
            )
        number = lax.broadcasted_iota(jnp.int32, (EXTRA, w_sc.shape[1]), 0)
        terms = jnp.zeros((EXTRA, w_sc.shape[1]), f32)
        for i in range(3):
            term = column.astype(bf16).astype(f32)
            terms = jnp.where(number == i, term, terms)
            column = column - term
        w_sc[D:, :] = terms.astype(bf16)

    for j, ref in enumerate((dq_ref, dk_ref, dv_ref)):
        d_sc[j * block : (j + 1) * block, :] = ref[...]
    r_sc[...] = matmul(w_sc[...], d_sc[...])
    token = t * tt
    mine = jnp.where(
        jnp.logical_and(token >= meta_ref[cols], token < meta_ref[cols] + meta_ref[cols + 1]),
        1.0,
        0.0,
    )
    mean = mean_ref[...]
    inv = inv_ref[...]
    cross = jnp.zeros((1, tt), f32)
    for b in range(cols):
        own = relative_rows(b, block)
        n = (x_refs[b][...].astype(f32) - mean) * inv
        n_sc[own, :] = n.astype(bf16)
        m = r_sc[own, :] * (1.0 + mod_ref[own, 0:1])
        r_sc[own, :] = m
        cross = cross + jnp.sum(m * n, axis=0, keepdims=True)
    g_sc[...] += matmul(n_sc[...], d_sc[...], 1, 1)
    total = r_sc[D : D + 1, :] + r_sc[D + 1 : D + 2, :] + r_sc[D + 2 : D + 3, :]
    slope = inv * inv * cross * (1.0 / D)
    level = inv * total * (1.0 / D) - mean * slope
    for b in range(cols):
        own = relative_rows(b, block)
        grad = r_sc[own, :] * inv - x_refs[b][...].astype(f32) * slope - level
        half = relative_rows(b // 2, block)
        if b % 2 == 0:
            keep_ref[half, :] = grad + mine * kept_ref[half, :]
        else:
            send_ref[half, :] = grad.astype(bf16)

    @pl.when(t == pl.num_programs(0) - 1)
    def _():
        sums = g_sc[D : D + 1, :]
        for r in range(rows):
            start = pl.multiple_of(meta_ref[cols + 2 + r] * shard, shard)
            own = relative_rows(r, shard)
            weights = w_sc[own, :].astype(f32)
            products = g_sc[own, :]
            sums_ref[own, 0:1] = jnp.sum(weights * products, axis=1, keepdims=True)
            sums_ref[own, 1:2] = jnp.sum(weights * sums, axis=1, keepdims=True)
            gains = products * (1.0 + mod_ref[own, 0:1]) + mod_ref[own, 1:2] * sums
            g_ref[pl.ds(start, shard), :] = gains.astype(bf16)


def project_back(rows, meta, pieces, mean, inv, grads, w_qkv, mod, kept, tt=512):
    cols = len(pieces)
    block, tokens = pieces[0].shape
    part = kept.shape[1]
    tt = min(tt, part)
    width = w_qkv.shape[1]
    middle = tokens // tt // 2
    strip = lambda r: pl.BlockSpec((r, tt), lambda t, meta: (0, t))
    whole = lambda s: pl.BlockSpec(s, lambda t, meta: (0, 0), pipeline_mode=pl.Buffered(1))
    halves = pl.BlockSpec(
        (pl.Squeezed(), D // 2, tt), lambda t, meta: (t // middle, 0, t % middle)
    )

    def kept_strip(t, meta):
        last = part // tt - 1
        return (0, jnp.clip(t - meta[cols] // tt, 0, last))

    return pl.pallas_call(
        partial(project_back_kernel, cols=cols, rows=rows, tt=tt),
        out_shape=[
            jax.ShapeDtypeStruct((2, D // 2, tokens // 2), f32),
            jax.ShapeDtypeStruct((2, D // 2, tokens // 2), bf16),
            jax.ShapeDtypeStruct((D, width), bf16),
            jax.ShapeDtypeStruct((D, 2), f32),
        ],
        grid_spec=pltpu.PrefetchScalarGridSpec(
            num_scalar_prefetch=1,
            grid=(tokens // tt,),
            in_specs=[strip(block)] * cols
            + [strip(1), strip(1)]
            + [strip(block)] * 3
            + [whole(w_qkv.shape), whole(mod.shape), pl.BlockSpec((D // 2, tt), kept_strip)],
            out_specs=[halves, halves, whole((D, width)), whole((D, 2))],
            scratch_shapes=[
                pltpu.VMEM((D + EXTRA, width), bf16),
                pltpu.VMEM((width, tt), bf16),
                pltpu.VMEM((D + EXTRA, tt), bf16),
                pltpu.VMEM((D + EXTRA, tt), f32),
                pltpu.VMEM((D + EXTRA, width), f32),
            ],
        ),
        compiler_params=pltpu.CompilerParams(vmem_limit_bytes=VMEM_LIMIT),
        cost_estimate=pl.CostEstimate(
            flops=4 * D * width * tokens, bytes_accessed=8 * D * tokens, transcendentals=0
        ),
        name="project_back",
    )(meta, *pieces, mean, inv, *grads, w_qkv, mod, kept)


def time_features(time_steps, feature_count):
    half_dim = feature_count // 2
    frequency = jnp.exp(-math.log(10000.0) * jnp.arange(half_dim, dtype=f32) / half_dim)
    angles = time_steps.astype(f32)[:, None] * frequency[None, :]
    return jnp.concatenate([jnp.sin(angles), jnp.cos(angles)], axis=1)


def rotary_tables(places):
    inverse = jnp.exp(-math.log(10000.0) * jnp.arange(HALF, dtype=f32) * 2.0 / HEAD_DIM)
    angles = inverse[:, None] * places.astype(f32)[None, :]
    return jnp.cos(angles), jnp.sin(angles)


def local(
    chips,
    rows,
    hidden_in,
    query_key_value_weight,
    output_weight,
    up_weight,
    down_weight,
    w_time,
    segment_ids,
    positions,
    time_step,
    cotangent,
):
    cols = 2 * chips
    me = lax.axis_index("col")
    chip = me // 2
    core = me % 2
    row = lax.axis_index("row")
    block, tokens = hidden_in.shape
    part = tokens // chips

    def from_core(v):
        return lax.ppermute(v, "col", [(c, c ^ 1) for c in range(cols)])

    def from_chip(v, i):
        return lax.ppermute(v, "col", [(c, c ^ (2 * i)) for c in range(cols)])

    def from_col(v, b):
        return lax.ppermute(v, "col", [(c, c ^ b) for c in range(cols)])

    def from_row(v, a):
        return lax.ppermute(v, "row", [(r, r ^ a) for r in range(rows)])

    def gather_rows(v):
        return [v] + [from_row(v, a) for a in range(1, rows)]

    def gather_chips(v):
        return [v] + [from_chip(v, i) for i in range(1, chips)]

    def exchange_chips(pieces):
        return [pieces[0]] + [from_chip(pieces[i], i) for i in range(1, chips)]

    def token_part(v, i):
        return lax.dynamic_slice_in_dim(v, (chip ^ i) * part, part, axis=1)

    def place_parts(pieces):
        whole = jnp.zeros((pieces[0].shape[0], tokens), pieces[0].dtype)
        for i, piece in enumerate(pieces):
            whole = lax.dynamic_update_slice_in_dim(whole, piece, (chip ^ i) * part, axis=1)
        return whole

    qkv_shard = jnp.transpose(query_key_value_weight, (1, 0, 2)).reshape(
        query_key_value_weight.shape[1], -1
    )
    qkv_width = qkv_shard.shape[1]
    ff_local = up_weight.shape[1]
    hidden = ff_local * chips
    first_shard = jnp.concatenate(
        [qkv_shard, w_time.reshape(-1, block), down_weight.T], axis=1
    )
    first_all = lax.all_gather(first_shard, "row", axis=0, tiled=True)
    w_qkv = first_all[:, :qkv_width]
    w_time_all = first_all[:, qkv_width : qkv_width + block].reshape(TEMB, 4, block)
    down_own = first_all[:, qkv_width + block :]
    order = me ^ jnp.arange(cols, dtype=jnp.int32)
    per_block = rows // cols
    shard_order = (
        order[:, None] * per_block + jnp.arange(per_block, dtype=jnp.int32)[None, :]
    ).reshape(rows)
    meta = jnp.concatenate([order, jnp.stack([chip * part, jnp.int32(part)]), shard_order])
    up_shards = gather_chips(jnp.concatenate([up_weight, output_weight.T], axis=1))
    up_packed = jnp.concatenate(
        [s[:, :ff_local] for s in up_shards] + [s[:, ff_local:] for s in up_shards], axis=1
    )
    up_all = lax.all_gather(up_packed, "row", axis=0, tiled=True)

    seg = segment_ids[0]
    pos = positions[0]
    ranges = [block_ranges(seg, pos, tq, TK) for tq in (TQ_FORWARD, TQ_BACKWARD)]
    away = gather_chips(hidden_in)
    away[-1], ranges = lax.optimization_barrier((away[-1], ranges))
    pieces = []
    for piece in away:
        pieces += [piece, from_core(piece)]

    embedded = time_features(time_step, TEMB)[0]
    mod_own = jnp.sum(embedded[:, None, None] * w_time_all.astype(f32), axis=0)
    mod_all = jnp.stack([mod_own] + [from_col(mod_own, b) for b in range(1, cols)], axis=1)
    mod_columns = mod_all.reshape(4, D).T

    cosine, sine = rotary_tables(pos)

    after, _ = lax.optimization_barrier((cotangent, pieces[-2]))
    cot_x = exchange_chips([token_part(after, i) for i in range(chips)])

    q, k, v, mean_one, inv_one = project(
        rows, meta, pieces, w_qkv, mod_columns, cosine, sine
    )
    q, *cot_x = lax.optimization_barrier((q, *cot_x))
    downs = gather_chips(down_own)
    cot_pieces = []
    for piece in cot_x:
        cot_pieces += [piece, from_core(piece)]
    att_pieces = [None] * chips
    lse_pieces = [None] * chips
    for i in list(range(1, chips)) + [0]:
        att_pieces[i], lse_pieces[i] = attend(
            (chip ^ i) * part, part, q, k, v, ranges[0], segment_ids
        )
        if i + 1 == chips:
            q, cot_pieces, downs, att_pieces[1:] = lax.optimization_barrier(
                (q, cot_pieces, downs, att_pieces[1:])
            )
    mid_share, att_part = out_project(
        cols, meta, exchange_chips(att_pieces), up_all, hidden
    )

    active, grad_up_b, normed_two, cot, unit_two, inv_two, done_keep, done_send, dn_two = (
        feed_forward(
            meta, pieces, mid_share, from_core(mid_share), cot_pieces, up_all, downs, mod_columns
        )
    )
    dn_recv = from_core(dn_two)

    def rows_total(shares):
        return lax.psum_scatter(shares, "row", scatter_dimension=0, tiled=True)

    width = 2 * hidden + chips * block
    shares_ff = weight_grads(cols, meta, [(cot, active)], [hidden], width)
    done = (done_keep + from_core(done_send).astype(f32)).astype(bf16)
    done = done.reshape(chips, block, part)
    dn_recv, shares_ff = lax.optimization_barrier((dn_recv, shares_ff))
    grad_mid_kept, grad_branch, *grad_att_parts, sums_two = mid_back(
        cols, meta, dn_two, dn_recv, unit_two, inv_two, cot, mod_columns, up_all, hidden
    )
    grad_attended = exchange_chips(grad_att_parts)
    shares_ff = weight_grads(
        cols, meta, [(normed_two, grad_up_b), (grad_branch, att_part)], [0, 2 * hidden],
        width, shares_ff,
    )
    grad_attended, shares_ff, done = lax.optimization_barrier((grad_attended, shares_ff, done))
    grads_ff = rows_total(shares_ff)
    done_pieces = exchange_chips([done[i] for i in range(chips)])

    dq, dk, dv = attend_back(
        chip, q, k, v, att_pieces, grad_attended, lse_pieces, ranges[1], segment_ids, cosine, sine
    )
    dq, dk, dv, done_pieces = lax.optimization_barrier((dq, dk, dv, done_pieces))
    layer_result = place_parts(done_pieces)
    keep, send, shares_qkv, sums_one = project_back(
        rows, meta, pieces, mean_one, inv_one, (dq, dk, dv), w_qkv, mod_columns, grad_mid_kept
    )

    def core_total(keep, recv):
        total = (keep + recv.astype(f32)).reshape(chips, block, -1)
        return total[0], [total[i].astype(bf16) for i in range(1, chips)]

    def chip_total(total, away):
        for i in range(1, chips):
            total = total + from_chip(away[i - 1], i).astype(f32)
        return total.astype(bf16)

    recv = from_core(send)
    total_early, away_early = core_total(keep[0], recv[0])
    keep, away_early = lax.optimization_barrier((keep, away_early))
    total_late, away_late = core_total(keep[1], recv[1])
    shares_qkv, grads_ff, away_late = lax.optimization_barrier((shares_qkv, grads_ff, away_late))
    grad_hidden = jnp.concatenate(
        [chip_total(total_early, away_early), chip_total(total_late, away_late)], axis=1
    )

    once = (core == 0).astype(f32)
    grad_mod = jnp.concatenate([sums_one, sums_two * once], axis=1).T.reshape(4, cols, block)
    mod_total = grad_mod[:, 0]
    for b in range(1, cols):
        mod_total = mod_total + from_col(grad_mod[:, b], b)

    high = mod_total.astype(bf16)
    low = (mod_total - high.astype(f32)).astype(bf16)
    step = time_step[0]
    numbers = jnp.stack([step // 256, step % 256]).astype(bf16)
    extra = jnp.concatenate([high, low], axis=0)
    extra = jnp.concatenate(
        [extra, jnp.broadcast_to(jnp.tile(numbers, 4)[:, None], (8, qkv_width - block))], axis=1
    )
    shares = jnp.concatenate(
        [
            shares_qkv.reshape(rows, -1, qkv_width),
            jnp.broadcast_to(extra[None], (rows, 8, qkv_width)),
        ],
        axis=1,
    )
    row_shares = lax.all_to_all(shares, "row", split_axis=0, concat_axis=0, tiled=True)
    shard = D // rows
    grads_qkv = jnp.sum(row_shares[:, :shard].astype(f32), axis=0)
    extras = row_shares[:, shard:].astype(f32)
    mod_rows = extras[:, :4, :block] + extras[:, 4:, :block]
    steps = extras[:, 0, block] * 256.0 + extras[:, 1, block]

    pieces_ff = [
        jnp.concatenate(
            [
                grads_ff[:, i * ff_local : (i + 1) * ff_local],
                grads_ff[:, hidden + i * ff_local : hidden + (i + 1) * ff_local],
                grads_ff[:, 2 * hidden + i * block : 2 * hidden + (i + 1) * block],
            ],
            axis=1,
        )
        for i in range(chips)
    ]
    summed = pieces_ff[0].astype(f32)
    for piece in exchange_chips(pieces_ff)[1:]:
        summed = summed + piece.astype(f32)
    summed_up = summed[:, :ff_local]
    summed_down = summed[:, ff_local : 2 * ff_local].T
    summed_out = summed[:, 2 * ff_local :].T
    summed_qkv = jnp.transpose(grads_qkv.reshape(-1, 3, block), (1, 0, 2))

    temb_share = w_time.shape[0]
    embed_rows = time_features(steps, TEMB)
    embed_share = lax.dynamic_slice_in_dim(embed_rows, row * temb_share, temb_share, axis=1)
    grad_time = jnp.einsum("st,skc->tkc", embed_share, mod_rows, precision=highest_precision)
    return (layer_result, grad_hidden, summed_qkv, summed_out, summed_up, summed_down, grad_time)


def solution(mesh):
    in_specs = (
        P("col", "row"),
        P(None, "row", "col"),
        P("col", "row"),
        P("row", "col"),
        P("col", "row"),
        P("row", None, "col"),
        P("row", None),
        P("row", None),
        P("row"),
        P("col", "row"),
    )
    out_specs = (
        P("col", "row"),
        P("col", "row"),
        P(None, "row", "col"),
        P("col", "row"),
        P("row", "col"),
        P("col", "row"),
        P("row", None, "col"),
    )
    return jax.shard_map(
        partial(local, mesh.shape["col"] // 2, mesh.shape["row"]),
        mesh=mesh,
        in_specs=in_specs,
        out_specs=out_specs,
        check_vma=False,
    )
```

```python
from functools import partial
import math

import jax
import jax.numpy as jnp
from jax import lax
from jax.experimental import pallas as pl
from jax.experimental.pallas import tpu as pltpu
from jax.sharding import PartitionSpec as P

D = 1024
HEAD_DIM = 64
TEMB = 256
HALF = HEAD_DIM // 2
SCORE_SCALE = HEAD_DIM**-0.5
SCORE_LOG2 = SCORE_SCALE * math.log2(math.e)
SAFE_LOG2 = 60.0
STRIP = 512
TQ_FORWARD = 512
TQ_BACKWARD = 256
TK_FORWARD = 1024
TK_BACKWARD = 512
SEGMENTS = 16
DEPTH = 128
AWAY = 2.0**100
EXTRA = 16
VMEM_LIMIT = 60 << 20

norm_eps = 1e-05
masked_score = -1e30
highest_precision = lax.Precision.HIGHEST
f32 = jnp.float32
bf16 = jnp.bfloat16


def matmul(a, b, ca=1, cb=0):
    return lax.dot_general(a, b, (((ca,), (cb,)), ((), ())), preferred_element_type=f32)


def head_rows(h):
    return slice(h * HEAD_DIM, (h + 1) * HEAD_DIM)


def attend_kernel(
    lo_ref, n_ref, base_ref, q_ref, k_ref, v_ref, segq_ref, segs_ref, o_ref, lse_ref,
    k_sc, v_sc, q_sc, acc_sc, kmax_sc, *, heads, tq, tk,
):
    i = pl.program_id(0)
    tokens = k_ref.shape[1]
    rest = DEPTH - HEAD_DIM - SEGMENTS

    @pl.when(i == 0)
    def _():
        number = lax.broadcasted_iota(jnp.int32, (SEGMENTS, STRIP), 0)

        def strip(b, most):
            cols = pl.ds(pl.multiple_of(b * STRIP, STRIP), STRIP)
            member = jnp.where(number == segs_ref[:, cols], 1.0, 0.0).astype(bf16)
            for h in range(heads):
                kk = k_ref[head_rows(h), cols]
                k_sc[h, cols, :] = jnp.concatenate(
                    [kk, member, jnp.zeros((rest, STRIP), bf16)], axis=0
                ).T
                kf = kk.astype(f32)
                most = jnp.maximum(most, jnp.sum(kf * kf, axis=0, keepdims=True))
                v_sc[h, :HEAD_DIM, cols] = v_ref[head_rows(h), cols]
                v_sc[h, HEAD_DIM:, cols] = jnp.ones((8, STRIP), bf16)
            return most

        most = lax.fori_loop(0, tokens // STRIP, strip, jnp.zeros((1, STRIP), f32))
        kmax_sc[0] = jnp.max(most)

    number = lax.broadcasted_iota(jnp.int32, (SEGMENTS, tq), 0)
    away = jnp.where(number == segq_ref[...], 0.0, -AWAY).astype(bf16)
    qmost = jnp.zeros((1, tq), f32)
    for h in range(heads):
        qq = q_ref[head_rows(h), :]
        qf = qq.astype(f32)
        qmost = jnp.maximum(qmost, jnp.sum(qf * qf, axis=0, keepdims=True))
        q_sc[h, :HEAD_DIM, :] = qq
        q_sc[h, HEAD_DIM : HEAD_DIM + SEGMENTS, :] = away
        q_sc[h, HEAD_DIM + SEGMENTS :, :] = jnp.zeros((rest, tq), bf16)
    small = jnp.max(qmost) * kmax_sc[0] * (SCORE_LOG2 * SCORE_LOG2) <= SAFE_LOG2 * SAFE_LOG2
    lo = lo_ref[base_ref[0] + i]
    n = n_ref[base_ref[0] + i]
    more = n_ref[tokens // tq + base_ref[0] + i]
    acc_sc[...] = jnp.zeros_like(acc_sc)

    def finish(tops):
        for h in range(heads):
            total = acc_sc[h, HEAD_DIM : HEAD_DIM + 1, :]
            o_ref[head_rows(h), :] = (acc_sc[h, :HEAD_DIM, :] / total).astype(bf16)
            lse_ref[h : h + 1, :] = tops[h] + jnp.log2(total)

    @pl.when(small)
    def _():
        def tile(off, keys):
            off = pl.multiple_of(off, 128)
            scores = lambda h: matmul(k_sc[h, pl.ds(off, keys), :], q_sc[h])
            ahead = scores(0)
            for h in range(heads):
                s = ahead
                if h + 1 < heads:
                    ahead = scores(h + 1)
                p = jnp.exp2(s * SCORE_LOG2).astype(bf16)
                acc_sc[h] += matmul(v_sc[h, :, pl.ds(off, keys)], p)

        def step(j, _):
            tile(lo + j * tk, tk)
            return 0

        lax.fori_loop(0, n, step, 0)

        @pl.when(more > 0)
        def _():
            tile(lo + n * tk, tk // 2)

        finish([jnp.zeros((1, tq), f32)] * heads)

    @pl.when(jnp.logical_not(small))
    def _():
        def step(j, tops):
            off = pl.multiple_of(lo + j * (tk // 2), 128)
            grown = []
            for h in range(heads):
                s = matmul(k_sc[h, pl.ds(off, tk // 2), :], q_sc[h]) * SCORE_LOG2
                top = jnp.maximum(tops[h], jnp.max(s, axis=0, keepdims=True))
                p = jnp.exp2(s - top).astype(bf16)
                acc_sc[h] = acc_sc[h] * jnp.exp2(tops[h] - top) + matmul(
                    v_sc[h, :, pl.ds(off, tk // 2)], p
                )
                grown.append(top)
            return tuple(grown)

        start = tuple(jnp.full((1, tq), masked_score, f32) for _ in range(heads))
        finish(lax.fori_loop(0, 2 * n + more, step, start))


def block_ranges(segments, positions, tq, tk):
    tokens = segments.shape[0]
    blocks = tokens // tq
    firsts = jnp.arange(blocks, dtype=jnp.int32) * tq
    lo = ((firsts - positions[::tq]) // 128) * 128
    last = segments.reshape(blocks, tq)[:, -1]
    end = jnp.sum((segments[None, :] <= last[:, None]).astype(jnp.int32), axis=1)
    halves = (end - lo + tk // 2 - 1) // (tk // 2)
    lo = jnp.minimum(lo, tokens - halves * (tk // 2))
    n = jnp.concatenate([halves // 2, halves % 2])
    return lo.astype(jnp.int32), n.astype(jnp.int32)


def attend(first, part, q, k, v, ranges, seg_rows, tq=TQ_FORWARD, tk=TK_FORWARD):
    rows, tokens = q.shape
    heads = rows // HEAD_DIM
    lo, n = ranges
    block = lambda r: pl.BlockSpec((r, tq), lambda i, lo, n, base: (0, base[0] + i))
    out = lambda r: pl.BlockSpec((r, tq), lambda i, lo, n, base: (0, i))
    whole = lambda s: pl.BlockSpec(
        s, lambda i, lo, n, base: (0, 0), pipeline_mode=pl.Buffered(1)
    )
    pairs = tokens * part * heads // 2
    return pl.pallas_call(
        partial(attend_kernel, heads=heads, tq=tq, tk=tk),
        out_shape=(
            jax.ShapeDtypeStruct((rows, part), bf16),
            jax.ShapeDtypeStruct((heads, part), f32),
        ),
        grid_spec=pltpu.PrefetchScalarGridSpec(
            num_scalar_prefetch=3,
            grid=(part // tq,),
            in_specs=[
                block(rows), whole((rows, tokens)), whole((rows, tokens)),
                block(1), whole((1, tokens)),
            ],
            out_specs=(out(rows), out(heads)),
            scratch_shapes=[
                pltpu.VMEM((heads, tokens, DEPTH), bf16),
                pltpu.VMEM((heads, HEAD_DIM + 8, tokens), bf16),
                pltpu.VMEM((heads, DEPTH, tq), bf16),
                pltpu.VMEM((heads, HEAD_DIM + 8, tq), f32),
                pltpu.SMEM((1,), f32),
            ],
        ),
        compiler_params=pltpu.CompilerParams(vmem_limit_bytes=VMEM_LIMIT),
        cost_estimate=pl.CostEstimate(
            flops=16 * HEAD_DIM * pairs, bytes_accessed=8 * rows * tokens, transcendentals=pairs
        ),
        name="attend",
    )(lo, n, jnp.reshape(first // tq, (1,)).astype(jnp.int32), q, k, v, seg_rows, seg_rows)


def unrotate(g, cosine, sine):
    a = g[:HALF]
    b = g[HALF:]
    return jnp.concatenate([a * cosine + b * sine, b * cosine - a * sine], axis=0).astype(bf16)


def attend_back_kernel(lo_ref, n_ref, start_ref, *refs, chips, heads, tq, tk):
    q_ref, k_ref, v_ref = refs[:3]
    o_refs = refs[3 : 3 + chips]
    do_refs = refs[3 + chips : 3 + 2 * chips]
    lse_refs = refs[3 + 2 * chips : 3 + 3 * chips]
    (
        segq_ref, segs_ref, cosq_ref, sinq_ref, cos_ref, sin_ref, dq_ref, dk_ref, dv_ref,
        k_sc, v_sc, segk_ref, dk_sc, dv_sc, dq_sc, do_ref, lse_ref,
    ) = refs[3 + 3 * chips :]
    i = pl.program_id(0)

    def of_block(parts):
        value = parts[0][...]
        for p in range(1, chips):
            value = jnp.where(i >= start_ref[p], jnp.where(i < start_ref[p] + start_ref[chips], parts[p][...], value), value)
        return value

    tokens = k_ref.shape[1]

    @pl.when(i == 0)
    def _():
        def strip(b, _):
            cols = pl.ds(pl.multiple_of(b * STRIP, STRIP), STRIP)
            segk_ref[cols, :] = jnp.broadcast_to(segs_ref[:, cols], (128, STRIP)).T
            for h in range(heads):
                k_sc[h, cols, :] = k_ref[head_rows(h), cols].T
                v_sc[h, cols, :] = v_ref[head_rows(h), cols].T
            return 0

        lax.fori_loop(0, tokens // STRIP, strip, 0)
        dk_sc[...] = jnp.zeros_like(dk_sc)
        dv_sc[...] = jnp.zeros_like(dv_sc)

    segq = segq_ref[...]
    do_ref[...] = of_block(do_refs)
    lse_ref[...] = of_block(lse_refs)
    both = do_ref[...].astype(f32) * of_block(o_refs).astype(f32)
    deltas = [jnp.sum(both[head_rows(h)], axis=0, keepdims=True) for h in range(heads)]
    lo = lo_ref[i]
    dq_sc[...] = jnp.zeros_like(dq_sc)

    def tile(off, keys):
        off = pl.multiple_of(off, 128)
        cols = pl.ds(off, keys)
        same = segk_ref[cols, :][:, :1] == segq

        def products(h):
            rows = head_rows(h)
            return matmul(k_sc[h, cols, :], q_ref[rows, :]), matmul(v_sc[h, cols, :], do_ref[rows, :])

        ahead = products(0)
        for h in range(heads):
            rows = head_rows(h)
            s, dp = ahead
            if h + 1 < heads:
                ahead = products(h + 1)
            p = jnp.exp2(jnp.where(same, s * SCORE_LOG2 - lse_ref[h : h + 1, :], masked_score))
            ds = (p * (dp - deltas[h])).astype(bf16)
            dv_sc[rows, cols] += matmul(do_ref[rows, :], p.astype(bf16), 1, 1)
            dk_sc[rows, cols] += matmul(q_ref[rows, :], ds, 1, 1)
            dq_sc[rows, :] += matmul(k_ref[rows, cols], ds)

    def step(j, _):
        tile(lo + j * tk, tk)
        return 0

    lax.fori_loop(0, n_ref[i], step, 0)

    @pl.when(n_ref[tokens // tq + i] > 0)
    def _():
        tile(lo + n_ref[i] * tk, tk // 2)

    cosine = cosq_ref[...] * SCORE_SCALE
    sine = sinq_ref[...] * SCORE_SCALE
    for h in range(heads):
        dq_ref[head_rows(h), :] = unrotate(dq_sc[head_rows(h), :], cosine, sine)

    @pl.when(i == pl.num_programs(0) - 1)
    def _():
        def strip(b, _):
            cols = pl.ds(pl.multiple_of(b * STRIP, STRIP), STRIP)
            c = cos_ref[:, cols] * SCORE_SCALE
            s = sin_ref[:, cols] * SCORE_SCALE
            for h in range(heads):
                dk_ref[head_rows(h), cols] = unrotate(dk_sc[head_rows(h), cols], c, s)
            dv_ref[:, cols] = dv_sc[:, cols].astype(bf16)
            return 0

        lax.fori_loop(0, tokens // STRIP, strip, 0)


def attend_back(
    chip, q, k, v, o, do, lse, ranges, seg_rows, cosine, sine, tq=TQ_BACKWARD, tk=TK_BACKWARD
):
    rows, tokens = q.shape
    heads = rows // HEAD_DIM
    lo, n = ranges
    chips = len(o)
    per_part = tokens // chips // tq
    starts = jnp.concatenate(
        [
            (chip ^ jnp.arange(chips, dtype=jnp.int32)) * per_part,
            jnp.full((1,), per_part, jnp.int32),
        ]
    )
    block = lambda r: pl.BlockSpec((r, tq), lambda i, lo, n, start: (0, i))
    resident = lambda s: pl.BlockSpec(
        s, lambda i, lo, n, start: (0, 0), pipeline_mode=pl.Buffered(1)
    )
    whole = resident((rows, tokens))

    def part_block(r, p):
        return pl.BlockSpec(
            (r, tq), lambda i, lo, n, start: (0, jnp.clip(i - start[p], 0, per_part - 1))
        )

    part_blocks = lambda r: [part_block(r, p) for p in range(chips)]
    pairs = tokens * tokens * heads // 2
    return pl.pallas_call(
        partial(attend_back_kernel, chips=chips, heads=heads, tq=tq, tk=tk),
        out_shape=[jax.ShapeDtypeStruct((rows, tokens), bf16)] * 3,
        grid_spec=pltpu.PrefetchScalarGridSpec(
            num_scalar_prefetch=3,
            grid=(tokens // tq,),
            in_specs=[
                block(rows), whole, whole,
                *part_blocks(rows), *part_blocks(rows), *part_blocks(heads),
                block(1), resident((1, tokens)), block(HALF), block(HALF),
                resident((HALF, tokens)), resident((HALF, tokens)),
            ],
            out_specs=[block(rows), whole, whole],
            scratch_shapes=[
                pltpu.VMEM((heads, tokens, HEAD_DIM), bf16),
                pltpu.VMEM((heads, tokens, HEAD_DIM), bf16),
                pltpu.VMEM((tokens, 128), jnp.int32),
                pltpu.VMEM((rows, tokens), f32),
                pltpu.VMEM((rows, tokens), f32),
                pltpu.VMEM((rows, tq), f32),
                pltpu.VMEM((rows, tq), bf16),
                pltpu.VMEM((heads, tq), f32),
            ],
        ),
        compiler_params=pltpu.CompilerParams(vmem_limit_bytes=VMEM_LIMIT),
        cost_estimate=pl.CostEstimate(
            flops=40 * HEAD_DIM * pairs, bytes_accessed=16 * rows * tokens, transcendentals=pairs
        ),
        name="attend_back",
    )(
        lo, n, starts, q, k, v, *o, *do, *lse, seg_rows, seg_rows, cosine, sine, cosine, sine
    )


def project_kernel(meta_ref, *refs, cols, rows, tt):
    x_refs = refs[:cols]
    w_ref, mod_ref, cos_ref, sin_ref, q_ref, k_ref, v_ref, mean_ref, inv_ref = refs[cols : cols + 9]
    w_sc, n_sc = refs[cols + 9 :]
    block = x_refs[0].shape[0]
    shard = D // rows

    @pl.when(pl.program_id(0) == 0)
    def _():
        for r in range(rows):
            start = pl.multiple_of(meta_ref[cols + 2 + r] * shard, shard)
            w_sc[:, r * shard : (r + 1) * shard] = w_ref[pl.ds(start, shard), :].T

    total = jnp.zeros((1, tt), f32)
    squares = jnp.zeros((1, tt), f32)
    for b in range(cols):
        x = x_refs[b][...].astype(f32)
        total = total + jnp.sum(x, axis=0, keepdims=True)
        squares = squares + jnp.sum(x * x, axis=0, keepdims=True)
    mean = total * (1.0 / D)
    inv = lax.rsqrt(squares * (1.0 / D) - mean * mean + norm_eps)
    mean_ref[...] = mean
    inv_ref[...] = inv
    for b in range(cols):
        own = slice(b * block, (b + 1) * block)
        n = (x_refs[b][...].astype(f32) - mean) * inv
        n_sc[own, :] = (n * (1.0 + mod_ref[own, 0:1]) + mod_ref[own, 1:2]).astype(bf16)
    out = matmul(w_sc[...], n_sc[...])
    cosine = cos_ref[...]
    sine = sin_ref[...]
    for j, ref in ((0, q_ref), (1, k_ref)):
        for h in range(block // HEAD_DIM):
            first = j * block + h * HEAD_DIM
            a = out[first : first + HALF]
            b = out[first + HALF : first + HEAD_DIM]
            ref[h * HEAD_DIM : h * HEAD_DIM + HALF, :] = (a * cosine - b * sine).astype(bf16)
            ref[h * HEAD_DIM + HALF : (h + 1) * HEAD_DIM, :] = (a * sine + b * cosine).astype(bf16)
    v_ref[...] = out[2 * block :].astype(bf16)


def project(rows, meta, pieces, w_qkv, mod, cosine, sine, tt=1024):
    cols = len(pieces)
    block, tokens = pieces[0].shape
    strip = lambda r: pl.BlockSpec((r, tt), lambda t, order: (0, t))
    whole = lambda s: pl.BlockSpec(s, lambda t, order: (0, 0), pipeline_mode=pl.Buffered(1))
    return pl.pallas_call(
        partial(project_kernel, cols=cols, rows=rows, tt=tt),
        out_shape=[jax.ShapeDtypeStruct((block, tokens), bf16)] * 3
        + [jax.ShapeDtypeStruct((1, tokens), f32)] * 2,
        grid_spec=pltpu.PrefetchScalarGridSpec(
            num_scalar_prefetch=1,
            grid=(tokens // tt,),
            in_specs=[strip(block)] * cols
            + [whole(w_qkv.shape), whole(mod.shape), strip(HALF), strip(HALF)],
            out_specs=[strip(block)] * 3 + [strip(1)] * 2,
            scratch_shapes=[pltpu.VMEM((3 * block, D), bf16), pltpu.VMEM((D, tt), bf16)],
        ),
        compiler_params=pltpu.CompilerParams(vmem_limit_bytes=VMEM_LIMIT),
        cost_estimate=pl.CostEstimate(
            flops=6 * D * block * tokens,
            bytes_accessed=2 * (D + 3 * block) * tokens,
            transcendentals=tokens,
        ),
        name="project",
    )(meta, *pieces, w_qkv, mod, cosine, sine)


def out_project_kernel(meta_ref, *refs, cols):
    chips = cols // 2
    att_refs = refs[:chips]
    w_refs = refs[chips : chips + cols]
    share_ref, att_ref = refs[chips + cols :]
    block = att_refs[0].shape[0]
    for i in range(chips):
        att_ref[i * block : (i + 1) * block, :] = att_refs[i][...]
    for b in range(cols):
        share_ref[b * block : (b + 1) * block, :] = matmul(w_refs[b][...], att_ref[...]).astype(
            bf16
        )


def out_project(cols, meta, att, up_all, hidden, tb=512):
    block, part = att[0].shape
    tb = min(tb, part)
    width = up_all.shape[1] - hidden
    strip = lambda r: pl.BlockSpec((r, tb), lambda t, meta: (0, t))

    def weight_rows(b):
        return pl.BlockSpec(
            (block, width),
            lambda t, meta: (meta[b], hidden // width),
            pipeline_mode=pl.Buffered(1),
        )

    return pl.pallas_call(
        partial(out_project_kernel, cols=cols),
        out_shape=[
            jax.ShapeDtypeStruct((D, part), bf16), jax.ShapeDtypeStruct((width, part), bf16)
        ],
        grid_spec=pltpu.PrefetchScalarGridSpec(
            num_scalar_prefetch=1,
            grid=(part // tb,),
            in_specs=[strip(block)] * len(att) + [weight_rows(b) for b in range(cols)],
            out_specs=[strip(D), strip(width)],
        ),
        compiler_params=pltpu.CompilerParams(vmem_limit_bytes=VMEM_LIMIT),
        cost_estimate=pl.CostEstimate(
            flops=2 * D * width * part, bytes_accessed=2 * (D + 2 * width) * part, transcendentals=0
        ),
        name="out_project",
    )(meta, *att, *([up_all] * cols))


def relative_rows(b, block):
    return slice(b * block, (b + 1) * block)


def feed_forward_kernel(meta_ref, *refs, cols, ff_local, tb, sub):
    chips = cols // 2
    hidden = chips * ff_local
    x_refs = refs[:cols]
    own_ref, recv_ref = refs[cols : cols + 2]
    cot_refs = refs[cols + 2 : 2 * cols + 2]
    up_refs = refs[2 * cols + 2 : 3 * cols + 2]
    down_refs = refs[3 * cols + 2 : 3 * cols + 2 + chips]
    (
        mod_ref, act_ref, du_ref, n_ref, cot_ref, unit_ref,  inv_ref,
        keep_ref, send_ref, dn_ref, up_sc, down_sc, mid_sc,
    ) = refs[3 * cols + 2 + chips :]
    block = x_refs[0].shape[0]

    @pl.when(pl.program_id(0) == 0)
    def _():
        for b in range(cols):
            rows = relative_rows(b, block)
            start = pl.multiple_of(meta_ref[b] * block, block)
            up_sc[rows, :] = up_refs[b][...]
            for i in range(chips):
                for c in range(ff_local // sub):
                    first = i * ff_local + c * sub
                    weights = down_refs[i][pl.ds(start, block), c * sub : (c + 1) * sub]
                    down_sc[rows, first : first + sub] = weights

    total = jnp.zeros((1, tb), f32)
    squares = jnp.zeros((1, tb), f32)
    for b in range(cols):
        rows = relative_rows(b, block)
        mid = (
            x_refs[b][...].astype(f32)
            + own_ref[rows, :].astype(f32)
            + recv_ref[relative_rows(b ^ 1, block), :].astype(f32)
        )
        mid_sc[rows, :] = mid
        total = total + jnp.sum(mid, axis=0, keepdims=True)
        squares = squares + jnp.sum(mid * mid, axis=0, keepdims=True)
        cot_ref[rows, :] = cot_refs[b][...]
    mean = total * (1.0 / D)
    inv = lax.rsqrt(squares * (1.0 / D) - mean * mean + norm_eps)
    inv_ref[...] = inv
    for b in range(cols):
        rows = relative_rows(b, block)
        n = (mid_sc[rows, :] - mean) * inv
        unit_ref[rows, :] = n.astype(bf16)
        n_ref[rows, :] = (n * (1.0 + mod_ref[rows, 2:3]) + mod_ref[rows, 3:4]).astype(bf16)

    def products(s):
        rows = slice(s * sub, (s + 1) * sub)
        return matmul(up_sc[:, rows], n_ref[...], 0, 0), matmul(
            down_sc[:, rows], cot_ref[...], 0, 0
        )

    ahead = products(0)
    for s in range(hidden // sub):
        up, grad_active = ahead
        if s + 1 < hidden // sub:
            ahead = products(s + 1)
        cdf = 0.5 * (1.0 + lax.erf(up * math.sqrt(0.5)))
        density = jnp.exp(-0.5 * up * up) * (1.0 / math.sqrt(2.0 * math.pi))
        act_ref[s * sub : (s + 1) * sub, :] = (up * cdf).astype(bf16)
        du_ref[s * sub : (s + 1) * sub, :] = (grad_active * (cdf + up * density)).astype(bf16)
    for b in range(cols):
        rows = relative_rows(b, block)
        dn_ref[rows, :] = matmul(up_sc[rows, :], du_ref[...]).astype(bf16)
        y = matmul(down_sc[rows, :], act_ref[...])
        half = relative_rows(b // 2, block)
        if b % 2 == 0:
            keep_ref[half, :] = mid_sc[rows, :] + y
        else:
            send_ref[half, :] = y.astype(bf16)


def feed_forward(meta, pieces, own, recv, cot_pieces, up_all, downs, mod, tb=512):
    cols = len(pieces)
    ff_local = downs[0].shape[1]
    hidden = ff_local * len(downs)
    block = pieces[0].shape[0]
    part = own.shape[1]
    tb = min(tb, part)
    strip = lambda r: pl.BlockSpec((r, tb), lambda t, meta: (0, t))
    whole = lambda s: pl.BlockSpec(s, lambda t, meta: (0, 0), pipeline_mode=pl.Buffered(1))

    def weight_rows(b):
        return pl.BlockSpec(
            (block, hidden), lambda t, meta: (meta[b], 0), pipeline_mode=pl.Buffered(1)
        )

    shape = lambda r, kind: jax.ShapeDtypeStruct((r, part), kind)
    return pl.pallas_call(
        partial(feed_forward_kernel, cols=cols, ff_local=ff_local, tb=tb, sub=128),
        out_shape=[
            shape(hidden, bf16), shape(hidden, bf16), shape(D, bf16), shape(D, bf16),
            shape(D, bf16), shape(1, f32), shape(D // 2, f32), shape(D // 2, bf16),
            shape(D, bf16),
        ],
        grid_spec=pltpu.PrefetchScalarGridSpec(
            num_scalar_prefetch=1,
            grid=(part // tb,),
            in_specs=[pl.BlockSpec((block, tb), lambda t, meta: (0, meta[cols] // tb + t))] * cols
            + [strip(D), strip(D)]
            + [strip(block)] * cols
            + [weight_rows(b) for b in range(cols)]
            + [whole(down.shape) for down in downs]
            + [whole(mod.shape)],
            out_specs=[
                strip(hidden), strip(hidden), strip(D), strip(D), strip(D), strip(1),
                strip(D // 2), strip(D // 2), strip(D),
            ],
            scratch_shapes=[
                pltpu.VMEM((D, hidden), bf16),
                pltpu.VMEM((D, hidden), bf16),
                pltpu.VMEM((D, tb), f32),
            ],
        ),
        compiler_params=pltpu.CompilerParams(vmem_limit_bytes=VMEM_LIMIT),
        cost_estimate=pl.CostEstimate(
            flops=8 * D * hidden * part,
            bytes_accessed=4 * D * hidden + 24 * D * part,
            transcendentals=2 * hidden * part,
        ),
        name="feed_forward",
    )(meta, *pieces, own, recv, *cot_pieces, *([up_all] * cols), *downs, mod)


def weight_grad_kernel(meta_ref, *refs, pairs, cols, starts):
    lefts = refs[:pairs]
    rights = refs[pairs : 2 * pairs]
    g_ref, g_sc = refs[-2:]
    block = D // cols
    j = pl.program_id(0)
    for p in range(pairs):

        @pl.when(jnp.logical_and(j >= starts[p], j < starts[p + 1]))
        def _():
            g_sc[...] = matmul(lefts[p][...], rights[p][...], 1, 1).astype(bf16)

    for b in range(cols):
        start = pl.multiple_of(meta_ref[b] * block, block)
        g_ref[pl.ds(start, block), :] = g_sc[relative_rows(b, block), :]


def weight_grads(cols, meta, pairs, places, width, into=None, step=512):
    sizes = [right.shape[0] for _, right in pairs]
    counts = [size // step for size in sizes]
    starts = [sum(counts[:p]) for p in range(len(pairs) + 1)]
    part = pairs[0][0].shape[1]

    def right_map(p):
        return lambda j, meta: (jnp.clip(j - starts[p], 0, counts[p] - 1), 0)

    def out_map(j, meta):
        column = places[0] // step + j
        for p in range(1, len(pairs)):
            column = jnp.where(j >= starts[p], places[p] // step + j - starts[p], column)
        return (0, column)

    lefts = [left for left, _ in pairs]
    rights = [right for _, right in pairs]
    whole = lambda s: pl.BlockSpec(s, lambda j, meta: (0, 0), pipeline_mode=pl.Buffered(1))
    more = [] if into is None else [into]
    return pl.pallas_call(
        partial(weight_grad_kernel, pairs=len(pairs), cols=cols, starts=starts),
        out_shape=jax.ShapeDtypeStruct((D, width), bf16),
        grid_spec=pltpu.PrefetchScalarGridSpec(
            num_scalar_prefetch=1,
            grid=(starts[-1],),
            in_specs=[whole((D, part))] * len(pairs)
            + [pl.BlockSpec((step, part), right_map(p)) for p in range(len(pairs))]
            + [pl.BlockSpec(memory_space=pl.ANY)] * len(more),
            out_specs=pl.BlockSpec((D, step), out_map),
            scratch_shapes=[pltpu.VMEM((D, step), bf16)],
        ),
        input_output_aliases={} if into is None else {1 + 2 * len(pairs): 0},
        compiler_params=pltpu.CompilerParams(vmem_limit_bytes=VMEM_LIMIT),
        cost_estimate=pl.CostEstimate(
            flops=2 * D * part * sum(sizes),
            bytes_accessed=2 * (D * part * len(pairs) + (D + part) * sum(sizes)),
            transcendentals=0,
        ),
        name="weight_grads",
    )(meta, *lefts, *rights, *more)


def mid_back_kernel(meta_ref, *refs, cols):
    dn_ref, recv_ref, unit_ref, inv_ref, cot_ref, mod_ref = refs[:6]
    w_refs = refs[6 : 6 + cols]
    kept_ref, branch_ref = refs[6 + cols : 8 + cols]
    att_refs = refs[8 + cols : 8 + cols + cols // 2]
    sums_ref, r_sc, w_sc, sum_sc = refs[8 + cols + cols // 2 :]
    block = w_refs[0].shape[0]
    tb = dn_ref.shape[1]
    t = pl.program_id(0)

    @pl.when(t == 0)
    def _():
        sum_sc[...] = jnp.zeros_like(sum_sc)
        for b in range(cols):
            w_sc[:, relative_rows(b, block)] = w_refs[b][...].T

    inv = inv_ref[...]
    total = jnp.zeros((1, tb), f32)
    cross = jnp.zeros((1, tb), f32)
    for b in range(cols):
        rows = relative_rows(b, block)
        r = dn_ref[rows, :].astype(f32) + recv_ref[relative_rows(b ^ 1, block), :].astype(f32)
        n = unit_ref[rows, :].astype(f32)
        sum_sc[rows, 0:1] += jnp.sum(r * n, axis=1, keepdims=True)
        sum_sc[rows, 1:2] += jnp.sum(r, axis=1, keepdims=True)
        m = r * (1.0 + mod_ref[rows, 2:3])
        total = total + jnp.sum(m, axis=0, keepdims=True)
        cross = cross + jnp.sum(m * n, axis=0, keepdims=True)
        r_sc[rows, :] = m
    total = total * (1.0 / D)
    cross = cross * (1.0 / D)
    for b in range(cols):
        rows = relative_rows(b, block)
        n = unit_ref[rows, :].astype(f32)
        grad = cot_ref[rows, :].astype(f32) + inv * (r_sc[rows, :] - total - n * cross)
        if b % 2 == 0:
            kept_ref[relative_rows(b // 2, block), :] = grad
        branch_ref[rows, :] = grad.astype(bf16)
    att = matmul(w_sc[...], branch_ref[...]).astype(bf16)
    for i in range(cols // 2):
        att_refs[i][...] = att[i * block : (i + 1) * block]

    @pl.when(t == pl.num_programs(0) - 1)
    def _():
        sums_ref[...] = sum_sc[...]


def mid_back(cols, meta, own, recv, unit, inv, cot, mod, up_all, hidden, tb=512):
    block = D // cols
    part = own.shape[1]
    tb = min(tb, part)
    width = up_all.shape[1] - hidden
    strip = lambda r: pl.BlockSpec((r, tb), lambda t, meta: (0, t))
    whole = lambda s: pl.BlockSpec(s, lambda t, meta: (0, 0), pipeline_mode=pl.Buffered(1))

    def weight_rows(b):
        return pl.BlockSpec(
            (block, width),
            lambda t, meta: (meta[b], hidden // width),
            pipeline_mode=pl.Buffered(1),
        )

    shape = lambda r, kind: jax.ShapeDtypeStruct((r, part), kind)
    return pl.pallas_call(
        partial(mid_back_kernel, cols=cols),
        out_shape=[
            shape(D // 2, f32), shape(D, bf16), *[shape(block, bf16)] * (cols // 2),
            jax.ShapeDtypeStruct((D, 2), f32),
        ],
        grid_spec=pltpu.PrefetchScalarGridSpec(
            num_scalar_prefetch=1,
            grid=(part // tb,),
            in_specs=[strip(D), strip(D), strip(D), strip(1), strip(D), whole(mod.shape)]
            + [weight_rows(b) for b in range(cols)],
            out_specs=[strip(D // 2), strip(D), *[strip(block)] * (cols // 2), whole((D, 2))],
            scratch_shapes=[
                pltpu.VMEM((D, tb), f32),
                pltpu.VMEM((width, D), bf16),
                pltpu.VMEM((D, 2), f32),
            ],
        ),
        compiler_params=pltpu.CompilerParams(vmem_limit_bytes=VMEM_LIMIT),
        cost_estimate=pl.CostEstimate(
            flops=2 * D * width * part, bytes_accessed=18 * D * part, transcendentals=0
        ),
        name="mid_back",
    )(meta, own, recv, unit, inv, cot, mod, *([up_all] * cols))


def project_back_kernel(meta_ref, *refs, cols, rows, tt):
    x_refs = refs[:cols]
    (
        mean_ref, inv_ref, dq_ref, dk_ref, dv_ref, w_ref, mod_ref, kept_ref,
        keep_ref, send_ref, g_ref, sums_ref, w_sc, d_sc, n_sc, r_sc, g_sc,
    ) = refs[cols:]
    block = x_refs[0].shape[0]
    shard = D // rows
    t = pl.program_id(0)

    @pl.when(t == 0)
    def _():
        g_sc[...] = jnp.zeros_like(g_sc)
        n_sc[D:, :] = jnp.ones((EXTRA, tt), bf16)
        column = jnp.zeros((1, w_sc.shape[1]), f32)
        for r in range(rows):
            start = pl.multiple_of(meta_ref[cols + 2 + r] * shard, shard)
            own = relative_rows(r, shard)
            weights = w_ref[pl.ds(start, shard), :]
            w_sc[own, :] = weights
            column = column + jnp.sum(
                weights.astype(f32) * (1.0 + mod_ref[own, 0:1]), axis=0, keepdims=True
            )
        number = lax.broadcasted_iota(jnp.int32, (EXTRA, w_sc.shape[1]), 0)
        terms = jnp.zeros((EXTRA, w_sc.shape[1]), f32)
        for i in range(3):
            term = column.astype(bf16).astype(f32)
            terms = jnp.where(number == i, term, terms)
            column = column - term
        w_sc[D:, :] = terms.astype(bf16)

    for j, ref in enumerate((dq_ref, dk_ref, dv_ref)):
        d_sc[j * block : (j + 1) * block, :] = ref[...]
    r_sc[...] = matmul(w_sc[...], d_sc[...])
    token = t * tt
    mine = jnp.where(
        jnp.logical_and(token >= meta_ref[cols], token < meta_ref[cols] + meta_ref[cols + 1]),
        1.0,
        0.0,
    )
    mean = mean_ref[...]
    inv = inv_ref[...]
    cross = jnp.zeros((1, tt), f32)
    for b in range(cols):
        own = relative_rows(b, block)
        n = (x_refs[b][...].astype(f32) - mean) * inv
        n_sc[own, :] = n.astype(bf16)
        m = r_sc[own, :] * (1.0 + mod_ref[own, 0:1])
        r_sc[own, :] = m
        cross = cross + jnp.sum(m * n, axis=0, keepdims=True)
    g_sc[...] += matmul(n_sc[...], d_sc[...], 1, 1)
    total = r_sc[D : D + 1, :] + r_sc[D + 1 : D + 2, :] + r_sc[D + 2 : D + 3, :]
    slope = inv * inv * cross * (1.0 / D)
    level = inv * total * (1.0 / D) - mean * slope
    for b in range(cols):
        own = relative_rows(b, block)
        grad = r_sc[own, :] * inv - x_refs[b][...].astype(f32) * slope - level
        half = relative_rows(b // 2, block)
        if b % 2 == 0:
            keep_ref[half, :] = grad + mine * kept_ref[half, :]
        else:
            send_ref[half, :] = grad.astype(bf16)

    @pl.when(t == pl.num_programs(0) - 1)
    def _():
        sums = g_sc[D : D + 1, :]
        for r in range(rows):
            start = pl.multiple_of(meta_ref[cols + 2 + r] * shard, shard)
            own = relative_rows(r, shard)
            weights = w_sc[own, :].astype(f32)
            products = g_sc[own, :]
            sums_ref[own, 0:1] = jnp.sum(weights * products, axis=1, keepdims=True)
            sums_ref[own, 1:2] = jnp.sum(weights * sums, axis=1, keepdims=True)
            gains = products * (1.0 + mod_ref[own, 0:1]) + mod_ref[own, 1:2] * sums
            g_ref[pl.ds(start, shard), :] = gains.astype(bf16)


def project_back(rows, meta, pieces, mean, inv, grads, w_qkv, mod, kept, tt=512):
    cols = len(pieces)
    block, tokens = pieces[0].shape
    part = kept.shape[1]
    tt = min(tt, part)
    width = w_qkv.shape[1]
    middle = tokens // tt // 2
    strip = lambda r: pl.BlockSpec((r, tt), lambda t, meta: (0, t))
    whole = lambda s: pl.BlockSpec(s, lambda t, meta: (0, 0), pipeline_mode=pl.Buffered(1))
    halves = pl.BlockSpec(
        (pl.Squeezed(), D // 2, tt), lambda t, meta: (t // middle, 0, t % middle)
    )

    def kept_strip(t, meta):
        last = part // tt - 1
        return (0, jnp.clip(t - meta[cols] // tt, 0, last))

    return pl.pallas_call(
        partial(project_back_kernel, cols=cols, rows=rows, tt=tt),
        out_shape=[
            jax.ShapeDtypeStruct((2, D // 2, tokens // 2), f32),
            jax.ShapeDtypeStruct((2, D // 2, tokens // 2), bf16),
            jax.ShapeDtypeStruct((D, width), bf16),
            jax.ShapeDtypeStruct((D, 2), f32),
        ],
        grid_spec=pltpu.PrefetchScalarGridSpec(
            num_scalar_prefetch=1,
            grid=(tokens // tt,),
            in_specs=[strip(block)] * cols
            + [strip(1), strip(1)]
            + [strip(block)] * 3
            + [whole(w_qkv.shape), whole(mod.shape), pl.BlockSpec((D // 2, tt), kept_strip)],
            out_specs=[halves, halves, whole((D, width)), whole((D, 2))],
            scratch_shapes=[
                pltpu.VMEM((D + EXTRA, width), bf16),
                pltpu.VMEM((width, tt), bf16),
                pltpu.VMEM((D + EXTRA, tt), bf16),
                pltpu.VMEM((D + EXTRA, tt), f32),
                pltpu.VMEM((D + EXTRA, width), f32),
            ],
        ),
        compiler_params=pltpu.CompilerParams(vmem_limit_bytes=VMEM_LIMIT),
        cost_estimate=pl.CostEstimate(
            flops=4 * D * width * tokens, bytes_accessed=8 * D * tokens, transcendentals=0
        ),
        name="project_back",
    )(meta, *pieces, mean, inv, *grads, w_qkv, mod, kept)


def time_features(time_steps, feature_count):
    half_dim = feature_count // 2
    frequency = jnp.exp(-math.log(10000.0) * jnp.arange(half_dim, dtype=f32) / half_dim)
    angles = time_steps.astype(f32)[:, None] * frequency[None, :]
    return jnp.concatenate([jnp.sin(angles), jnp.cos(angles)], axis=1)


def rotary_tables(places):
    inverse = jnp.exp(-math.log(10000.0) * jnp.arange(HALF, dtype=f32) * 2.0 / HEAD_DIM)
    angles = inverse[:, None] * places.astype(f32)[None, :]
    return jnp.cos(angles), jnp.sin(angles)


def local(
    chips,
    rows,
    hidden_in,
    query_key_value_weight,
    output_weight,
    up_weight,
    down_weight,
    w_time,
    segment_ids,
    positions,
    time_step,
    cotangent,
):
    cols = 2 * chips
    me = lax.axis_index("col")
    chip = me // 2
    core = me % 2
    row = lax.axis_index("row")
    block, tokens = hidden_in.shape
    part = tokens // chips

    def from_core(v):
        return lax.ppermute(v, "col", [(c, c ^ 1) for c in range(cols)])

    def from_chip(v, i):
        return lax.ppermute(v, "col", [(c, c ^ (2 * i)) for c in range(cols)])

    def from_col(v, b):
        return lax.ppermute(v, "col", [(c, c ^ b) for c in range(cols)])

    def from_row(v, a):
        return lax.ppermute(v, "row", [(r, r ^ a) for r in range(rows)])

    def gather_rows(v):
        return [v] + [from_row(v, a) for a in range(1, rows)]

    def gather_chips(v):
        return [v] + [from_chip(v, i) for i in range(1, chips)]

    def exchange_chips(pieces):
        return [pieces[0]] + [from_chip(pieces[i], i) for i in range(1, chips)]

    def token_part(v, i):
        return lax.dynamic_slice_in_dim(v, (chip ^ i) * part, part, axis=1)

    def place_parts(pieces):
        whole = jnp.zeros((pieces[0].shape[0], tokens), pieces[0].dtype)
        for i, piece in enumerate(pieces):
            whole = lax.dynamic_update_slice_in_dim(whole, piece, (chip ^ i) * part, axis=1)
        return whole

    qkv_shard = jnp.transpose(query_key_value_weight, (1, 0, 2)).reshape(
        query_key_value_weight.shape[1], -1
    )
    qkv_width = qkv_shard.shape[1]
    ff_local = up_weight.shape[1]
    hidden = ff_local * chips
    first_shard = jnp.concatenate(
        [qkv_shard, w_time.reshape(-1, block), down_weight.T], axis=1
    )
    first_all = lax.all_gather(first_shard, "row", axis=0, tiled=True)
    w_qkv = first_all[:, :qkv_width]
    w_time_all = first_all[:, qkv_width : qkv_width + block].reshape(TEMB, 4, block)
    down_own = first_all[:, qkv_width + block :]
    order = me ^ jnp.arange(cols, dtype=jnp.int32)
    per_block = rows // cols
    shard_order = (
        order[:, None] * per_block + jnp.arange(per_block, dtype=jnp.int32)[None, :]
    ).reshape(rows)
    meta = jnp.concatenate([order, jnp.stack([chip * part, jnp.int32(part)]), shard_order])
    up_shards = gather_chips(jnp.concatenate([up_weight, output_weight.T], axis=1))
    up_packed = jnp.concatenate(
        [s[:, :ff_local] for s in up_shards] + [s[:, ff_local:] for s in up_shards], axis=1
    )
    up_all = lax.all_gather(up_packed, "row", axis=0, tiled=True)

    seg = segment_ids[0]
    pos = positions[0]
    ranges = [
        block_ranges(seg, pos, TQ_FORWARD, TK_FORWARD),
        block_ranges(seg, pos, TQ_BACKWARD, TK_BACKWARD),
    ]
    away = gather_chips(hidden_in)
    away[-1], ranges = lax.optimization_barrier((away[-1], ranges))
    pieces = []
    for piece in away:
        pieces += [piece, from_core(piece)]

    embedded = time_features(time_step, TEMB)[0]
    mod_own = jnp.sum(embedded[:, None, None] * w_time_all.astype(f32), axis=0)
    mod_all = jnp.stack([mod_own] + [from_col(mod_own, b) for b in range(1, cols)], axis=1)
    mod_columns = mod_all.reshape(4, D).T

    cosine, sine = rotary_tables(pos)

    after, _ = lax.optimization_barrier((cotangent, pieces[-2]))
    cot_x = exchange_chips([token_part(after, i) for i in range(chips)])

    q, k, v, mean_one, inv_one = project(
        rows, meta, pieces, w_qkv, mod_columns, cosine, sine
    )
    q, *cot_x = lax.optimization_barrier((q, *cot_x))
    downs = gather_chips(down_own)
    cot_pieces = []
    for piece in cot_x:
        cot_pieces += [piece, from_core(piece)]
    att_pieces = [None] * chips
    lse_pieces = [None] * chips
    for i in list(range(1, chips)) + [0]:
        att_pieces[i], lse_pieces[i] = attend(
            (chip ^ i) * part, part, q, k, v, ranges[0], segment_ids
        )
        if i + 1 == chips:
            q, cot_pieces, downs, att_pieces[1:] = lax.optimization_barrier(
                (q, cot_pieces, downs, att_pieces[1:])
            )
    mid_share, att_part = out_project(
        cols, meta, exchange_chips(att_pieces), up_all, hidden
    )

    active, grad_up_b, normed_two, cot, unit_two, inv_two, done_keep, done_send, dn_two = (
        feed_forward(
            meta, pieces, mid_share, from_core(mid_share), cot_pieces, up_all, downs, mod_columns
        )
    )
    dn_recv = from_core(dn_two)

    def rows_total(shares):
        return lax.psum_scatter(shares, "row", scatter_dimension=0, tiled=True)

    width = 2 * hidden + chips * block
    shares_ff = weight_grads(cols, meta, [(cot, active)], [hidden], width)
    done = (done_keep + from_core(done_send).astype(f32)).astype(bf16)
    done = done.reshape(chips, block, part)
    dn_recv, shares_ff = lax.optimization_barrier((dn_recv, shares_ff))
    grad_mid_kept, grad_branch, *grad_att_parts, sums_two = mid_back(
        cols, meta, dn_two, dn_recv, unit_two, inv_two, cot, mod_columns, up_all, hidden
    )
    grad_attended = exchange_chips(grad_att_parts)
    shares_ff = weight_grads(
        cols, meta, [(normed_two, grad_up_b), (grad_branch, att_part)], [0, 2 * hidden],
        width, shares_ff,
    )
    grad_attended, shares_ff, done = lax.optimization_barrier((grad_attended, shares_ff, done))
    grads_ff = rows_total(shares_ff)
    done_pieces = exchange_chips([done[i] for i in range(chips)])

    dq, dk, dv = attend_back(
        chip, q, k, v, att_pieces, grad_attended, lse_pieces, ranges[1], segment_ids, cosine, sine
    )
    dq, dk, dv, done_pieces = lax.optimization_barrier((dq, dk, dv, done_pieces))
    layer_result = place_parts(done_pieces)
    keep, send, shares_qkv, sums_one = project_back(
        rows, meta, pieces, mean_one, inv_one, (dq, dk, dv), w_qkv, mod_columns, grad_mid_kept
    )

    def core_total(keep, recv):
        total = (keep + recv.astype(f32)).reshape(chips, block, -1)
        return total[0], [total[i].astype(bf16) for i in range(1, chips)]

    def chip_total(total, away):
        for i in range(1, chips):
            total = total + from_chip(away[i - 1], i).astype(f32)
        return total.astype(bf16)

    recv = from_core(send)
    total_early, away_early = core_total(keep[0], recv[0])
    keep, away_early = lax.optimization_barrier((keep, away_early))
    total_late, away_late = core_total(keep[1], recv[1])
    shares_qkv, grads_ff, away_late = lax.optimization_barrier((shares_qkv, grads_ff, away_late))
    grad_hidden = jnp.concatenate(
        [chip_total(total_early, away_early), chip_total(total_late, away_late)], axis=1
    )

    once = (core == 0).astype(f32)
    grad_mod = jnp.concatenate([sums_one, sums_two * once], axis=1).T.reshape(4, cols, block)
    mod_total = grad_mod[:, 0]
    for b in range(1, cols):
        mod_total = mod_total + from_col(grad_mod[:, b], b)

    high = mod_total.astype(bf16)
    low = (mod_total - high.astype(f32)).astype(bf16)
    step = time_step[0]
    numbers = jnp.stack([step // 256, step % 256]).astype(bf16)
    extra = jnp.concatenate([high, low], axis=0)
    extra = jnp.concatenate(
        [extra, jnp.broadcast_to(jnp.tile(numbers, 4)[:, None], (8, qkv_width - block))], axis=1
    )
    shares = jnp.concatenate(
        [
            shares_qkv.reshape(rows, -1, qkv_width),
            jnp.broadcast_to(extra[None], (rows, 8, qkv_width)),
        ],
        axis=1,
    )
    row_shares = lax.all_to_all(shares, "row", split_axis=0, concat_axis=0, tiled=True)
    shard = D // rows
    grads_qkv = jnp.sum(row_shares[:, :shard].astype(f32), axis=0)
    extras = row_shares[:, shard:].astype(f32)
    mod_rows = extras[:, :4, :block] + extras[:, 4:, :block]
    steps = extras[:, 0, block] * 256.0 + extras[:, 1, block]

    pieces_ff = [
        jnp.concatenate(
            [
                grads_ff[:, i * ff_local : (i + 1) * ff_local],
                grads_ff[:, hidden + i * ff_local : hidden + (i + 1) * ff_local],
                grads_ff[:, 2 * hidden + i * block : 2 * hidden + (i + 1) * block],
            ],
            axis=1,
        )
        for i in range(chips)
    ]
    summed = pieces_ff[0].astype(f32)
    for piece in exchange_chips(pieces_ff)[1:]:
        summed = summed + piece.astype(f32)
    summed_up = summed[:, :ff_local]
    summed_down = summed[:, ff_local : 2 * ff_local].T
    summed_out = summed[:, 2 * ff_local :].T
    summed_qkv = jnp.transpose(grads_qkv.reshape(-1, 3, block), (1, 0, 2))

    temb_share = w_time.shape[0]
    embed_rows = time_features(steps, TEMB)
    embed_share = lax.dynamic_slice_in_dim(embed_rows, row * temb_share, temb_share, axis=1)
    grad_time = jnp.einsum("st,skc->tkc", embed_share, mod_rows, precision=highest_precision)
    return (layer_result, grad_hidden, summed_qkv, summed_out, summed_up, summed_down, grad_time)


def solution(mesh):
    in_specs = (
        P("col", "row"),
        P(None, "row", "col"),
        P("col", "row"),
        P("row", "col"),
        P("col", "row"),
        P("row", None, "col"),
        P("row", None),
        P("row", None),
        P("row"),
        P("col", "row"),
    )
    out_specs = (
        P("col", "row"),
        P("col", "row"),
        P(None, "row", "col"),
        P("col", "row"),
        P("row", "col"),
        P("col", "row"),
        P("row", None, "col"),
    )
    return jax.shard_map(
        partial(local, mesh.shape["col"] // 2, mesh.shape["row"]),
        mesh=mesh,
        in_specs=in_specs,
        out_specs=out_specs,
        check_vma=False,
    )
```
